32 devices in a mesh: grp: 4 (over x, core), chan: 8 (over z, y).
Axes of the slice: x: 2, y: 2, z: 4, core: 2. Of those that a mesh axis runs over, the one named last changes fastest.
Arguments:
- voltages: int32 [256, 31, 8192], P('grp', None, 'chan'), may hold values from -128 to 127
- plan: int32 [3, 4], replicated, may hold values from 0 to 3, as said below
Outputs:
- visibility: bfloat16 [3, 256, 2048, 128], P(None, 'grp', 'chan')
The draws below stay inside these ranges and needn't reach their ends.
Inputs may be any that keep to these rules, and one draw needn't show every extreme that they name: Every row is a perfect matching of the 4 groups: plan[r, plan[r, g]] = g and plan[r, g] != g; the 3 partners of a group are all different.
All inputs are finite; a program needn't handle non-finite values.
Results may differ from the reference program's by a relative error of at most 0.0057.
Values may be sent and summed in bfloat16 or wider, within the bound.
No kernel may reach another device: no remote copies, remote signals or barrier semaphores. Data moves between devices by JAX's collectives and lax.ppermute only.
A program may use at most 128 MiB of HBM per device.

```python
import math
import jax
import jax.numpy as jnp
from jax import lax

SIG = 64
CH = 4096
TAPS = 16
SPEC = 16
ROUNDS = 3
GROUPS = 4
NSIG = 256
NFFT = 8192
FRAMES = 31
HALF = 256
HALF_ALL = 2048
N_CHAN = 8


def draw_plan(key, part):
    key_teams = jax.random.fold_in(key, 4099)
    key_rounds = jax.random.fold_in(key, 7919)
    labels = jax.random.permutation(key_teams, GROUPS)
    chosen = jax.random.permutation(key_rounds, GROUPS - 1)[:ROUNDS]
    team_ids = jnp.arange(GROUPS)
    last_team = GROUPS - 1

    def one_round(round_index):
        opposite = (2 * round_index - team_ids) % last_team
        team_partner = jnp.where(team_ids == last_team, round_index, jnp.where(team_ids == round_index, last_team, opposite))
        return jnp.zeros((GROUPS,), jnp.int32).at[labels].set(labels[team_partner].astype(jnp.int32))
    return jax.vmap(one_round)(chosen).astype(jnp.int32)


def place_ends(entries, stream_key, low, high):
    shape = entries.shape
    index_at = [jax.random.randint(jax.random.fold_in(stream_key, axis), (), 0, shape[axis]) for axis in range(len(shape))]
    entries = entries.at[tuple(index_at)].set(low)
    longest = shape.index(max(shape))
    index_at[longest] = (index_at[longest] + 1) % shape[longest]
    return entries.at[tuple(index_at)].set(high)


def setup_inputs(seed: int = 0) -> dict:
    key_of = jax.random.split(jax.random.key(seed), 3)
    voltages = place_ends(jax.random.randint(key_of[0], (NSIG, FRAMES, NFFT), -128, 128), jax.random.fold_in(key_of[0], 1), -128, 127).astype(jnp.int32)
    plan = draw_plan(jax.random.fold_in(key_of[2], 71), 0)
    return dict(voltages=voltages, plan=plan)


def taper_coeff(position, length_total, fft_len):
    window = 0.5 - 0.5 * jnp.cos(2.0 * math.pi * position / length_total)
    return window * jnp.sinc((position - 0.5 * length_total) / fft_len)

def reference(voltages, plan):
    fft_len = 2 * CH
    samples = voltages.astype(jnp.float32)
    positions = jnp.arange(TAPS * fft_len).astype(jnp.float32)
    coeffs = taper_coeff(positions, TAPS * fft_len, fft_len).reshape(TAPS, fft_len)
    filtered = jnp.zeros((NSIG, SPEC, fft_len), jnp.float32)
    for tap_index in range(TAPS):
        filtered = filtered + coeffs[tap_index] * samples[:, tap_index:tap_index + SPEC, :]
    spectra = jnp.fft.rfft(filtered, axis=-1)[..., :CH] * (1.0 / (64.0 * math.sqrt(fft_len)))
    chan_re = lax.optimization_barrier(jnp.real(spectra).astype(jnp.bfloat16)).astype(jnp.float32)
    chan_im = lax.optimization_barrier(jnp.imag(spectra).astype(jnp.bfloat16)).astype(jnp.float32)
    chan_pos = jnp.arange(HALF_ALL)
    device_of = chan_pos // HALF
    inner_pos = chan_pos % HALF
    low_index = (device_of + N_CHAN * inner_pos).astype(jnp.int32)
    high_index = (device_of + N_CHAN * (inner_pos + HALF)).astype(jnp.int32)

    def one_pair(pair_index):
        round_index = pair_index // GROUPS
        group_index = pair_index % GROUPS
        partner = plan[round_index, group_index]
        chosen = jnp.where(group_index > partner, high_index, low_index)

        def pick(data, group):
            rows = lax.dynamic_slice_in_dim(data, (group * SIG).astype(jnp.int32), SIG, 0)
            return jnp.take(rows, chosen, axis=2)
        mine_re = pick(chan_re, group_index)
        mine_im = pick(chan_im, group_index)
        other_re = pick(chan_re, partner)
        other_im = pick(chan_im, partner)
        vis_re = jnp.einsum('asq,bsq->aqb', mine_re, other_re) + jnp.einsum('asq,bsq->aqb', mine_im, other_im)
        vis_im = jnp.einsum('asq,bsq->aqb', mine_im, other_re) - jnp.einsum('asq,bsq->aqb', mine_re, other_im)
        return (jnp.concatenate([vis_re, vis_im], axis=-1) / SPEC).astype(jnp.bfloat16)
    stacked = lax.map(one_pair, jnp.arange(ROUNDS * GROUPS, dtype=jnp.int32))
    return stacked.reshape(ROUNDS, NSIG, HALF_ALL, 2 * SIG)
```

```python
import functools
import math

import jax
import jax.numpy as jnp
import numpy as np
from jax import lax
from jax.experimental import pallas as pl
from jax.experimental.pallas import tpu as pltpu
from jax.sharding import PartitionSpec as P

TAPS = 16
LANES = 128
RADIX = 64
VMEM_LIMIT = 60 * 1024 * 1024


def tap_table(fft_len):
    position = np.arange(TAPS * fft_len, dtype=np.float64)
    total = TAPS * fft_len
    window = 0.5 - 0.5 * np.cos(2.0 * np.pi * position / total)
    return (window * np.sinc((position - 0.5 * total) / fft_len)).reshape(TAPS, fft_len)


def filter_kernel(chan_ref, volt_ref, coeff_ref, out_ref):
    del chan_ref
    frames, sig_tile, block_len = volt_ref.shape
    spec_count = frames - TAPS + 1

    def one_tile(tile, carry):
        cols = pl.ds(pl.multiple_of(tile * LANES, LANES), LANES)
        coeff = [
            jnp.broadcast_to(coeff_ref[0, t : t + 1, cols], (sig_tile, LANES)) for t in range(TAPS)
        ]
        total = [None] * spec_count
        for frame in range(frames):
            sample = volt_ref[frame, :, cols].astype(jnp.float32)
            for s in range(max(0, frame - TAPS + 1), min(spec_count - 1, frame) + 1):
                term = coeff[frame - s] * sample
                total[s] = term if total[s] is None else total[s] + term
            if frame >= TAPS - 1:
                s = frame - TAPS + 1
                out_ref[s, :, cols] = total[s].astype(jnp.bfloat16)
                total[s] = None
        return carry

    lax.fori_loop(0, block_len // LANES, one_tile, 0)


def filter_taps(frames_first, chan_id, chan_count):
    frames, sig_count, block_len = frames_first.shape
    spec_count = frames - TAPS + 1
    table = tap_table(block_len * chan_count).astype(np.float32)
    table = np.ascontiguousarray(table.reshape(TAPS, chan_count, block_len).transpose(1, 0, 2))
    sig_tile = 16
    return pl.pallas_call(
        filter_kernel,
        out_shape=jax.ShapeDtypeStruct((spec_count, sig_count, block_len), jnp.bfloat16),
        grid_spec=pltpu.PrefetchScalarGridSpec(
            num_scalar_prefetch=1,
            grid=(sig_count // sig_tile,),
            in_specs=[
                pl.BlockSpec((frames, sig_tile, block_len), lambda i, c: (0, i, 0)),
                pl.BlockSpec((1, TAPS, block_len), lambda i, c: (c[0], 0, 0)),
            ],
            out_specs=pl.BlockSpec((spec_count, sig_tile, block_len), lambda i, c: (0, i, 0)),
        ),
        compiler_params=pltpu.CompilerParams(vmem_limit_bytes=VMEM_LIMIT),
        name="filter_taps",
    )(chan_id.reshape(1), frames_first, jnp.asarray(table))


def cadd(a, b):
    if a is None:
        return b
    if b is None:
        return a
    return a + b


def csub(a, b):
    if b is None:
        return a
    if a is None:
        return -b
    return a - b


def scale_by(value, re, im):
    vr, vi = value
    eps = 1e-12

    def mul(x, f):
        if x is None or abs(f) < eps:
            return None
        if abs(f - 1.0) < eps:
            return x
        if abs(f + 1.0) < eps:
            return -x
        return x * f

    return csub(mul(vr, re), mul(vi, im)), cadd(mul(vr, im), mul(vi, re))


def plus(a, b):
    return cadd(a[0], b[0]), cadd(a[1], b[1])


def minus(a, b):
    return csub(a[0], b[0]), csub(a[1], b[1])


def dft(values, wanted=None):
    n = len(values)
    if n == 1:
        return list(values)
    even = dft(values[0::2])
    odd = dft(values[1::2])
    out = [None] * n
    for k in range(n // 2):
        if wanted is not None and k not in wanted and k + n // 2 not in wanted:
            continue
        angle = -2.0 * math.pi * k / n
        turned = scale_by(odd[k], math.cos(angle), math.sin(angle))
        out[k] = plus(even[k], turned)
        out[k + n // 2] = minus(even[k], turned)
    return out


def first_index_list():
    chosen = []
    for c in range(5):
        for e in range(8):
            k1 = c + 8 * e
            if c in (0, 4) and k1 > RADIX // 2:
                continue
            chosen.append(k1)
    return chosen


def turn_tables(fft_len):
    k1 = np.array(first_index_list())[:, None]
    angle = 2.0 * np.pi * ((k1 * np.arange(LANES)[None, :]) % fft_len) / fft_len
    return np.cos(angle), np.sin(angle)


def wave_matrix(fft_len):
    gain = 1.0 / (64.0 * math.sqrt(fft_len))
    half = LANES // 2
    n2 = np.arange(LANES)[None, :]
    k2 = np.arange(half)[:, None]
    rows = []
    for index, flip in ((k2, 1.0), (LANES - 1 - k2, -1.0)):
        angle = 2.0 * np.pi * ((index * n2) % LANES) / LANES
        cos, sin = np.cos(angle) * gain, np.sin(angle) * gain
        rows.append(np.concatenate([cos, sin], axis=1))
        rows.append(np.concatenate([-sin, cos], axis=1) * flip)
    return np.concatenate(rows, axis=0)


def split_two(value):
    high = value.astype(jnp.bfloat16)
    return high, (value - high.astype(jnp.float32)).astype(jnp.bfloat16)


def transform_kernel(
    chan_count, in_ref, cos_ref, sin_ref, wave_high_ref, wave_low_ref, out_ref, mid_ref, high_ref, low_ref
):
    _, rows, block_len = in_ref.shape
    per_block = block_len // LANES
    tile = 16
    chosen = first_index_list()

    def row_tile(step, carry):
        at = pl.ds(pl.multiple_of(step * tile, tile), tile)
        present = set()
        for low_n in range(8):
            column = []
            for high_n in range(8):
                n1 = high_n * 8 + low_n
                lanes = slice((n1 % per_block) * LANES, (n1 % per_block + 1) * LANES)
                column.append((in_ref[n1 // per_block, at, lanes].astype(jnp.float32), None))
            spread = dft(column, wanted=range(5))
            for c in range(5):
                angle = -2.0 * math.pi * low_n * c / RADIX
                re, im = scale_by(spread[c], math.cos(angle), math.sin(angle))
                for part, value in enumerate((re, im)):
                    if value is not None:
                        mid_ref[low_n, c, part] = value
                        present.add((low_n, c, part))
        for c in range(5):
            wanted = [e for e in range(8) if c + 8 * e in chosen]
            values = []
            for low_n in range(8):
                values.append(
                    tuple(
                        mid_ref[low_n, c, part] if (low_n, c, part) in present else None
                        for part in range(2)
                    )
                )
            spread = dft(values, wanted=wanted)
            for e in wanted:
                place = chosen.index(c + 8 * e)
                cos = cos_ref[place : place + 1, :]
                sin = sin_ref[place : place + 1, :]
                re, im = spread[e]
                if im is None:
                    turned_re, turned_im = re * cos, -(re * sin)
                else:
                    turned_re, turned_im = re * cos + im * sin, im * cos - re * sin
                a, b = split_two(turned_re)
                high_ref[place, at, :LANES] = a
                low_ref[place, at, :LANES] = b
                a, b = split_two(turned_im)
                high_ref[place, at, LANES:] = a
                low_ref[place, at, LANES:] = b
        return carry

    lax.fori_loop(0, rows // tile, row_tile, 0)

    dims = (((1,), (1,)), ((), ()))
    wave_high = wave_high_ref[...]
    wave_low = wave_low_ref[...]
    for first in range(0, len(chosen), 2):
        places = [p for p in (first, first + 1) if p < len(chosen)]
        high = high_ref[first : first + len(places)].reshape(len(places) * rows, 2 * LANES)
        low = low_ref[first : first + len(places)].reshape(len(places) * rows, 2 * LANES)
        total = lax.dot_general(wave_high, high, dims, preferred_element_type=jnp.float32)
        total += lax.dot_general(wave_high, low, dims, preferred_element_type=jnp.float32)
        total += lax.dot_general(wave_low, high, dims, preferred_element_type=jnp.float32)
        total = total.astype(jnp.bfloat16)
        for i, place in enumerate(places):
            k1 = chosen[place]
            columns = total[:, i * rows : (i + 1) * rows]
            quarter = LANES // 4
            for side, index in ((0, k1), (1, RADIX - k1)):
                if side == 1 and (k1 == 0 or k1 == RADIX // 2):
                    continue
                for part in range(2):
                    for half in range(2):
                        at = side * LANES + part * 2 * quarter + half * quarter
                        out_ref[index % chan_count, half, index // chan_count, part] = columns[
                            at : at + quarter
                        ]


def transform(samples):
    chan_count, rows, block_len = samples.shape
    fft_len = chan_count * block_len
    count = len(first_index_list())
    cos, sin = turn_tables(fft_len)
    wave = wave_matrix(fft_len)
    wave_high = wave.astype(jnp.bfloat16)
    wave_low = (wave - wave_high.astype(np.float64)).astype(jnp.bfloat16)
    tables = (
        jnp.asarray(cos, jnp.float32),
        jnp.asarray(sin, jnp.float32),
        jnp.asarray(wave_high),
        jnp.asarray(wave_low),
    )
    whole = pl.BlockSpec(memory_space=pltpu.VMEM)
    return pl.pallas_call(
        functools.partial(transform_kernel, chan_count),
        out_shape=jax.ShapeDtypeStruct(
            (chan_count, 2, RADIX // chan_count, 2, LANES // 4, rows), jnp.bfloat16
        ),
        in_specs=[whole] * 5,
        out_specs=whole,
        scratch_shapes=[
            pltpu.VMEM((8, 5, 2, 16, LANES), jnp.float32),
            pltpu.VMEM((count, rows, 2 * LANES), jnp.bfloat16),
            pltpu.VMEM((count, rows, 2 * LANES), jnp.bfloat16),
        ],
        compiler_params=pltpu.CompilerParams(vmem_limit_bytes=VMEM_LIMIT),
        name="transform",
    )(samples, *tables)


def correlate(mine, theirs):
    left = mine.reshape(*mine.shape[:2], -1)
    right_re = theirs.reshape(left.shape)
    right_im = jnp.stack([-theirs[..., 1], theirs[..., 0]], axis=-1).reshape(left.shape)
    vis_re = jnp.einsum("kas,kbs->akb", left, right_re, preferred_element_type=jnp.float32)
    vis_im = jnp.einsum("kas,kbs->akb", left, right_im, preferred_element_type=jnp.float32)
    return jnp.concatenate([vis_re, vis_im], axis=-1) * (1.0 / mine.shape[2])


def by_channel(half, sig_count, spec_count):
    chan_count, per, parts, k2, rows = half.shape
    turned = half.transpose(3, 1, 0, 4, 2).reshape(k2 * per, spec_count, sig_count, parts)
    return turned.transpose(0, 2, 1, 3)


def local(voltages, plan):
    sig_count, frames, block_len = voltages.shape
    chan_count = lax.axis_size("chan")
    group_count = lax.axis_size("grp")
    spec_count = frames - TAPS + 1
    rows = spec_count * sig_count // chan_count
    chan_id = lax.axis_index("chan").astype(jnp.int32)
    group_id = lax.axis_index("grp")

    filtered = filter_taps(voltages.transpose(1, 0, 2), chan_id, chan_count)
    filtered = filtered.reshape(chan_count, rows, block_len)
    frames_here = lax.all_to_all(filtered, "chan", split_axis=0, concat_axis=0, tiled=True)
    spectra = transform(frames_here)
    channel = lax.all_to_all(spectra, "chan", split_axis=0, concat_axis=0, tiled=True)

    lower_half, upper_half = channel[:, 0], channel[:, 1]
    group_ids = jnp.arange(group_count)
    partner = jnp.sum(jnp.where(group_ids[None, :] == group_id, plan, 0), axis=1)
    listed = jnp.any(partner[:, None] == group_ids[None, :], axis=0)
    slot_shape = (group_count,) + (1,) * lower_half.ndim
    chosen_half = jnp.where(
        (group_ids > group_id).reshape(slot_shape), upper_half[None], lower_half[None]
    )
    slots = jnp.where(listed.reshape(slot_shape), chosen_half, jnp.zeros_like(chosen_half))
    received = lax.all_to_all(slots, "grp", split_axis=0, concat_axis=0, tiled=True)
    results = []
    for round_index in range(plan.shape[0]):
        partner_id = partner[round_index]
        upper_flag = (group_id > partner_id).astype(jnp.int32)
        mine = lax.dynamic_index_in_dim(channel, upper_flag, 1, keepdims=False)
        theirs = lax.dynamic_index_in_dim(received, partner_id, 0, keepdims=False)
        results.append(
            correlate(
                by_channel(mine, sig_count, spec_count), by_channel(theirs, sig_count, spec_count)
            )
        )
    return jnp.stack(results).astype(jnp.bfloat16)


def solution(mesh):
    in_specs = (P("grp", None, "chan"), P())
    out_specs = P(None, "grp", "chan", None)
    return jax.shard_map(local, mesh=mesh, in_specs=in_specs, out_specs=out_specs, check_vma=False)
```

```python
import functools
import math

import jax
import jax.numpy as jnp
import numpy as np
from jax import lax
from jax.experimental import pallas as pl
from jax.experimental.pallas import tpu as pltpu
from jax.sharding import PartitionSpec as P

TAPS = 16
LANES = 128
RADIX = 64
VMEM_LIMIT = 60 * 1024 * 1024


def tap_table(fft_len):
    position = np.arange(TAPS * fft_len, dtype=np.float64)
    total = TAPS * fft_len
    window = 0.5 - 0.5 * np.cos(2.0 * np.pi * position / total)
    return (window * np.sinc((position - 0.5 * total) / fft_len)).reshape(TAPS, fft_len)


def filter_kernel(chan_ref, volt_ref, coeff_ref, out_ref):
    del chan_ref
    frames, sig_tile, block_len = volt_ref.shape
    spec_count = frames - TAPS + 1

    def one_tile(tile, carry):
        cols = pl.ds(pl.multiple_of(tile * LANES, LANES), LANES)
        coeff = [
            jnp.broadcast_to(coeff_ref[0, t : t + 1, cols], (sig_tile, LANES)) for t in range(TAPS)
        ]
        total = [None] * spec_count
        for frame in range(frames):
            sample = volt_ref[frame, :, cols].astype(jnp.float32)
            for s in range(max(0, frame - TAPS + 1), min(spec_count - 1, frame) + 1):
                term = coeff[frame - s] * sample
                total[s] = term if total[s] is None else total[s] + term
            if frame >= TAPS - 1:
                s = frame - TAPS + 1
                out_ref[s, :, cols] = total[s].astype(jnp.bfloat16)
                total[s] = None
        return carry

    lax.fori_loop(0, block_len // LANES, one_tile, 0)


def filter_taps(frames_first, chan_id, chan_count):
    frames, sig_count, block_len = frames_first.shape
    spec_count = frames - TAPS + 1
    table = tap_table(block_len * chan_count).astype(np.float32)
    table = np.ascontiguousarray(table.reshape(TAPS, chan_count, block_len).transpose(1, 0, 2))
    sig_tile = 16
    return pl.pallas_call(
        filter_kernel,
        out_shape=jax.ShapeDtypeStruct((spec_count, sig_count, block_len), jnp.bfloat16),
        grid_spec=pltpu.PrefetchScalarGridSpec(
            num_scalar_prefetch=1,
            grid=(sig_count // sig_tile,),
            in_specs=[
                pl.BlockSpec((frames, sig_tile, block_len), lambda i, c: (0, i, 0)),
                pl.BlockSpec((1, TAPS, block_len), lambda i, c: (c[0], 0, 0)),
            ],
            out_specs=pl.BlockSpec((spec_count, sig_tile, block_len), lambda i, c: (0, i, 0)),
        ),
        compiler_params=pltpu.CompilerParams(vmem_limit_bytes=VMEM_LIMIT),
        name="filter_taps",
    )(chan_id.reshape(1), frames_first, jnp.asarray(table))


def cadd(a, b):
    if a is None:
        return b
    if b is None:
        return a
    return a + b


def csub(a, b):
    if b is None:
        return a
    if a is None:
        return -b
    return a - b


def scale_by(value, re, im):
    vr, vi = value
    eps = 1e-12

    def mul(x, f):
        if x is None or abs(f) < eps:
            return None
        if abs(f - 1.0) < eps:
            return x
        if abs(f + 1.0) < eps:
            return -x
        return x * f

    return csub(mul(vr, re), mul(vi, im)), cadd(mul(vr, im), mul(vi, re))


def plus(a, b):
    return cadd(a[0], b[0]), cadd(a[1], b[1])


def minus(a, b):
    return csub(a[0], b[0]), csub(a[1], b[1])


def dft(values, wanted=None):
    n = len(values)
    if n == 1:
        return list(values)
    even = dft(values[0::2])
    odd = dft(values[1::2])
    out = [None] * n
    for k in range(n // 2):
        if wanted is not None and k not in wanted and k + n // 2 not in wanted:
            continue
        angle = -2.0 * math.pi * k / n
        turned = scale_by(odd[k], math.cos(angle), math.sin(angle))
        out[k] = plus(even[k], turned)
        out[k + n // 2] = minus(even[k], turned)
    return out


def first_index_list():
    chosen = []
    for c in range(5):
        for e in range(8):
            k1 = c + 8 * e
            if c in (0, 4) and k1 > RADIX // 2:
                continue
            chosen.append(k1)
    return chosen


def turn_tables(fft_len):
    k1 = np.array(first_index_list())[:, None]
    angle = 2.0 * np.pi * ((k1 * np.arange(LANES)[None, :]) % fft_len) / fft_len
    return np.cos(angle), np.sin(angle)


def wave_matrix(fft_len):
    gain = 1.0 / (64.0 * math.sqrt(fft_len))
    half = LANES // 2
    n2 = np.arange(LANES)[None, :]
    k2 = np.arange(half)[:, None]
    rows = []
    for index, flip in ((k2, 1.0), (LANES - 1 - k2, -1.0)):
        angle = 2.0 * np.pi * ((index * n2) % LANES) / LANES
        cos, sin = np.cos(angle) * gain, np.sin(angle) * gain
        rows.append(np.concatenate([cos, sin], axis=1))
        rows.append(np.concatenate([-sin, cos], axis=1) * flip)
    return np.concatenate(rows, axis=0)


def split_two(value):
    high = value.astype(jnp.bfloat16)
    return high, (value - high.astype(jnp.float32)).astype(jnp.bfloat16)


def transform_kernel(
    chan_count, in_ref, cos_ref, sin_ref, wave_high_ref, wave_low_ref, out_ref, mid_ref, high_ref, low_ref
):
    _, rows, block_len = in_ref.shape
    per_block = block_len // LANES
    tile = 16
    chosen = first_index_list()

    def row_tile(step, carry):
        at = pl.ds(pl.multiple_of(step * tile, tile), tile)
        present = set()
        for low_n in range(8):
            column = []
            for high_n in range(8):
                n1 = high_n * 8 + low_n
                lanes = slice((n1 % per_block) * LANES, (n1 % per_block + 1) * LANES)
                column.append((in_ref[n1 // per_block, at, lanes].astype(jnp.float32), None))
            spread = dft(column, wanted=range(5))
            for c in range(5):
                angle = -2.0 * math.pi * low_n * c / RADIX
                re, im = scale_by(spread[c], math.cos(angle), math.sin(angle))
                for part, value in enumerate((re, im)):
                    if value is not None:
                        mid_ref[low_n, c, part] = value
                        present.add((low_n, c, part))
        for c in range(5):
            wanted = [e for e in range(8) if c + 8 * e in chosen]
            values = []
            for low_n in range(8):
                values.append(
                    tuple(
                        mid_ref[low_n, c, part] if (low_n, c, part) in present else None
                        for part in range(2)
                    )
                )
            spread = dft(values, wanted=wanted)
            for e in wanted:
                place = chosen.index(c + 8 * e)
                cos = cos_ref[place : place + 1, :]
                sin = sin_ref[place : place + 1, :]
                re, im = spread[e]
                if im is None:
                    turned_re, turned_im = re * cos, -(re * sin)
                else:
                    turned_re, turned_im = re * cos + im * sin, im * cos - re * sin
                a, b = split_two(turned_re)
                high_ref[place, at, :LANES] = a
                low_ref[place, at, :LANES] = b
                a, b = split_two(turned_im)
                high_ref[place, at, LANES:] = a
                low_ref[place, at, LANES:] = b
        return carry

    lax.fori_loop(0, rows // tile, row_tile, 0)

    dims = (((1,), (1,)), ((), ()))
    wave_high = wave_high_ref[...]
    wave_low = wave_low_ref[...]
    for first in range(0, len(chosen), 2):
        places = [p for p in (first, first + 1) if p < len(chosen)]
        high = high_ref[first : first + len(places)].reshape(len(places) * rows, 2 * LANES)
        low = low_ref[first : first + len(places)].reshape(len(places) * rows, 2 * LANES)
        total = lax.dot_general(wave_high, high, dims, preferred_element_type=jnp.float32)
        total += lax.dot_general(wave_high, low, dims, preferred_element_type=jnp.float32)
        total += lax.dot_general(wave_low, high, dims, preferred_element_type=jnp.float32)
        total = total.astype(jnp.bfloat16)
        for i, place in enumerate(places):
            k1 = chosen[place]
            columns = total[:, i * rows : (i + 1) * rows]
            quarter = LANES // 4
            for side, index in ((0, k1), (1, RADIX - k1)):
                if side == 1 and (k1 == 0 or k1 == RADIX // 2):
                    continue
                for part in range(2):
                    for half in range(2):
                        at = side * LANES + part * 2 * quarter + half * quarter
                        out_ref[index % chan_count, half, index // chan_count, part] = columns[
                            at : at + quarter
                        ]


def transform(samples):
    chan_count, rows, block_len = samples.shape
    fft_len = chan_count * block_len
    count = len(first_index_list())
    cos, sin = turn_tables(fft_len)
    wave = wave_matrix(fft_len)
    wave_high = wave.astype(jnp.bfloat16)
    wave_low = (wave - wave_high.astype(np.float64)).astype(jnp.bfloat16)
    tables = (
        jnp.asarray(cos, jnp.float32),
        jnp.asarray(sin, jnp.float32),
        jnp.asarray(wave_high),
        jnp.asarray(wave_low),
    )
    whole = pl.BlockSpec(memory_space=pltpu.VMEM)
    return pl.pallas_call(
        functools.partial(transform_kernel, chan_count),
        out_shape=jax.ShapeDtypeStruct(
            (chan_count, 2, RADIX // chan_count, 2, LANES // 4, rows), jnp.bfloat16
        ),
        in_specs=[whole] * 5,
        out_specs=whole,
        scratch_shapes=[
            pltpu.VMEM((8, 5, 2, 16, LANES), jnp.float32),
            pltpu.VMEM((count, rows, 2 * LANES), jnp.bfloat16),
            pltpu.VMEM((count, rows, 2 * LANES), jnp.bfloat16),
        ],
        compiler_params=pltpu.CompilerParams(vmem_limit_bytes=VMEM_LIMIT),
        name="transform",
    )(samples, *tables)


def correlate_kernel(
    sig_count, spec_count, halves_ref, mates_ref, mine_ref, mate_ref, out_ref, left_ref, right_ref, sum_ref
):
    del halves_ref, mates_ref
    chan_count, _, per, parts, k2_tile, lanes = mine_ref.shape
    depth = 2 * parts * chan_count
    channels = per * k2_tile
    eight = 8
    low_lanes = lax.broadcasted_iota(jnp.int32, (eight, lanes), 1) < sig_count

    def roll(value):
        return pltpu.roll(value, sig_count, 1)

    def spread(step, carry):
        source = step // per
        e = step % per
        for k2 in range(0, k2_tile, eight):
            at = pl.ds(k2, eight)
            channel = e * k2_tile + k2

            def put(ref, spectrum, part, value):
                row = channel * depth + (spectrum * chan_count + source) * parts + part
                ref[pl.ds(row, eight, stride=depth), :] = value

            left_re = mine_ref[source, 0, e, 0, at, :].astype(jnp.float32)
            left_im = mine_ref[source, 0, e, 1, at, :].astype(jnp.float32)
            put(left_ref, 0, 0, left_re)
            put(left_ref, 0, 1, left_im)
            put(left_ref, 1, 0, roll(left_re))
            put(left_ref, 1, 1, roll(left_im))
            right_re = mate_ref[0, source, e, 0, at, :].astype(jnp.float32)
            right_im = mate_ref[0, source, e, 1, at, :].astype(jnp.float32)
            turned_re, turned_im = roll(right_re), roll(right_im)
            put(right_ref, 0, 0, jnp.where(low_lanes, right_re, -turned_im))
            put(right_ref, 0, 1, jnp.where(low_lanes, right_im, turned_re))
            put(right_ref, 1, 0, jnp.where(low_lanes, turned_re, -right_im))
            put(right_ref, 1, 1, jnp.where(low_lanes, turned_im, right_re))
        return carry

    lax.fori_loop(0, chan_count * per, spread, 0)

    def pair(step, carry):
        e = step // (k2_tile // 2)
        k2 = (step % (k2_tile // 2)) * 2
        first = pl.multiple_of((e * k2_tile + k2) * depth, 2 * depth)
        left = left_ref[pl.ds(first, 2 * depth), :].T[:sig_count].astype(jnp.bfloat16)
        right = right_ref[pl.ds(first, 2 * depth), :].astype(jnp.bfloat16)
        zero = jnp.zeros((depth, lanes), jnp.bfloat16)
        weights = jnp.concatenate(
            [
                jnp.concatenate([right[:depth], zero], axis=1),
                jnp.concatenate([zero, right[depth:]], axis=1),
            ],
            axis=0,
        )
        both = jnp.dot(left, weights, preferred_element_type=jnp.float32)
        for i in range(2):
            q = e + per * (k2 + i)
            for a in range(0, sig_count, eight):
                sum_ref[pl.ds(a * channels + q, eight, stride=channels), :] = both[
                    a : a + eight, i * lanes : (i + 1) * lanes
                ]
        return carry

    lax.fori_loop(0, channels // 2, pair, 0, unroll=4)

    def finish(a, carry):
        rows = pl.ds(pl.multiple_of(a * channels, channels), channels)
        out_ref[0, a] = (sum_ref[rows, :] * (1.0 / spec_count)).astype(jnp.bfloat16)
        return carry

    lax.fori_loop(0, sig_count, finish, 0)


def correlate(mine, theirs, halves, mates, sig_count, spec_count):
    chan_count, _, per, parts, k2_count, lanes = mine.shape
    rounds = halves.shape[0]
    k2_tile = 16
    channels = per * k2_tile
    depth = 2 * parts * chan_count
    return pl.pallas_call(
        functools.partial(correlate_kernel, sig_count, spec_count),
        out_shape=jax.ShapeDtypeStruct(
            (rounds, sig_count, per * k2_count, 2 * sig_count), jnp.bfloat16
        ),
        grid_spec=pltpu.PrefetchScalarGridSpec(
            num_scalar_prefetch=2,
            grid=(rounds, k2_count // k2_tile),
            in_specs=[
                pl.BlockSpec(
                    (chan_count, 1, per, parts, k2_tile, lanes),
                    lambda r, i, h, m: (0, h[r], 0, 0, i, 0),
                ),
                pl.BlockSpec(
                    (1, chan_count, per, parts, k2_tile, lanes),
                    lambda r, i, h, m: (m[r], 0, 0, 0, i, 0),
                ),
            ],
            out_specs=pl.BlockSpec(
                (1, sig_count, channels, 2 * sig_count), lambda r, i, h, m: (r, 0, i, 0)
            ),
            scratch_shapes=[
                pltpu.VMEM((channels * depth, lanes), jnp.float32),
                pltpu.VMEM((channels * depth, lanes), jnp.float32),
                pltpu.VMEM((sig_count * channels, lanes), jnp.float32),
            ],
        ),
        compiler_params=pltpu.CompilerParams(vmem_limit_bytes=VMEM_LIMIT),
        name="correlate",
    )(halves, mates, mine, theirs)


def correlate_plain(mine, theirs):
    left = mine.reshape(*mine.shape[:2], -1)
    right_re = theirs.reshape(left.shape)
    right_im = jnp.stack([-theirs[..., 1], theirs[..., 0]], axis=-1).reshape(left.shape)
    vis_re = jnp.einsum("kas,kbs->akb", left, right_re, preferred_element_type=jnp.float32)
    vis_im = jnp.einsum("kas,kbs->akb", left, right_im, preferred_element_type=jnp.float32)
    return jnp.concatenate([vis_re, vis_im], axis=-1) * (1.0 / mine.shape[2])


def by_channel(half, sig_count, spec_count):
    chan_count, per, parts, k2, rows = half.shape
    turned = half.transpose(3, 1, 0, 4, 2).reshape(k2 * per, spec_count, sig_count, parts)
    return turned.transpose(0, 2, 1, 3)


def local(voltages, plan):
    sig_count, frames, block_len = voltages.shape
    chan_count = lax.axis_size("chan")
    group_count = lax.axis_size("grp")
    spec_count = frames - TAPS + 1
    rows = spec_count * sig_count // chan_count
    chan_id = lax.axis_index("chan").astype(jnp.int32)
    group_id = lax.axis_index("grp")

    filtered = filter_taps(voltages.transpose(1, 0, 2), chan_id, chan_count)
    filtered = filtered.reshape(chan_count, rows, block_len)
    frames_here = lax.all_to_all(filtered, "chan", split_axis=0, concat_axis=0, tiled=True)
    spectra = transform(frames_here)
    channel = lax.all_to_all(spectra, "chan", split_axis=0, concat_axis=0, tiled=True)

    lower_half, upper_half = channel[:, 0], channel[:, 1]
    group_ids = jnp.arange(group_count)
    partner = jnp.sum(jnp.where(group_ids[None, :] == group_id, plan, 0), axis=1)
    listed = jnp.any(partner[:, None] == group_ids[None, :], axis=0)
    slot_shape = (group_count,) + (1,) * lower_half.ndim
    chosen_half = jnp.where(
        (group_ids > group_id).reshape(slot_shape), upper_half[None], lower_half[None]
    )
    slots = jnp.where(listed.reshape(slot_shape), chosen_half, jnp.zeros_like(chosen_half))
    received = lax.all_to_all(slots, "grp", split_axis=0, concat_axis=0, tiled=True)
    halves = (group_id > partner).astype(jnp.int32)
    if rows == LANES and rows == 2 * sig_count:
        return correlate(channel, received, halves, partner, sig_count, spec_count)
    results = []
    for round_index in range(plan.shape[0]):
        mine = lax.dynamic_index_in_dim(channel, halves[round_index], 1, keepdims=False)
        theirs = lax.dynamic_index_in_dim(received, partner[round_index], 0, keepdims=False)
        results.append(
            correlate_plain(
                by_channel(mine, sig_count, spec_count), by_channel(theirs, sig_count, spec_count)
            )
        )
    return jnp.stack(results).astype(jnp.bfloat16)


def solution(mesh):
    in_specs = (P("grp", None, "chan"), P())
    out_specs = P(None, "grp", "chan", None)
    return jax.shard_map(local, mesh=mesh, in_specs=in_specs, out_specs=out_specs, check_vma=False)
```

```python
import functools
import math

import jax
import jax.numpy as jnp
import numpy as np
from jax import lax
from jax.experimental import pallas as pl
from jax.experimental.pallas import tpu as pltpu
from jax.sharding import PartitionSpec as P

TAPS = 16
LANES = 128
RADIX = 64
VMEM_LIMIT = 60 * 1024 * 1024


def tap_table(fft_len):
    position = np.arange(TAPS * fft_len, dtype=np.float64)
    total = TAPS * fft_len
    window = 0.5 - 0.5 * np.cos(2.0 * np.pi * position / total)
    return (window * np.sinc((position - 0.5 * total) / fft_len)).reshape(TAPS, fft_len)


def filter_kernel(chan_ref, volt_ref, coeff_ref, out_ref):
    del chan_ref
    frames, sig_tile, block_len = volt_ref.shape
    spec_count = frames - TAPS + 1

    def one_tile(tile, carry):
        cols = pl.ds(pl.multiple_of(tile * LANES, LANES), LANES)
        coeff = [
            jnp.broadcast_to(coeff_ref[0, t : t + 1, cols], (sig_tile, LANES)) for t in range(TAPS)
        ]
        total = [None] * spec_count
        for frame in range(frames):
            sample = volt_ref[frame, :, cols].astype(jnp.float32)
            for s in range(max(0, frame - TAPS + 1), min(spec_count - 1, frame) + 1):
                term = coeff[frame - s] * sample
                total[s] = term if total[s] is None else total[s] + term
            if frame >= TAPS - 1:
                s = frame - TAPS + 1
                out_ref[s, :, cols] = total[s].astype(jnp.bfloat16)
                total[s] = None
        return carry

    lax.fori_loop(0, block_len // LANES, one_tile, 0)


def filter_taps(frames_first, chan_id, chan_count, first, spec_count):
    _, sig_count, block_len = frames_first.shape
    frames = spec_count + TAPS - 1
    table = tap_table(block_len * chan_count).astype(np.float32)
    table = np.ascontiguousarray(table.reshape(TAPS, chan_count, block_len).transpose(1, 0, 2))
    sig_tile = 16
    return pl.pallas_call(
        filter_kernel,
        out_shape=jax.ShapeDtypeStruct((spec_count, sig_count, block_len), jnp.bfloat16),
        grid_spec=pltpu.PrefetchScalarGridSpec(
            num_scalar_prefetch=1,
            grid=(sig_count // sig_tile,),
            in_specs=[
                pl.BlockSpec(
                    (pl.Element(frames), pl.Element(sig_tile), pl.Element(block_len)),
                    lambda i, c: (first, i * sig_tile, 0),
                ),
                pl.BlockSpec((1, TAPS, block_len), lambda i, c: (c[0], 0, 0)),
            ],
            out_specs=pl.BlockSpec((spec_count, sig_tile, block_len), lambda i, c: (0, i, 0)),
        ),
        compiler_params=pltpu.CompilerParams(vmem_limit_bytes=VMEM_LIMIT),
        name="filter_taps",
    )(chan_id.reshape(1), frames_first, jnp.asarray(table))


def cadd(a, b):
    if a is None:
        return b
    if b is None:
        return a
    return a + b


def csub(a, b):
    if b is None:
        return a
    if a is None:
        return -b
    return a - b


def scale_by(value, re, im):
    vr, vi = value
    eps = 1e-12

    def mul(x, f):
        if x is None or abs(f) < eps:
            return None
        if abs(f - 1.0) < eps:
            return x
        if abs(f + 1.0) < eps:
            return -x
        return x * f

    return csub(mul(vr, re), mul(vi, im)), cadd(mul(vr, im), mul(vi, re))


def plus(a, b):
    return cadd(a[0], b[0]), cadd(a[1], b[1])


def minus(a, b):
    return csub(a[0], b[0]), csub(a[1], b[1])


def dft(values, wanted=None):
    n = len(values)
    if n == 1:
        return list(values)
    even = dft(values[0::2])
    odd = dft(values[1::2])
    out = [None] * n
    for k in range(n // 2):
        if wanted is not None and k not in wanted and k + n // 2 not in wanted:
            continue
        angle = -2.0 * math.pi * k / n
        turned = scale_by(odd[k], math.cos(angle), math.sin(angle))
        out[k] = plus(even[k], turned)
        out[k + n // 2] = minus(even[k], turned)
    return out


def first_index_list():
    chosen = []
    for c in range(5):
        for e in range(8):
            k1 = c + 8 * e
            if c in (0, 4) and k1 > RADIX // 2:
                continue
            chosen.append(k1)
    return chosen


def turn_tables(fft_len):
    k1 = np.array(first_index_list())[:, None]
    angle = 2.0 * np.pi * ((k1 * np.arange(LANES)[None, :]) % fft_len) / fft_len
    return np.cos(angle), np.sin(angle)


def wave_matrix(fft_len):
    gain = 1.0 / (64.0 * math.sqrt(fft_len))
    half = LANES // 2
    n2 = np.arange(LANES)[None, :]
    k2 = np.arange(half)[:, None]
    rows = []
    for index, flip in ((k2, 1.0), (LANES - 1 - k2, -1.0)):
        angle = 2.0 * np.pi * ((index * n2) % LANES) / LANES
        cos, sin = np.cos(angle) * gain, np.sin(angle) * gain
        rows.append(np.concatenate([cos, sin], axis=1))
        rows.append(np.concatenate([-sin, cos], axis=1) * flip)
    return np.concatenate(rows, axis=0)


def split_two(value):
    high = value.astype(jnp.bfloat16)
    return high, (value - high.astype(jnp.float32)).astype(jnp.bfloat16)


def transform_kernel(
    chan_count, joined, in_ref, cos_ref, sin_ref, wave_high_ref, wave_low_ref, out_ref, mid_ref, high_ref, low_ref
):
    _, rows, block_len = in_ref.shape
    per_block = block_len // LANES
    tile = 16
    chosen = first_index_list()

    def row_tile(step, carry):
        at = pl.ds(pl.multiple_of(step * tile, tile), tile)
        present = set()
        for low_n in range(8):
            column = []
            for high_n in range(8):
                n1 = high_n * 8 + low_n
                lanes = slice((n1 % per_block) * LANES, (n1 % per_block + 1) * LANES)
                column.append((in_ref[n1 // per_block, at, lanes].astype(jnp.float32), None))
            spread = dft(column, wanted=range(5))
            for c in range(5):
                angle = -2.0 * math.pi * low_n * c / RADIX
                re, im = scale_by(spread[c], math.cos(angle), math.sin(angle))
                for part, value in enumerate((re, im)):
                    if value is not None:
                        mid_ref[low_n, c, part] = value
                        present.add((low_n, c, part))
        for c in range(5):
            wanted = [e for e in range(8) if c + 8 * e in chosen]
            values = []
            for low_n in range(8):
                values.append(
                    tuple(
                        mid_ref[low_n, c, part] if (low_n, c, part) in present else None
                        for part in range(2)
                    )
                )
            spread = dft(values, wanted=wanted)
            for e in wanted:
                place = chosen.index(c + 8 * e)
                cos = cos_ref[place : place + 1, :]
                sin = sin_ref[place : place + 1, :]
                re, im = spread[e]
                if im is None:
                    turned_re, turned_im = re * cos, -(re * sin)
                else:
                    turned_re, turned_im = re * cos + im * sin, im * cos - re * sin
                a, b = split_two(turned_re)
                high_ref[place, at, :LANES] = a
                low_ref[place, at, :LANES] = b
                a, b = split_two(turned_im)
                high_ref[place, at, LANES:] = a
                low_ref[place, at, LANES:] = b
        return carry

    lax.fori_loop(0, rows // tile, row_tile, 0)

    dims = (((1,), (1,)), ((), ()))
    wave_high = wave_high_ref[...]
    wave_low = wave_low_ref[...]
    quarter = LANES // 4
    group = max(2, 2 * LANES // rows)
    for first in range(0, len(chosen), group):
        places = range(first, min(first + group, len(chosen)))
        high = high_ref[first : first + len(places)].reshape(len(places) * rows, 2 * LANES)
        low = low_ref[first : first + len(places)].reshape(len(places) * rows, 2 * LANES)
        total = lax.dot_general(wave_high, high, dims, preferred_element_type=jnp.float32)
        total += lax.dot_general(wave_high, low, dims, preferred_element_type=jnp.float32)
        total += lax.dot_general(wave_low, high, dims, preferred_element_type=jnp.float32)

        def put(place, side, half, part, value):
            k1 = chosen[place]
            if side == 1 and (k1 == 0 or k1 == RADIX // 2):
                return
            index = RADIX - k1 if side else k1
            at = (index % chan_count, half, index // chan_count)
            if not joined:
                at += (part,)
            out_ref[at] = value.astype(jnp.bfloat16)

        for side in range(2):
            for half in range(2):
                row_re = side * LANES + half * quarter
                row_im = row_re + 2 * quarter
                if not joined:
                    for i, place in enumerate(places):
                        columns = slice(i * rows, (i + 1) * rows)
                        put(place, side, half, 0, total[row_re : row_re + quarter, columns])
                        put(place, side, half, 1, total[row_im : row_im + quarter, columns])
                    continue
                for i in range(0, len(places), 2):
                    columns = slice(i * rows, min((i + 2) * rows, len(places) * rows))
                    re = total[row_re : row_re + quarter, columns]
                    im = total[row_im : row_im + quarter, columns]
                    if i + 1 == len(places):
                        put(places[i], side, half, 0, jnp.concatenate([re, im], axis=1))
                        continue
                    low_lanes = lax.broadcasted_iota(jnp.int32, re.shape, 1) < rows
                    put(places[i], side, half, 0, jnp.where(low_lanes, re, pltpu.roll(im, rows, 1)))
                    put(
                        places[i + 1], side, half, 0, jnp.where(low_lanes, pltpu.roll(re, rows, 1), im)
                    )


def transform(samples, joined):
    chan_count, rows, block_len = samples.shape
    fft_len = chan_count * block_len
    count = len(first_index_list())
    cos, sin = turn_tables(fft_len)
    wave = wave_matrix(fft_len)
    wave_high = wave.astype(jnp.bfloat16)
    wave_low = (wave - wave_high.astype(np.float64)).astype(jnp.bfloat16)
    tables = (
        jnp.asarray(cos, jnp.float32),
        jnp.asarray(sin, jnp.float32),
        jnp.asarray(wave_high),
        jnp.asarray(wave_low),
    )
    whole = pl.BlockSpec(memory_space=pltpu.VMEM)
    shape = (chan_count, 2, RADIX // chan_count)
    shape += (LANES // 4, 2 * rows) if joined else (2, LANES // 4, rows)
    return pl.pallas_call(
        functools.partial(transform_kernel, chan_count, joined),
        out_shape=jax.ShapeDtypeStruct(shape, jnp.bfloat16),
        in_specs=[whole] * 5,
        out_specs=whole,
        scratch_shapes=[
            pltpu.VMEM((8, 5, 2, 16, LANES), jnp.float32),
            pltpu.VMEM((count, rows, 2 * LANES), jnp.bfloat16),
            pltpu.VMEM((count, rows, 2 * LANES), jnp.bfloat16),
        ],
        compiler_params=pltpu.CompilerParams(vmem_limit_bytes=VMEM_LIMIT),
        name="transform",
    )(samples, *tables)


EIGHT = 8


def turn_kernel(in_ref, out_ref, wide_ref):
    chan_count, _, per, k2_count, lanes = in_ref.shape
    channels = per * k2_count

    def spread(step, carry):
        source, e = step // per, step % per
        for k2 in range(0, k2_count, EIGHT):
            value = in_ref[source, 0, e, k2 : k2 + EIGHT, :].astype(jnp.float32)
            row = (e + per * k2) * chan_count + source
            wide_ref[pl.ds(row, EIGHT, stride=per * chan_count), :] = value
        return carry

    lax.fori_loop(0, chan_count * per, spread, 0, unroll=4)

    def narrow(step, carry):
        base = pl.multiple_of(step * EIGHT, EIGHT)
        rows = pl.ds(pl.multiple_of(step * EIGHT * chan_count, EIGHT * chan_count), EIGHT * chan_count)
        value = wide_ref[rows, :].astype(jnp.bfloat16)
        out_ref[0, pl.ds(base, EIGHT)] = value.reshape(EIGHT, chan_count, lanes)
        return carry

    lax.fori_loop(0, channels // EIGHT, narrow, 0, unroll=2)


def turn(channel):
    chan_count, halves, per, k2_count, lanes = channel.shape
    channels = per * k2_count
    return pl.pallas_call(
        turn_kernel,
        out_shape=jax.ShapeDtypeStruct((halves, channels, chan_count, lanes), jnp.bfloat16),
        grid=(halves,),
        in_specs=[
            pl.BlockSpec((chan_count, 1, per, k2_count, lanes), lambda u: (0, u, 0, 0, 0))
        ],
        out_specs=pl.BlockSpec((1, channels, chan_count, lanes), lambda u: (u, 0, 0, 0)),
        scratch_shapes=[pltpu.VMEM((channels * chan_count, lanes), jnp.float32)],
        compiler_params=pltpu.CompilerParams(vmem_limit_bytes=VMEM_LIMIT),
        name="turn",
    )(channel)


def left_kernel(*refs):
    chunk_refs, out_ref = refs[:-1], refs[-1]
    _, channels, _, lanes = chunk_refs[0].shape
    sig_count = lanes // 2

    def pair(step, carry):
        rows = []
        for i in range(2):
            values = [ref[0, 2 * step + i].astype(jnp.float32) for ref in chunk_refs]
            rows += values + [pltpu.roll(value, sig_count, 1) for value in values]
        stacked = jnp.concatenate(rows, axis=0)
        out_ref[0, step] = stacked.T[:sig_count].astype(jnp.bfloat16)
        return carry

    lax.fori_loop(0, channels // 2, pair, 0, unroll=4)


def left_operand(chunks):
    halves, channels, chan_count, lanes = chunks[0].shape
    depth = 2 * 2 * len(chunks) * chan_count
    tile = 64
    return pl.pallas_call(
        left_kernel,
        out_shape=jax.ShapeDtypeStruct((halves, channels // 2, lanes // 2, depth), jnp.bfloat16),
        grid=(halves, channels // tile),
        in_specs=[pl.BlockSpec((1, tile, chan_count, lanes), lambda u, i: (u, i, 0, 0))]
        * len(chunks),
        out_specs=pl.BlockSpec((1, tile // 2, lanes // 2, depth), lambda u, i: (u, i, 0, 0)),
        compiler_params=pltpu.CompilerParams(vmem_limit_bytes=VMEM_LIMIT),
        name="left_operand",
    )(*chunks)


def correlate_kernel(chunk_count, spec_count, place_ref, left_ref, *refs):
    del place_ref
    chunk_refs = refs[:chunk_count]
    out_ref, sum_ref = refs[-2:]
    _, channels, chan_count, lanes = (1,) + chunk_refs[0].shape
    sig_count = lanes // 2
    sign = jnp.where(
        lax.broadcasted_iota(jnp.int32, (chan_count, lanes), 1) < sig_count, 1.0, -1.0
    ).astype(jnp.float32)

    def pair(step, carry):
        blocks = []
        for i in range(2):
            values = [ref[2 * step + i].astype(jnp.float32) for ref in chunk_refs]
            rows = [value * sign for value in values]
            rows += [pltpu.roll(value, sig_count, 1) for value in values]
            blocks.append(jnp.concatenate(rows, axis=0).astype(jnp.bfloat16))
        zero = jnp.zeros_like(blocks[0])
        weights = jnp.concatenate(
            [
                jnp.concatenate([blocks[0], zero], axis=1),
                jnp.concatenate([zero, blocks[1]], axis=1),
            ],
            axis=0,
        )
        both = jnp.dot(left_ref[0, step], weights, preferred_element_type=jnp.float32)
        for i in range(2):
            q = 2 * step + i
            for a in range(0, sig_count, EIGHT):
                sum_ref[pl.ds(a * channels + q, EIGHT, stride=channels), :] = both[
                    a : a + EIGHT, i * lanes : (i + 1) * lanes
                ]
        return carry

    lax.fori_loop(0, channels // 2, pair, 0, unroll=4)

    def finish(a, carry):
        rows = pl.ds(pl.multiple_of(a * channels, channels), channels)
        out_ref[0, a] = (sum_ref[rows, :] * (1.0 / spec_count)).astype(jnp.bfloat16)
        return carry

    lax.fori_loop(0, sig_count, finish, 0, unroll=4)


def correlate(left, chunks, place, rounds, spec_count, so_far):
    channels, chan_count, lanes = chunks[0].shape
    sig_count, depth = left.shape[2:]
    tile = 32
    in_specs = [
        pl.BlockSpec((1, tile // 2, sig_count, depth), lambda i, p: (p[1], i, 0, 0)),
    ] + [pl.BlockSpec((tile, chan_count, lanes), lambda i, p: (i, 0, 0))] * len(chunks)
    operands = [left, *chunks]
    aliases = {}
    if so_far is not None:
        in_specs.append(pl.BlockSpec(memory_space=pl.ANY))
        operands.append(so_far)
        aliases = {len(operands): 0}
    return pl.pallas_call(
        functools.partial(correlate_kernel, len(chunks), spec_count),
        out_shape=jax.ShapeDtypeStruct((rounds, sig_count, channels, lanes), jnp.bfloat16),
        grid_spec=pltpu.PrefetchScalarGridSpec(
            num_scalar_prefetch=1,
            grid=(channels // tile,),
            in_specs=in_specs,
            out_specs=pl.BlockSpec((1, sig_count, tile, lanes), lambda i, p: (p[0], 0, i, 0)),
            scratch_shapes=[pltpu.VMEM((sig_count * tile, lanes), jnp.float32)],
        ),
        input_output_aliases=aliases,
        compiler_params=pltpu.CompilerParams(vmem_limit_bytes=VMEM_LIMIT),
        name="correlate",
    )(place, *operands)


def correlate_plain(mine, theirs):
    left = mine.reshape(*mine.shape[:2], -1)
    right_re = theirs.reshape(left.shape)
    right_im = jnp.stack([-theirs[..., 1], theirs[..., 0]], axis=-1).reshape(left.shape)
    vis_re = jnp.einsum("kas,kbs->akb", left, right_re, preferred_element_type=jnp.float32)
    vis_im = jnp.einsum("kas,kbs->akb", left, right_im, preferred_element_type=jnp.float32)
    return jnp.concatenate([vis_re, vis_im], axis=-1) * (1.0 / mine.shape[2])


def by_channel(half, sig_count, spec_count):
    chan_count, per, parts, k2, rows = half.shape
    turned = half.transpose(3, 1, 0, 4, 2).reshape(k2 * per, spec_count, sig_count, parts)
    return turned.transpose(0, 2, 1, 3)


def local_plain(voltages, plan):
    sig_count, frames, block_len = voltages.shape
    chan_count = lax.axis_size("chan")
    group_count = lax.axis_size("grp")
    spec_count = frames - TAPS + 1
    rows = spec_count * sig_count // chan_count
    chan_id = lax.axis_index("chan").astype(jnp.int32)
    group_id = lax.axis_index("grp")

    filtered = filter_taps(voltages.transpose(1, 0, 2), chan_id, chan_count, 0, spec_count)
    filtered = filtered.reshape(chan_count, rows, block_len)
    frames_here = lax.all_to_all(filtered, "chan", split_axis=0, concat_axis=0, tiled=True)
    spectra = transform(frames_here, False)
    channel = lax.all_to_all(spectra, "chan", split_axis=0, concat_axis=0, tiled=True)

    lower_half, upper_half = channel[:, 0], channel[:, 1]
    group_ids = jnp.arange(group_count)
    partner = jnp.sum(jnp.where(group_ids[None, :] == group_id, plan, 0), axis=1)
    listed = jnp.any(partner[:, None] == group_ids[None, :], axis=0)
    slot_shape = (group_count,) + (1,) * lower_half.ndim
    chosen_half = jnp.where(
        (group_ids > group_id).reshape(slot_shape), upper_half[None], lower_half[None]
    )
    slots = jnp.where(listed.reshape(slot_shape), chosen_half, jnp.zeros_like(chosen_half))
    received = lax.all_to_all(slots, "grp", split_axis=0, concat_axis=0, tiled=True)
    halves = (group_id > partner).astype(jnp.int32)
    results = []
    for round_index in range(plan.shape[0]):
        mine = lax.dynamic_index_in_dim(channel, halves[round_index], 1, keepdims=False)
        theirs = lax.dynamic_index_in_dim(received, partner[round_index], 0, keepdims=False)
        results.append(
            correlate_plain(
                by_channel(mine, sig_count, spec_count), by_channel(theirs, sig_count, spec_count)
            )
        )
    return jnp.stack(results).astype(jnp.bfloat16)


def local_overlapped(voltages, plan):
    _, frames, _ = voltages.shape
    chan_count = lax.axis_size("chan")
    group_count = lax.axis_size("grp")
    rounds = plan.shape[0]
    spec_count = frames - TAPS + 1
    chan_id = lax.axis_index("chan").astype(jnp.int32)
    group_id = lax.axis_index("grp").astype(jnp.int32)
    frames_first = voltages.transpose(1, 0, 2)

    def over_chan(value):
        return lax.all_to_all(value, "chan", split_axis=0, concat_axis=0, tiled=True)

    def to_mate(value, distance):
        return lax.ppermute(value, "grp", [(g, g ^ distance) for g in range(group_count)])

    group_ids = jnp.arange(group_count, dtype=jnp.int32)
    partner = jnp.sum(jnp.where(group_ids[None, :] == group_id, plan, 0), axis=1)
    turned, near, across, relayed = [], [], [], []
    for first in range(0, spec_count, chan_count):
        filtered = filter_taps(frames_first, chan_id, chan_count, first, chan_count)
        channel = over_chan(transform(over_chan(filtered), True))
        halves = turn(channel)
        turned.append(halves)
        for_near = lax.dynamic_index_in_dim(halves, 1 - group_id % 2, 0, keepdims=False)
        for_across = lax.dynamic_index_in_dim(halves, 1 - group_id // 2, 0, keepdims=False)
        near.append(to_mate(for_near, 1))
        across.append(to_mate(for_across, 2))
        relayed.append(to_mate(across[-1], 1))
    left = left_operand(turned)
    result = None
    for distance, chunks in ((1, near), (2, across), (3, relayed)):
        mate = group_id ^ distance
        round_of = jnp.sum(jnp.where(partner == mate, jnp.arange(rounds, dtype=jnp.int32), 0))
        place = jnp.stack([round_of, (group_id > mate).astype(jnp.int32)])
        result = correlate(left, chunks, place, rounds, spec_count, result)
    return result


def local(voltages, plan):
    sig_count, frames, _ = voltages.shape
    chan_count = lax.axis_size("chan")
    group_count = lax.axis_size("grp")
    if (
        group_count == 4
        and plan.shape[0] == group_count - 1
        and chan_count == EIGHT
        and (frames - TAPS + 1) % chan_count == 0
        and 2 * sig_count == LANES
    ):
        return local_overlapped(voltages, plan)
    return local_plain(voltages, plan)


def solution(mesh):
    in_specs = (P("grp", None, "chan"), P())
    out_specs = P(None, "grp", "chan", None)
    return jax.shard_map(local, mesh=mesh, in_specs=in_specs, out_specs=out_specs, check_vma=False)
```

```python
import functools
import math

import jax
import jax.numpy as jnp
import numpy as np
from jax import lax
from jax.experimental import pallas as pl
from jax.experimental.pallas import tpu as pltpu
from jax.sharding import PartitionSpec as P

TAPS = 16
LANES = 128
RADIX = 64
VMEM_LIMIT = 60 * 1024 * 1024


def tap_table(fft_len):
    position = np.arange(TAPS * fft_len, dtype=np.float64)
    total = TAPS * fft_len
    window = 0.5 - 0.5 * np.cos(2.0 * np.pi * position / total)
    return (window * np.sinc((position - 0.5 * total) / fft_len)).reshape(TAPS, fft_len)


def filter_kernel(chan_ref, volt_ref, coeff_ref, out_ref):
    del chan_ref
    frames, sig_tile, block_len = volt_ref.shape
    spec_count = frames - TAPS + 1

    def one_tile(tile, carry):
        cols = pl.ds(pl.multiple_of(tile * LANES, LANES), LANES)
        coeff = [
            jnp.broadcast_to(coeff_ref[0, t : t + 1, cols], (sig_tile, LANES)) for t in range(TAPS)
        ]
        total = [None] * spec_count
        for frame in range(frames):
            sample = volt_ref[frame, :, cols].astype(jnp.float32)
            for s in range(max(0, frame - TAPS + 1), min(spec_count - 1, frame) + 1):
                term = coeff[frame - s] * sample
                total[s] = term if total[s] is None else total[s] + term
            if frame >= TAPS - 1:
                s = frame - TAPS + 1
                out_ref[s, :, cols] = total[s].astype(jnp.bfloat16)
                total[s] = None
        return carry

    lax.fori_loop(0, block_len // LANES, one_tile, 0)


def filter_taps(frames_first, chan_id, chan_count, first, spec_count):
    _, sig_count, block_len = frames_first.shape
    frames = spec_count + TAPS - 1
    table = tap_table(block_len * chan_count).astype(np.float32)
    table = np.ascontiguousarray(table.reshape(TAPS, chan_count, block_len).transpose(1, 0, 2))
    sig_tile = 16
    return pl.pallas_call(
        filter_kernel,
        out_shape=jax.ShapeDtypeStruct((spec_count, sig_count, block_len), jnp.bfloat16),
        grid_spec=pltpu.PrefetchScalarGridSpec(
            num_scalar_prefetch=1,
            grid=(sig_count // sig_tile,),
            in_specs=[
                pl.BlockSpec(
                    (pl.Element(frames), pl.Element(sig_tile), pl.Element(block_len)),
                    lambda i, c: (first, i * sig_tile, 0),
                ),
                pl.BlockSpec((1, TAPS, block_len), lambda i, c: (c[0], 0, 0)),
            ],
            out_specs=pl.BlockSpec((spec_count, sig_tile, block_len), lambda i, c: (0, i, 0)),
        ),
        compiler_params=pltpu.CompilerParams(vmem_limit_bytes=VMEM_LIMIT),
        name="filter_taps",
    )(chan_id.reshape(1), frames_first, jnp.asarray(table))


def cadd(a, b):
    if a is None:
        return b
    if b is None:
        return a
    return a + b


def csub(a, b):
    if b is None:
        return a
    if a is None:
        return -b
    return a - b


def scale_by(value, re, im):
    vr, vi = value
    eps = 1e-12

    def mul(x, f):
        if x is None or abs(f) < eps:
            return None
        if abs(f - 1.0) < eps:
            return x
        if abs(f + 1.0) < eps:
            return -x
        return x * f

    return csub(mul(vr, re), mul(vi, im)), cadd(mul(vr, im), mul(vi, re))


def plus(a, b):
    return cadd(a[0], b[0]), cadd(a[1], b[1])


def minus(a, b):
    return csub(a[0], b[0]), csub(a[1], b[1])


def dft(values, wanted=None):
    n = len(values)
    if n == 1:
        return list(values)
    even = dft(values[0::2])
    odd = dft(values[1::2])
    out = [None] * n
    for k in range(n // 2):
        if wanted is not None and k not in wanted and k + n // 2 not in wanted:
            continue
        angle = -2.0 * math.pi * k / n
        turned = scale_by(odd[k], math.cos(angle), math.sin(angle))
        out[k] = plus(even[k], turned)
        out[k + n // 2] = minus(even[k], turned)
    return out


def first_index_list():
    chosen = []
    for c in range(5):
        for e in range(8):
            k1 = c + 8 * e
            if c in (0, 4) and k1 > RADIX // 2:
                continue
            chosen.append(k1)
    return chosen


def turn_tables(fft_len):
    k1 = np.array(first_index_list())[:, None]
    angle = 2.0 * np.pi * ((k1 * np.arange(LANES)[None, :]) % fft_len) / fft_len
    return np.cos(angle), np.sin(angle)


def wave_matrix(fft_len):
    gain = 1.0 / (64.0 * math.sqrt(fft_len))
    half = LANES // 2
    n2 = np.arange(LANES)[None, :]
    k2 = np.arange(half)[:, None]
    rows = []
    for index, flip in ((k2, 1.0), (LANES - 1 - k2, -1.0)):
        angle = 2.0 * np.pi * ((index * n2) % LANES) / LANES
        cos, sin = np.cos(angle) * gain, np.sin(angle) * gain
        rows.append(np.concatenate([cos, sin], axis=1))
        rows.append(np.concatenate([-sin, cos], axis=1) * flip)
    return np.concatenate(rows, axis=0)


def split_two(value):
    high = value.astype(jnp.bfloat16)
    return high, (value - high.astype(jnp.float32)).astype(jnp.bfloat16)


def transform_kernel(
    chan_count, joined, in_ref, cos_ref, sin_ref, wave_high_ref, wave_low_ref, out_ref, mid_ref, high_ref, low_ref
):
    _, rows, block_len = in_ref.shape
    per_block = block_len // LANES
    tile = 16
    chosen = first_index_list()

    def row_tile(step, carry):
        at = pl.ds(pl.multiple_of(step * tile, tile), tile)
        present = set()
        for low_n in range(8):
            column = []
            for high_n in range(8):
                n1 = high_n * 8 + low_n
                lanes = slice((n1 % per_block) * LANES, (n1 % per_block + 1) * LANES)
                column.append((in_ref[n1 // per_block, at, lanes].astype(jnp.float32), None))
            spread = dft(column, wanted=range(5))
            for c in range(5):
                angle = -2.0 * math.pi * low_n * c / RADIX
                re, im = scale_by(spread[c], math.cos(angle), math.sin(angle))
                for part, value in enumerate((re, im)):
                    if value is not None:
                        mid_ref[low_n, c, part] = value
                        present.add((low_n, c, part))
        for c in range(5):
            wanted = [e for e in range(8) if c + 8 * e in chosen]
            values = []
            for low_n in range(8):
                values.append(
                    tuple(
                        mid_ref[low_n, c, part] if (low_n, c, part) in present else None
                        for part in range(2)
                    )
                )
            spread = dft(values, wanted=wanted)
            for e in wanted:
                place = chosen.index(c + 8 * e)
                cos = cos_ref[place : place + 1, :]
                sin = sin_ref[place : place + 1, :]
                re, im = spread[e]
                if im is None:
                    turned_re, turned_im = re * cos, -(re * sin)
                else:
                    turned_re, turned_im = re * cos + im * sin, im * cos - re * sin
                a, b = split_two(turned_re)
                high_ref[place, at, :LANES] = a
                low_ref[place, at, :LANES] = b
                a, b = split_two(turned_im)
                high_ref[place, at, LANES:] = a
                low_ref[place, at, LANES:] = b
        return carry

    lax.fori_loop(0, rows // tile, row_tile, 0)

    dims = (((1,), (1,)), ((), ()))
    wave_high = wave_high_ref[...]
    wave_low = wave_low_ref[...]
    quarter = LANES // 4
    group = max(2, 2 * LANES // rows)
    for first in range(0, len(chosen), group):
        places = range(first, min(first + group, len(chosen)))
        high = high_ref[first : first + len(places)].reshape(len(places) * rows, 2 * LANES)
        low = low_ref[first : first + len(places)].reshape(len(places) * rows, 2 * LANES)
        total = lax.dot_general(wave_high, high, dims, preferred_element_type=jnp.float32)
        total += lax.dot_general(wave_high, low, dims, preferred_element_type=jnp.float32)
        total += lax.dot_general(wave_low, high, dims, preferred_element_type=jnp.float32)

        def put(place, side, half, part, value):
            k1 = chosen[place]
            if side == 1 and (k1 == 0 or k1 == RADIX // 2):
                return
            index = RADIX - k1 if side else k1
            at = (index % chan_count, half, index // chan_count)
            if not joined:
                at += (part,)
            out_ref[at] = value.astype(jnp.bfloat16)

        for side in range(2):
            for half in range(2):
                row_re = side * LANES + half * quarter
                row_im = row_re + 2 * quarter
                if not joined:
                    for i, place in enumerate(places):
                        columns = slice(i * rows, (i + 1) * rows)
                        put(place, side, half, 0, total[row_re : row_re + quarter, columns])
                        put(place, side, half, 1, total[row_im : row_im + quarter, columns])
                    continue
                for i in range(0, len(places), 2):
                    columns = slice(i * rows, min((i + 2) * rows, len(places) * rows))
                    re = total[row_re : row_re + quarter, columns]
                    im = total[row_im : row_im + quarter, columns]
                    if i + 1 == len(places):
                        put(places[i], side, half, 0, jnp.concatenate([re, im], axis=1))
                        continue
                    low_lanes = lax.broadcasted_iota(jnp.int32, re.shape, 1) < rows
                    put(places[i], side, half, 0, jnp.where(low_lanes, re, pltpu.roll(im, rows, 1)))
                    put(
                        places[i + 1], side, half, 0, jnp.where(low_lanes, pltpu.roll(re, rows, 1), im)
                    )


def transform(samples, joined):
    chan_count, rows, block_len = samples.shape
    fft_len = chan_count * block_len
    count = len(first_index_list())
    cos, sin = turn_tables(fft_len)
    wave = wave_matrix(fft_len)
    wave_high = wave.astype(jnp.bfloat16)
    wave_low = (wave - wave_high.astype(np.float64)).astype(jnp.bfloat16)
    tables = (
        jnp.asarray(cos, jnp.float32),
        jnp.asarray(sin, jnp.float32),
        jnp.asarray(wave_high),
        jnp.asarray(wave_low),
    )
    whole = pl.BlockSpec(memory_space=pltpu.VMEM)
    shape = (chan_count, 2, RADIX // chan_count)
    shape += (LANES // 4, 2 * rows) if joined else (2, LANES // 4, rows)
    return pl.pallas_call(
        functools.partial(transform_kernel, chan_count, joined),
        out_shape=jax.ShapeDtypeStruct(shape, jnp.bfloat16),
        in_specs=[whole] * 5,
        out_specs=whole,
        scratch_shapes=[
            pltpu.VMEM((8, 5, 2, 16, LANES), jnp.float32),
            pltpu.VMEM((count, rows, 2 * LANES), jnp.bfloat16),
            pltpu.VMEM((count, rows, 2 * LANES), jnp.bfloat16),
        ],
        compiler_params=pltpu.CompilerParams(vmem_limit_bytes=VMEM_LIMIT),
        name="transform",
    )(samples, *tables)


EIGHT = 8


def turn_kernel(group_ref, in_ref, out_ref, near_ref, across_ref, wide_ref):
    chan_count, _, per, k2_count, lanes = in_ref.shape
    pitch = per * chan_count + 1

    def spread(step, carry):
        source, e = step // per, step % per
        for k2 in range(0, k2_count, EIGHT):
            value = in_ref[source, 0, e, k2 : k2 + EIGHT, :].astype(jnp.float32)
            row = k2 * pitch + e * chan_count + source
            wide_ref[pl.ds(row, EIGHT, stride=pitch), :] = value
        return carry

    lax.fori_loop(0, chan_count * per, spread, 0, unroll=4)

    def narrow(k2, carry):
        base = pl.multiple_of(k2 * per, per)
        for e in range(per):
            rows = pl.ds(k2 * pitch + e * chan_count, chan_count)
            out_ref[0, base + e] = wide_ref[rows, :].astype(jnp.bfloat16)
        return carry

    lax.fori_loop(0, k2_count, narrow, 0, unroll=2)

    half, group = pl.program_id(0), group_ref[0]

    @pl.when(half == 1 - group % 2)
    def _():
        near_ref[...] = out_ref[0]

    @pl.when(half == 1 - group // 2)
    def _():
        across_ref[...] = out_ref[0]


def turn(channel, group_id):
    chan_count, halves, per, k2_count, lanes = channel.shape
    channels = per * k2_count
    one_half = (channels, chan_count, lanes)
    return pl.pallas_call(
        turn_kernel,
        out_shape=[
            jax.ShapeDtypeStruct((halves,) + one_half, jnp.bfloat16),
            jax.ShapeDtypeStruct(one_half, jnp.bfloat16),
            jax.ShapeDtypeStruct(one_half, jnp.bfloat16),
        ],
        grid_spec=pltpu.PrefetchScalarGridSpec(
            num_scalar_prefetch=1,
            grid=(halves,),
            in_specs=[
                pl.BlockSpec((chan_count, 1, per, k2_count, lanes), lambda u, g: (0, u, 0, 0, 0))
            ],
            out_specs=[
                pl.BlockSpec((1,) + one_half, lambda u, g: (u, 0, 0, 0)),
                pl.BlockSpec(one_half, lambda u, g: (0, 0, 0)),
                pl.BlockSpec(one_half, lambda u, g: (0, 0, 0)),
            ],
            scratch_shapes=[pltpu.VMEM((k2_count * (per * chan_count + 1), lanes), jnp.float32)],
        ),
        compiler_params=pltpu.CompilerParams(vmem_limit_bytes=VMEM_LIMIT),
        name="turn",
    )(group_id, channel)


def left_kernel(*refs):
    chunk_refs, out_ref = refs[:-1], refs[-1]
    _, channels, _, lanes = chunk_refs[0].shape
    sig_count = lanes // 2

    def pair(step, carry):
        rows = []
        for i in range(2):
            values = [ref[0, 2 * step + i].astype(jnp.float32) for ref in chunk_refs]
            rows += values + [pltpu.roll(value, sig_count, 1) for value in values]
        stacked = jnp.concatenate(rows, axis=0)
        out_ref[0, step] = stacked.T[:sig_count].astype(jnp.bfloat16)
        return carry

    lax.fori_loop(0, channels // 2, pair, 0, unroll=32)


def left_operand(chunks):
    halves, channels, chan_count, lanes = chunks[0].shape
    depth = 2 * 2 * len(chunks) * chan_count
    tile = 128
    return pl.pallas_call(
        left_kernel,
        out_shape=jax.ShapeDtypeStruct((halves, channels // 2, lanes // 2, depth), jnp.bfloat16),
        grid=(halves, channels // tile),
        in_specs=[pl.BlockSpec((1, tile, chan_count, lanes), lambda u, i: (u, i, 0, 0))]
        * len(chunks),
        out_specs=pl.BlockSpec((1, tile // 2, lanes // 2, depth), lambda u, i: (u, i, 0, 0)),
        compiler_params=pltpu.CompilerParams(vmem_limit_bytes=VMEM_LIMIT),
        name="left_operand",
    )(*chunks)


def correlate_kernel(chunk_count, spec_count, group_ref, plan_ref, left_ref, *refs):
    del group_ref, plan_ref
    chunk_refs = refs[:chunk_count]
    out_ref, sum_ref = refs[-2:]
    _, channels, chan_count, lanes = (1,) + chunk_refs[0].shape
    sig_count = lanes // 2
    pitch = channels + 1
    sign = jnp.where(
        lax.broadcasted_iota(jnp.int32, (chan_count, lanes), 1) < sig_count, 1.0, -1.0
    ).astype(jnp.float32)

    def pair(step, carry):
        blocks = []
        for i in range(2):
            values = [ref[2 * step + i].astype(jnp.float32) for ref in chunk_refs]
            rows = [value * sign for value in values]
            rows += [pltpu.roll(value, sig_count, 1) for value in values]
            blocks.append(jnp.concatenate(rows, axis=0).astype(jnp.bfloat16))
        zero = jnp.zeros_like(blocks[0])
        weights = jnp.concatenate(
            [
                jnp.concatenate([blocks[0], zero], axis=1),
                jnp.concatenate([zero, blocks[1]], axis=1),
            ],
            axis=0,
        )
        both = jnp.dot(left_ref[0, step], weights, preferred_element_type=jnp.float32)
        for i in range(2):
            q = 2 * step + i
            for a in range(0, sig_count, EIGHT):
                sum_ref[pl.ds(a * pitch + q, EIGHT, stride=pitch), :] = both[
                    a : a + EIGHT, i * lanes : (i + 1) * lanes
                ]
        return carry

    lax.fori_loop(0, channels // 2, pair, 0, unroll=32)

    def finish(a, carry):
        rows = pl.ds(a * pitch, channels)
        out_ref[0, a] = (sum_ref[rows, :] * (1.0 / spec_count)).astype(jnp.bfloat16)
        return carry

    lax.fori_loop(0, sig_count, finish, 0, unroll=16)


def correlate(left, chunks, group_id, plan, distance, spec_count, so_far):
    channels, chan_count, lanes = chunks[0].shape
    sig_count, depth = left.shape[2:]
    rounds = plan.shape[0]
    tile = 128

    def half_of(group):
        return (group[0] > (group[0] ^ distance)).astype(jnp.int32)

    def round_of(group, plan):
        mate = group[0] ^ distance
        found = jnp.int32(0)
        for r in range(1, rounds):
            found = jnp.where(plan[r, group[0]] == mate, r, found)
        return found

    in_specs = [
        pl.BlockSpec((1, tile // 2, sig_count, depth), lambda i, g, p: (half_of(g), i, 0, 0)),
    ] + [pl.BlockSpec((tile, chan_count, lanes), lambda i, g, p: (i, 0, 0))] * len(chunks)
    operands = [left, *chunks]
    aliases = {}
    if so_far is not None:
        in_specs.append(pl.BlockSpec(memory_space=pl.ANY))
        operands.append(so_far)
        aliases = {len(operands) + 1: 0}
    return pl.pallas_call(
        functools.partial(correlate_kernel, len(chunks), spec_count),
        out_shape=jax.ShapeDtypeStruct((rounds, sig_count, channels, lanes), jnp.bfloat16),
        grid_spec=pltpu.PrefetchScalarGridSpec(
            num_scalar_prefetch=2,
            grid=(channels // tile,),
            in_specs=in_specs,
            out_specs=pl.BlockSpec(
                (1, sig_count, tile, lanes), lambda i, g, p: (round_of(g, p), 0, i, 0)
            ),
            scratch_shapes=[pltpu.VMEM((sig_count * (tile + 1), lanes), jnp.float32)],
        ),
        input_output_aliases=aliases,
        compiler_params=pltpu.CompilerParams(vmem_limit_bytes=VMEM_LIMIT),
        cost_estimate=pl.CostEstimate(
            flops=2 * channels * sig_count * depth * lanes,
            bytes_accessed=16 * 1024 * 1024,
            transcendentals=0,
        ),
        name="correlate",
    )(group_id, plan, *operands)


def correlate_plain(mine, theirs):
    left = mine.reshape(*mine.shape[:2], -1)
    right_re = theirs.reshape(left.shape)
    right_im = jnp.stack([-theirs[..., 1], theirs[..., 0]], axis=-1).reshape(left.shape)
    vis_re = jnp.einsum("kas,kbs->akb", left, right_re, preferred_element_type=jnp.float32)
    vis_im = jnp.einsum("kas,kbs->akb", left, right_im, preferred_element_type=jnp.float32)
    return jnp.concatenate([vis_re, vis_im], axis=-1) * (1.0 / mine.shape[2])


def by_channel(half, sig_count, spec_count):
    chan_count, per, parts, k2, rows = half.shape
    turned = half.transpose(3, 1, 0, 4, 2).reshape(k2 * per, spec_count, sig_count, parts)
    return turned.transpose(0, 2, 1, 3)


def local_plain(voltages, plan):
    sig_count, frames, block_len = voltages.shape
    chan_count = lax.axis_size("chan")
    group_count = lax.axis_size("grp")
    spec_count = frames - TAPS + 1
    rows = spec_count * sig_count // chan_count
    chan_id = lax.axis_index("chan").astype(jnp.int32)
    group_id = lax.axis_index("grp")

    filtered = filter_taps(voltages.transpose(1, 0, 2), chan_id, chan_count, 0, spec_count)
    filtered = filtered.reshape(chan_count, rows, block_len)
    frames_here = lax.all_to_all(filtered, "chan", split_axis=0, concat_axis=0, tiled=True)
    spectra = transform(frames_here, False)
    channel = lax.all_to_all(spectra, "chan", split_axis=0, concat_axis=0, tiled=True)

    lower_half, upper_half = channel[:, 0], channel[:, 1]
    group_ids = jnp.arange(group_count)
    partner = jnp.sum(jnp.where(group_ids[None, :] == group_id, plan, 0), axis=1)
    listed = jnp.any(partner[:, None] == group_ids[None, :], axis=0)
    slot_shape = (group_count,) + (1,) * lower_half.ndim
    chosen_half = jnp.where(
        (group_ids > group_id).reshape(slot_shape), upper_half[None], lower_half[None]
    )
    slots = jnp.where(listed.reshape(slot_shape), chosen_half, jnp.zeros_like(chosen_half))
    received = lax.all_to_all(slots, "grp", split_axis=0, concat_axis=0, tiled=True)
    halves = (group_id > partner).astype(jnp.int32)
    results = []
    for round_index in range(plan.shape[0]):
        mine = lax.dynamic_index_in_dim(channel, halves[round_index], 1, keepdims=False)
        theirs = lax.dynamic_index_in_dim(received, partner[round_index], 0, keepdims=False)
        results.append(
            correlate_plain(
                by_channel(mine, sig_count, spec_count), by_channel(theirs, sig_count, spec_count)
            )
        )
    return jnp.stack(results).astype(jnp.bfloat16)


def local_overlapped(voltages, plan):
    _, frames, _ = voltages.shape
    chan_count = lax.axis_size("chan")
    group_count = lax.axis_size("grp")
    spec_count = frames - TAPS + 1
    chan_id = lax.axis_index("chan").astype(jnp.int32)
    group_id = lax.axis_index("grp").astype(jnp.int32).reshape(1)
    frames_first = voltages.transpose(1, 0, 2)

    def over_chan(value):
        return lax.all_to_all(value, "chan", split_axis=0, concat_axis=0, tiled=True)

    def to_mate(value, distance):
        return lax.ppermute(value, "grp", [(g, g ^ distance) for g in range(group_count)])

    turned, near, across, relayed = [], [], [], []
    channels = []
    for first in range(0, spec_count, chan_count):
        filtered = filter_taps(frames_first, chan_id, chan_count, first, chan_count)
        channels.append(over_chan(transform(over_chan(filtered), True)))
    for index, channel in enumerate(channels):
        if index:
            channel, near, across, relayed = lax.optimization_barrier(
                (channel, near, across, relayed)
            )
        halves, for_near, for_across = turn(channel, group_id)
        turned.append(halves)
        near = near + [to_mate(for_near, 1)]
        across = across + [to_mate(for_across, 2)]
        if index + 1 < len(channels):
            relayed = relayed + [to_mate(across[-1], 1)]
    left = left_operand(turned)
    result = correlate(left, near, group_id, plan, 1, spec_count, None)
    across, result = lax.optimization_barrier((across, result))
    relayed = relayed + [to_mate(across[-1], 1)]
    result = correlate(left, across, group_id, plan, 2, spec_count, result)
    return correlate(left, relayed, group_id, plan, 3, spec_count, result)


def local(voltages, plan):
    sig_count, frames, _ = voltages.shape
    chan_count = lax.axis_size("chan")
    group_count = lax.axis_size("grp")
    if (
        group_count == 4
        and plan.shape[0] == group_count - 1
        and chan_count == EIGHT
        and (frames - TAPS + 1) % chan_count == 0
        and 2 * sig_count == LANES
    ):
        return local_overlapped(voltages, plan)
    return local_plain(voltages, plan)


def solution(mesh):
    in_specs = (P("grp", None, "chan"), P())
    out_specs = P(None, "grp", "chan", None)
    return jax.shard_map(local, mesh=mesh, in_specs=in_specs, out_specs=out_specs, check_vma=False)
```

```python
import functools
import math

import jax
import jax.numpy as jnp
import numpy as np
from jax import lax
from jax.experimental import pallas as pl
from jax.experimental.pallas import tpu as pltpu
from jax.sharding import PartitionSpec as P


TAPS = 16
LANES = 128
RADIX = 64
VMEM_LIMIT = 60 * 1024 * 1024


def tap_table(fft_len):
    position = np.arange(TAPS * fft_len, dtype=np.float64)
    total = TAPS * fft_len
    window = 0.5 - 0.5 * np.cos(2.0 * np.pi * position / total)
    return (window * np.sinc((position - 0.5 * total) / fft_len)).reshape(TAPS, fft_len)


def filter_kernel(chan_ref, volt_ref, coeff_ref, out_ref):
    del chan_ref
    frames, sig_tile, block_len = volt_ref.shape
    spec_count = frames - TAPS + 1

    def one_tile(tile, carry):
        cols = pl.ds(pl.multiple_of(tile * LANES, LANES), LANES)
        coeff = [
            jnp.broadcast_to(coeff_ref[0, t : t + 1, cols], (sig_tile, LANES)) for t in range(TAPS)
        ]
        total = [None] * spec_count
        for frame in range(frames):
            sample = volt_ref[frame, :, cols].astype(jnp.float32)
            for s in range(max(0, frame - TAPS + 1), min(spec_count - 1, frame) + 1):
                term = coeff[frame - s] * sample
                total[s] = term if total[s] is None else total[s] + term
            if frame >= TAPS - 1:
                s = frame - TAPS + 1
                out_ref[s, :, cols] = total[s].astype(jnp.bfloat16)
                total[s] = None
        return carry

    lax.fori_loop(0, block_len // LANES, one_tile, 0)


def filter_taps(frames_first, chan_id, chan_count, first, spec_count):
    _, sig_count, block_len = frames_first.shape
    frames = spec_count + TAPS - 1
    table = tap_table(block_len * chan_count).astype(np.float32)
    table = np.ascontiguousarray(table.reshape(TAPS, chan_count, block_len).transpose(1, 0, 2))
    sig_tile = 16
    return pl.pallas_call(
        filter_kernel,
        out_shape=jax.ShapeDtypeStruct((spec_count, sig_count, block_len), jnp.bfloat16),
        grid_spec=pltpu.PrefetchScalarGridSpec(
            num_scalar_prefetch=1,
            grid=(sig_count // sig_tile,),
            in_specs=[
                pl.BlockSpec(
                    (pl.Element(frames), pl.Element(sig_tile), pl.Element(block_len)),
                    lambda i, c: (first, i * sig_tile, 0),
                ),
                pl.BlockSpec((1, TAPS, block_len), lambda i, c: (c[0], 0, 0)),
            ],
            out_specs=pl.BlockSpec((spec_count, sig_tile, block_len), lambda i, c: (0, i, 0)),
        ),
        compiler_params=pltpu.CompilerParams(vmem_limit_bytes=VMEM_LIMIT),
        name="filter_taps",
    )(chan_id, frames_first, jnp.asarray(table))


def filter_by_shift_kernel(chan_ref, volt_ref, coeff_ref, *refs):
    out_refs, block_ref = refs[:-1], refs[-1]
    filter_kernel(chan_ref, volt_ref, coeff_ref, block_ref)
    count = len(out_refs)
    for shift, out_ref in enumerate(out_refs):
        out_ref[...] = block_ref[lax.rem(chan_ref[0] + shift, count)]


def filter_by_shift(frames_first, chan_id, chan_count, first):
    _, sig_count, block_len = frames_first.shape
    frames = chan_count + TAPS - 1
    table = tap_table(block_len * chan_count).astype(np.float32)
    table = np.ascontiguousarray(table.reshape(TAPS, chan_count, block_len).transpose(1, 0, 2))
    sig_tile = 16
    return pl.pallas_call(
        filter_by_shift_kernel,
        out_shape=[jax.ShapeDtypeStruct((sig_count, block_len), jnp.bfloat16)] * chan_count,
        grid_spec=pltpu.PrefetchScalarGridSpec(
            num_scalar_prefetch=1,
            grid=(sig_count // sig_tile,),
            in_specs=[
                pl.BlockSpec(
                    (pl.Element(frames), pl.Element(sig_tile), pl.Element(block_len)),
                    lambda i, c: (first, i * sig_tile, 0),
                ),
                pl.BlockSpec((1, TAPS, block_len), lambda i, c: (c[0], 0, 0)),
            ],
            out_specs=[pl.BlockSpec((sig_tile, block_len), lambda i, c: (i, 0))] * chan_count,
            scratch_shapes=[pltpu.VMEM((chan_count, sig_tile, block_len), jnp.bfloat16)],
        ),
        compiler_params=pltpu.CompilerParams(vmem_limit_bytes=VMEM_LIMIT),
        name="filter_by_shift",
    )(chan_id, frames_first, jnp.asarray(table))


def cadd(a, b):
    if a is None:
        return b
    if b is None:
        return a
    return a + b


def csub(a, b):
    if b is None:
        return a
    if a is None:
        return -b
    return a - b


def scale_by(value, re, im):
    vr, vi = value
    eps = 1e-12

    def mul(x, f):
        if x is None or abs(f) < eps:
            return None
        if abs(f - 1.0) < eps:
            return x
        if abs(f + 1.0) < eps:
            return -x
        return x * f

    return csub(mul(vr, re), mul(vi, im)), cadd(mul(vr, im), mul(vi, re))


def plus(a, b):
    return cadd(a[0], b[0]), cadd(a[1], b[1])


def minus(a, b):
    return csub(a[0], b[0]), csub(a[1], b[1])


def dft(values, wanted=None):
    n = len(values)
    if n == 1:
        return list(values)
    even = dft(values[0::2])
    odd = dft(values[1::2])
    out = [None] * n
    for k in range(n // 2):
        if wanted is not None and k not in wanted and k + n // 2 not in wanted:
            continue
        angle = -2.0 * math.pi * k / n
        turned = scale_by(odd[k], math.cos(angle), math.sin(angle))
        out[k] = plus(even[k], turned)
        out[k + n // 2] = minus(even[k], turned)
    return out


def first_index_list():
    chosen = []
    for c in range(5):
        for e in range(8):
            k1 = c + 8 * e
            if c in (0, 4) and k1 > RADIX // 2:
                continue
            chosen.append(k1)
    return chosen


def turn_tables(fft_len):
    k1 = np.array(first_index_list())[:, None]
    angle = 2.0 * np.pi * ((k1 * np.arange(LANES)[None, :]) % fft_len) / fft_len
    return np.cos(angle), np.sin(angle)


def wave_matrix(fft_len):
    gain = 1.0 / (64.0 * math.sqrt(fft_len))
    half = LANES // 2
    n2 = np.arange(LANES)[None, :]
    k2 = np.arange(half)[:, None]
    rows = []
    for index, flip in ((k2, 1.0), (LANES - 1 - k2, -1.0)):
        angle = 2.0 * np.pi * ((index * n2) % LANES) / LANES
        cos, sin = np.cos(angle) * gain, np.sin(angle) * gain
        rows.append(np.concatenate([cos, sin], axis=1))
        rows.append(np.concatenate([-sin, cos], axis=1) * flip)
    return np.concatenate(rows, axis=0)


def split_two(value):
    high = value.astype(jnp.bfloat16)
    return high, (value - high.astype(jnp.float32)).astype(jnp.bfloat16)


def transform_kernel(
    chan_count, joined, in_ref, cos_ref, sin_ref, wave_high_ref, wave_low_ref, out_ref, mid_ref, high_ref, low_ref
):
    _, rows, block_len = in_ref.shape
    per_block = block_len // LANES
    tile = 16
    chosen = first_index_list()

    def row_tile(step, carry):
        at = pl.ds(pl.multiple_of(step * tile, tile), tile)
        present = set()
        for low_n in range(8):
            column = []
            for high_n in range(8):
                n1 = high_n * 8 + low_n
                lanes = slice((n1 % per_block) * LANES, (n1 % per_block + 1) * LANES)
                column.append((in_ref[n1 // per_block, at, lanes].astype(jnp.float32), None))
            spread = dft(column, wanted=range(5))
            for c in range(5):
                angle = -2.0 * math.pi * low_n * c / RADIX
                re, im = scale_by(spread[c], math.cos(angle), math.sin(angle))
                for part, value in enumerate((re, im)):
                    if value is not None:
                        mid_ref[low_n, c, part] = value
                        present.add((low_n, c, part))
        for c in range(5):
            wanted = [e for e in range(8) if c + 8 * e in chosen]
            values = []
            for low_n in range(8):
                values.append(
                    tuple(
                        mid_ref[low_n, c, part] if (low_n, c, part) in present else None
                        for part in range(2)
                    )
                )
            spread = dft(values, wanted=wanted)
            for e in wanted:
                place = chosen.index(c + 8 * e)
                cos = cos_ref[place : place + 1, :]
                sin = sin_ref[place : place + 1, :]
                re, im = spread[e]
                if im is None:
                    turned_re, turned_im = re * cos, -(re * sin)
                else:
                    turned_re, turned_im = re * cos + im * sin, im * cos - re * sin
                a, b = split_two(turned_re)
                high_ref[place, at, :LANES] = a
                low_ref[place, at, :LANES] = b
                a, b = split_two(turned_im)
                high_ref[place, at, LANES:] = a
                low_ref[place, at, LANES:] = b
        return carry

    lax.fori_loop(0, rows // tile, row_tile, 0)

    dims = (((1,), (1,)), ((), ()))
    wave_high = wave_high_ref[...]
    wave_low = wave_low_ref[...]
    quarter = LANES // 4
    group = max(2, 2 * LANES // rows)
    for first in range(0, len(chosen), group):
        places = range(first, min(first + group, len(chosen)))
        high = high_ref[first : first + len(places)].reshape(len(places) * rows, 2 * LANES)
        low = low_ref[first : first + len(places)].reshape(len(places) * rows, 2 * LANES)
        total = lax.dot_general(wave_high, high, dims, preferred_element_type=jnp.float32)
        total += lax.dot_general(wave_high, low, dims, preferred_element_type=jnp.float32)
        total += lax.dot_general(wave_low, high, dims, preferred_element_type=jnp.float32)

        def put(place, side, half, part, value):
            k1 = chosen[place]
            if side == 1 and (k1 == 0 or k1 == RADIX // 2):
                return
            index = RADIX - k1 if side else k1
            at = (index % chan_count, half, index // chan_count)
            if not joined:
                at += (part,)
            out_ref[at] = value.astype(jnp.bfloat16)

        for side in range(2):
            for half in range(2):
                row_re = side * LANES + half * quarter
                row_im = row_re + 2 * quarter
                if not joined:
                    for i, place in enumerate(places):
                        columns = slice(i * rows, (i + 1) * rows)
                        put(place, side, half, 0, total[row_re : row_re + quarter, columns])
                        put(place, side, half, 1, total[row_im : row_im + quarter, columns])
                    continue
                for i in range(0, len(places), 2):
                    columns = slice(i * rows, min((i + 2) * rows, len(places) * rows))
                    re = total[row_re : row_re + quarter, columns]
                    im = total[row_im : row_im + quarter, columns]
                    if i + 1 == len(places):
                        put(places[i], side, half, 0, jnp.concatenate([re, im], axis=1))
                        continue
                    low_lanes = lax.broadcasted_iota(jnp.int32, re.shape, 1) < rows
                    put(places[i], side, half, 0, jnp.where(low_lanes, re, pltpu.roll(im, rows, 1)))
                    put(
                        places[i + 1], side, half, 0, jnp.where(low_lanes, pltpu.roll(re, rows, 1), im)
                    )


def transform_tables(fft_len):
    cos, sin = turn_tables(fft_len)
    wave = wave_matrix(fft_len)
    wave_high = wave.astype(jnp.bfloat16)
    wave_low = (wave - wave_high.astype(np.float64)).astype(jnp.bfloat16)
    return (
        jnp.asarray(cos, jnp.float32),
        jnp.asarray(sin, jnp.float32),
        jnp.asarray(wave_high),
        jnp.asarray(wave_low),
    )


def transform_scratch(rows):
    count = len(first_index_list())
    return [
        pltpu.VMEM((8, 5, 2, 16, LANES), jnp.float32),
        pltpu.VMEM((count, rows, 2 * LANES), jnp.bfloat16),
        pltpu.VMEM((count, rows, 2 * LANES), jnp.bfloat16),
    ]


def transform(samples):
    chan_count, rows, block_len = samples.shape
    whole = pl.BlockSpec(memory_space=pltpu.VMEM)
    shape = (chan_count, 2, RADIX // chan_count, 2, LANES // 4, rows)
    return pl.pallas_call(
        functools.partial(transform_kernel, chan_count, False),
        out_shape=jax.ShapeDtypeStruct(shape, jnp.bfloat16),
        in_specs=[whole] * 5,
        out_specs=whole,
        scratch_shapes=transform_scratch(rows),
        compiler_params=pltpu.CompilerParams(vmem_limit_bytes=VMEM_LIMIT),
        name="transform",
    )(samples, *transform_tables(chan_count * block_len))


def transform_by_shift_kernel(chan_count, *refs):
    chan_ref, tables = refs[0], refs[1:5]
    in_refs, out_refs = refs[5 : 5 + chan_count], refs[5 + chan_count : 5 + 2 * chan_count]
    block_ref, result_ref, mid_ref, high_ref, low_ref, in_sem, out_sem = refs[5 + 2 * chan_count :]
    chan = chan_ref[0]
    fetches = []
    for shift, in_ref in enumerate(in_refs):
        source = lax.rem(chan + chan_count - shift, chan_count)
        fetches.append(pltpu.make_async_copy(in_ref, block_ref.at[source], in_sem.at[shift]))
        fetches[-1].start()
    for fetch in fetches:
        fetch.wait()
    transform_kernel(
        chan_count, True, block_ref, *tables, result_ref, mid_ref, high_ref, low_ref
    )
    sends = []
    for shift, out_ref in enumerate(out_refs):
        target = lax.rem(chan + shift, chan_count)
        sends.append(pltpu.make_async_copy(result_ref.at[target], out_ref, out_sem.at[shift]))
        sends[-1].start()
    for send in sends:
        send.wait()


def transform_by_shift(blocks, chan_id):
    chan_count = len(blocks)
    rows, block_len = blocks[0].shape
    whole = pl.BlockSpec(memory_space=pltpu.VMEM)
    apart = pl.BlockSpec(memory_space=pltpu.HBM)
    shape = (2, RADIX // chan_count, LANES // 4, 2 * rows)
    return pl.pallas_call(
        functools.partial(transform_by_shift_kernel, chan_count),
        out_shape=[jax.ShapeDtypeStruct(shape, jnp.bfloat16)] * chan_count,
        in_specs=[pl.BlockSpec(memory_space=pltpu.SMEM)] + [whole] * 4 + [apart] * chan_count,
        out_specs=[apart] * chan_count,
        scratch_shapes=[
            pltpu.VMEM((chan_count, rows, block_len), jnp.bfloat16),
            pltpu.VMEM((chan_count,) + shape, jnp.bfloat16),
        ]
        + transform_scratch(rows)
        + [pltpu.SemaphoreType.DMA((chan_count,)), pltpu.SemaphoreType.DMA((chan_count,))],
        compiler_params=pltpu.CompilerParams(vmem_limit_bytes=VMEM_LIMIT),
        name="transform_by_shift",
    )(chan_id, *transform_tables(chan_count * block_len), *blocks)


EIGHT = 8


def turn_kernel(group_ref, *refs):
    in_refs, (out_ref, near_ref, across_ref, wide_ref) = refs[:-4], refs[-4:]
    chan_count = len(in_refs)
    _, per, k2_count, _ = in_refs[0].shape
    pitch = per * chan_count + 1

    def spread(e, carry):
        for source, in_ref in enumerate(in_refs):
            for k2 in range(0, k2_count, EIGHT):
                value = in_ref[0, e, k2 : k2 + EIGHT, :].astype(jnp.float32)
                row = k2 * pitch + e * chan_count + source
                wide_ref[pl.ds(row, EIGHT, stride=pitch), :] = value
        return carry

    lax.fori_loop(0, per, spread, 0)

    def narrow(k2, carry):
        base = pl.multiple_of(k2 * per, per)
        for e in range(per):
            rows = pl.ds(k2 * pitch + e * chan_count, chan_count)
            out_ref[0, base + e] = wide_ref[rows, :].astype(jnp.bfloat16)
        return carry

    lax.fori_loop(0, k2_count, narrow, 0, unroll=2)

    half, group = pl.program_id(0), group_ref[0]

    @pl.when(half == 1 - group % 2)
    def _():
        near_ref[...] = out_ref[0]

    @pl.when(half == 1 - group // 2)
    def _():
        across_ref[...] = out_ref[0]


def turn(blocks, group_id):
    chan_count = len(blocks)
    halves, per, k2_count, lanes = blocks[0].shape
    one_half = (per * k2_count, chan_count, lanes)
    return pl.pallas_call(
        turn_kernel,
        out_shape=[
            jax.ShapeDtypeStruct((halves,) + one_half, jnp.bfloat16),
            jax.ShapeDtypeStruct(one_half, jnp.bfloat16),
            jax.ShapeDtypeStruct(one_half, jnp.bfloat16),
        ],
        grid_spec=pltpu.PrefetchScalarGridSpec(
            num_scalar_prefetch=1,
            grid=(halves,),
            in_specs=[pl.BlockSpec((1, per, k2_count, lanes), lambda u, g: (u, 0, 0, 0))]
            * chan_count,
            out_specs=[
                pl.BlockSpec((1,) + one_half, lambda u, g: (u, 0, 0, 0)),
                pl.BlockSpec(one_half, lambda u, g: (0, 0, 0)),
                pl.BlockSpec(one_half, lambda u, g: (0, 0, 0)),
            ],
            scratch_shapes=[pltpu.VMEM((k2_count * (per * chan_count + 1), lanes), jnp.float32)],
        ),
        compiler_params=pltpu.CompilerParams(vmem_limit_bytes=VMEM_LIMIT),
        name="turn",
    )(group_id, *blocks)


def left_kernel(*refs):
    chunk_refs, out_ref = refs[:-1], refs[-1]
    _, channels, _, lanes = chunk_refs[0].shape
    sig_count = lanes // 2

    def pair(step, carry):
        rows = []
        for i in range(2):
            values = [ref[0, 2 * step + i].astype(jnp.float32) for ref in chunk_refs]
            rows += values + [pltpu.roll(value, sig_count, 1) for value in values]
        stacked = jnp.concatenate(rows, axis=0)
        out_ref[0, step] = stacked.T[:sig_count].astype(jnp.bfloat16)
        return carry

    lax.fori_loop(0, channels // 2, pair, 0, unroll=32)


def left_operand(chunks):
    halves, channels, chan_count, lanes = chunks[0].shape
    depth = 2 * 2 * len(chunks) * chan_count
    tile = 128
    return pl.pallas_call(
        left_kernel,
        out_shape=jax.ShapeDtypeStruct((halves, channels // 2, lanes // 2, depth), jnp.bfloat16),
        grid=(halves, channels // tile),
        in_specs=[pl.BlockSpec((1, tile, chan_count, lanes), lambda u, i: (u, i, 0, 0))]
        * len(chunks),
        out_specs=pl.BlockSpec((1, tile // 2, lanes // 2, depth), lambda u, i: (u, i, 0, 0)),
        compiler_params=pltpu.CompilerParams(vmem_limit_bytes=VMEM_LIMIT),
        name="left_operand",
    )(*chunks)


def correlate_kernel(chunk_count, spec_count, group_ref, plan_ref, left_ref, *refs):
    del group_ref, plan_ref
    chunk_refs = refs[:chunk_count]
    out_ref, sum_ref = refs[-2:]
    _, channels, chan_count, lanes = (1,) + chunk_refs[0].shape
    sig_count = lanes // 2
    pitch = channels + 1
    sign = jnp.where(
        lax.broadcasted_iota(jnp.int32, (chan_count, lanes), 1) < sig_count, 1.0, -1.0
    ).astype(jnp.float32)

    def pair(step, carry):
        blocks = []
        for i in range(2):
            values = [ref[2 * step + i].astype(jnp.float32) for ref in chunk_refs]
            rows = [value * sign for value in values]
            rows += [pltpu.roll(value, sig_count, 1) for value in values]
            blocks.append(jnp.concatenate(rows, axis=0).astype(jnp.bfloat16))
        zero = jnp.zeros_like(blocks[0])
        weights = jnp.concatenate(
            [
                jnp.concatenate([blocks[0], zero], axis=1),
                jnp.concatenate([zero, blocks[1]], axis=1),
            ],
            axis=0,
        )
        both = jnp.dot(left_ref[0, step], weights, preferred_element_type=jnp.float32)
        for i in range(2):
            q = 2 * step + i
            for a in range(0, sig_count, EIGHT):
                sum_ref[pl.ds(a * pitch + q, EIGHT, stride=pitch), :] = both[
                    a : a + EIGHT, i * lanes : (i + 1) * lanes
                ]
        return carry

    lax.fori_loop(0, channels // 2, pair, 0, unroll=32)

    def finish(a, carry):
        rows = pl.ds(a * pitch, channels)
        out_ref[0, a] = (sum_ref[rows, :] * (1.0 / spec_count)).astype(jnp.bfloat16)
        return carry

    lax.fori_loop(0, sig_count, finish, 0, unroll=16)


def correlate(left, chunks, group_id, plan, distance, spec_count, so_far):
    channels, chan_count, lanes = chunks[0].shape
    sig_count, depth = left.shape[2:]
    rounds = plan.shape[0]
    tile = 128

    def half_of(group):
        return (group[0] > (group[0] ^ distance)).astype(jnp.int32)

    def round_of(group, plan):
        mate = group[0] ^ distance
        found = jnp.int32(0)
        for r in range(1, rounds):
            found = jnp.where(plan[r, group[0]] == mate, r, found)
        return found

    in_specs = [
        pl.BlockSpec((1, tile // 2, sig_count, depth), lambda i, g, p: (half_of(g), i, 0, 0)),
    ] + [pl.BlockSpec((tile, chan_count, lanes), lambda i, g, p: (i, 0, 0))] * len(chunks)
    operands = [left, *chunks]
    aliases = {}
    if so_far is not None:
        in_specs.append(pl.BlockSpec(memory_space=pl.ANY))
        operands.append(so_far)
        aliases = {len(operands) + 1: 0}
    return pl.pallas_call(
        functools.partial(correlate_kernel, len(chunks), spec_count),
        out_shape=jax.ShapeDtypeStruct((rounds, sig_count, channels, lanes), jnp.bfloat16),
        grid_spec=pltpu.PrefetchScalarGridSpec(
            num_scalar_prefetch=2,
            grid=(channels // tile,),
            in_specs=in_specs,
            out_specs=pl.BlockSpec(
                (1, sig_count, tile, lanes), lambda i, g, p: (round_of(g, p), 0, i, 0)
            ),
            scratch_shapes=[pltpu.VMEM((sig_count * (tile + 1), lanes), jnp.float32)],
        ),
        input_output_aliases=aliases,
        compiler_params=pltpu.CompilerParams(vmem_limit_bytes=VMEM_LIMIT),
        cost_estimate=pl.CostEstimate(
            flops=2 * channels * sig_count * depth * lanes,
            bytes_accessed=16 * 1024 * 1024,
            transcendentals=0,
        ),
        name="correlate",
    )(group_id, plan, *operands)


def correlate_plain(mine, theirs):
    left = mine.reshape(*mine.shape[:2], -1)
    right_re = theirs.reshape(left.shape)
    right_im = jnp.stack([-theirs[..., 1], theirs[..., 0]], axis=-1).reshape(left.shape)
    vis_re = jnp.einsum("kas,kbs->akb", left, right_re, preferred_element_type=jnp.float32)
    vis_im = jnp.einsum("kas,kbs->akb", left, right_im, preferred_element_type=jnp.float32)
    return jnp.concatenate([vis_re, vis_im], axis=-1) * (1.0 / mine.shape[2])


def by_channel(half, sig_count, spec_count):
    _, per, parts, k2, _ = half.shape
    turned = half.transpose(3, 1, 0, 4, 2).reshape(k2 * per, spec_count, sig_count, parts)
    return turned.transpose(0, 2, 1, 3)


def local_plain(voltages, plan):
    sig_count, frames, block_len = voltages.shape
    chan_count = lax.axis_size("chan")
    group_count = lax.axis_size("grp")
    spec_count = frames - TAPS + 1
    rows = spec_count * sig_count // chan_count
    chan_id = lax.axis_index("chan").astype(jnp.int32)
    group_id = lax.axis_index("grp")

    frames_first = voltages.transpose(1, 0, 2)
    filtered = filter_taps(frames_first, chan_id.reshape(1), chan_count, 0, spec_count)
    filtered = filtered.reshape(chan_count, rows, block_len)
    frames_here = lax.all_to_all(filtered, "chan", split_axis=0, concat_axis=0, tiled=True)
    spectra = transform(frames_here)
    channel = lax.all_to_all(spectra, "chan", split_axis=0, concat_axis=0, tiled=True)

    lower_half, upper_half = channel[:, 0], channel[:, 1]
    group_ids = jnp.arange(group_count)
    partner = jnp.sum(jnp.where(group_ids[None, :] == group_id, plan, 0), axis=1)
    listed = jnp.any(partner[:, None] == group_ids[None, :], axis=0)
    slot_shape = (group_count,) + (1,) * lower_half.ndim
    chosen_half = jnp.where(
        (group_ids > group_id).reshape(slot_shape), upper_half[None], lower_half[None]
    )
    slots = jnp.where(listed.reshape(slot_shape), chosen_half, jnp.zeros_like(chosen_half))
    received = lax.all_to_all(slots, "grp", split_axis=0, concat_axis=0, tiled=True)
    halves = (group_id > partner).astype(jnp.int32)
    results = []
    for round_index in range(plan.shape[0]):
        mine = lax.dynamic_index_in_dim(channel, halves[round_index], 1, keepdims=False)
        theirs = lax.dynamic_index_in_dim(received, partner[round_index], 0, keepdims=False)
        results.append(
            correlate_plain(
                by_channel(mine, sig_count, spec_count), by_channel(theirs, sig_count, spec_count)
            )
        )
    return jnp.stack(results).astype(jnp.bfloat16)


def local_overlapped(voltages, plan):
    _, frames, _ = voltages.shape
    chan_count = lax.axis_size("chan")
    group_count = lax.axis_size("grp")
    spec_count = frames - TAPS + 1
    chan_id = lax.axis_index("chan").astype(jnp.int32).reshape(1)
    group_id = lax.axis_index("grp").astype(jnp.int32).reshape(1)
    frames_first = voltages.transpose(1, 0, 2)

    def over_chan(blocks):
        moved = [blocks[0]]
        for shift in range(1, chan_count):
            pairs = [(c, (c + shift) % chan_count) for c in range(chan_count)]
            moved.append(lax.ppermute(blocks[shift], "chan", pairs))
        return moved

    def to_mate(value, distance):
        return lax.ppermute(value, "grp", [(g, g ^ distance) for g in range(group_count)])

    turned, near, across, relayed = [], [], [], []
    channels = []
    chunks = spec_count // chan_count
    for chunk in range(chunks):
        blocks = filter_by_shift(frames_first, chan_id, chan_count, chunk * chan_count)
        blocks = over_chan(blocks)
        blocks = transform_by_shift(blocks, chan_id)
        channels.append(over_chan(blocks))
    for chunk, channel in enumerate(channels):
        if chunk:
            channel, near, across, relayed = lax.optimization_barrier(
                (channel, near, across, relayed)
            )
        halves, for_near, for_across = turn(channel, group_id)
        turned.append(halves)
        near = near + [to_mate(for_near, 1)]
        across = across + [to_mate(for_across, 2)]
        if chunk + 1 < chunks:
            relayed = relayed + [to_mate(across[-1], 1)]
    left = left_operand(turned)
    result = correlate(left, near, group_id, plan, 1, spec_count, None)
    across, result = lax.optimization_barrier((across, result))
    relayed = relayed + [to_mate(across[-1], 1)]
    result = correlate(left, across, group_id, plan, 2, spec_count, result)
    return correlate(left, relayed, group_id, plan, 3, spec_count, result)


def overlaps(group_count, chan_count):
    return group_count == 4 and chan_count == EIGHT


def local(voltages, plan):
    sig_count, frames, _ = voltages.shape
    chan_count = lax.axis_size("chan")
    group_count = lax.axis_size("grp")
    if (
        overlaps(group_count, chan_count)
        and plan.shape[0] == group_count - 1
        and frames - TAPS + 1 == 2 * chan_count
        and 2 * sig_count == LANES
    ):
        return local_overlapped(voltages, plan)
    return local_plain(voltages, plan)


def solution(mesh):
    in_specs = (P("grp", None, "chan"), P())
    out_specs = P(None, "grp", "chan", None)
    return jax.shard_map(local, mesh=mesh, in_specs=in_specs, out_specs=out_specs, check_vma=False)
```

```python
import functools
import math

import jax
import jax.numpy as jnp
import numpy as np
from jax import lax
from jax.experimental import pallas as pl
from jax.experimental.pallas import tpu as pltpu
from jax.sharding import PartitionSpec as P


TAPS = 16
LANES = 128
RADIX = 64
VMEM_LIMIT = 60 * 1024 * 1024


def tap_table(fft_len):
    position = np.arange(TAPS * fft_len, dtype=np.float64)
    total = TAPS * fft_len
    window = 0.5 - 0.5 * np.cos(2.0 * np.pi * position / total)
    return (window * np.sinc((position - 0.5 * total) / fft_len)).reshape(TAPS, fft_len)


def filter_kernel(chan_ref, volt_ref, coeff_ref, out_ref):
    del chan_ref
    frames, sig_tile, block_len = volt_ref.shape
    spec_count = frames - TAPS + 1

    def one_tile(tile, carry):
        cols = pl.ds(pl.multiple_of(tile * LANES, LANES), LANES)
        coeff = [
            jnp.broadcast_to(coeff_ref[0, t : t + 1, cols], (sig_tile, LANES)) for t in range(TAPS)
        ]
        total = [None] * spec_count
        for frame in range(frames):
            sample = volt_ref[frame, :, cols].astype(jnp.float32)
            for s in range(max(0, frame - TAPS + 1), min(spec_count - 1, frame) + 1):
                term = coeff[frame - s] * sample
                total[s] = term if total[s] is None else total[s] + term
            if frame >= TAPS - 1:
                s = frame - TAPS + 1
                out_ref[s, :, cols] = total[s].astype(jnp.bfloat16)
                total[s] = None
        return carry

    lax.fori_loop(0, block_len // LANES, one_tile, 0)


def filter_taps(frames_first, chan_id, chan_count, first, spec_count):
    _, sig_count, block_len = frames_first.shape
    frames = spec_count + TAPS - 1
    table = tap_table(block_len * chan_count).astype(np.float32)
    table = np.ascontiguousarray(table.reshape(TAPS, chan_count, block_len).transpose(1, 0, 2))
    sig_tile = 16
    return pl.pallas_call(
        filter_kernel,
        out_shape=jax.ShapeDtypeStruct((spec_count, sig_count, block_len), jnp.bfloat16),
        grid_spec=pltpu.PrefetchScalarGridSpec(
            num_scalar_prefetch=1,
            grid=(sig_count // sig_tile,),
            in_specs=[
                pl.BlockSpec(
                    (pl.Element(frames), pl.Element(sig_tile), pl.Element(block_len)),
                    lambda i, c: (first, i * sig_tile, 0),
                ),
                pl.BlockSpec((1, TAPS, block_len), lambda i, c: (c[0], 0, 0)),
            ],
            out_specs=pl.BlockSpec((spec_count, sig_tile, block_len), lambda i, c: (0, i, 0)),
        ),
        compiler_params=pltpu.CompilerParams(vmem_limit_bytes=VMEM_LIMIT),
        name="filter_taps",
    )(chan_id, frames_first, jnp.asarray(table))


def filter_by_shift_kernel(chan_ref, volt_ref, coeff_ref, *refs):
    out_refs, block_ref = refs[:-1], refs[-1]
    filter_kernel(chan_ref, volt_ref, coeff_ref, block_ref)
    count = len(out_refs)
    for shift, out_ref in enumerate(out_refs):
        out_ref[...] = block_ref[lax.rem(chan_ref[0] + shift, count)]


def filter_by_shift(frames_first, chan_id, chan_count, first):
    _, sig_count, block_len = frames_first.shape
    frames = chan_count + TAPS - 1
    table = tap_table(block_len * chan_count).astype(np.float32)
    table = np.ascontiguousarray(table.reshape(TAPS, chan_count, block_len).transpose(1, 0, 2))
    sig_tile = 16
    return pl.pallas_call(
        filter_by_shift_kernel,
        out_shape=[jax.ShapeDtypeStruct((sig_count, block_len), jnp.bfloat16)] * chan_count,
        grid_spec=pltpu.PrefetchScalarGridSpec(
            num_scalar_prefetch=1,
            grid=(sig_count // sig_tile,),
            in_specs=[
                pl.BlockSpec(
                    (pl.Element(frames), pl.Element(sig_tile), pl.Element(block_len)),
                    lambda i, c: (first, i * sig_tile, 0),
                ),
                pl.BlockSpec((1, TAPS, block_len), lambda i, c: (c[0], 0, 0)),
            ],
            out_specs=[pl.BlockSpec((sig_tile, block_len), lambda i, c: (i, 0))] * chan_count,
            scratch_shapes=[pltpu.VMEM((chan_count, sig_tile, block_len), jnp.bfloat16)],
        ),
        compiler_params=pltpu.CompilerParams(vmem_limit_bytes=VMEM_LIMIT),
        name="filter_by_shift",
    )(chan_id, frames_first, jnp.asarray(table))


def cadd(a, b):
    if a is None:
        return b
    if b is None:
        return a
    return a + b


def csub(a, b):
    if b is None:
        return a
    if a is None:
        return -b
    return a - b


def scale_by(value, re, im):
    vr, vi = value
    eps = 1e-12

    def mul(x, f):
        if x is None or abs(f) < eps:
            return None
        if abs(f - 1.0) < eps:
            return x
        if abs(f + 1.0) < eps:
            return -x
        return x * f

    return csub(mul(vr, re), mul(vi, im)), cadd(mul(vr, im), mul(vi, re))


def plus(a, b):
    return cadd(a[0], b[0]), cadd(a[1], b[1])


def minus(a, b):
    return csub(a[0], b[0]), csub(a[1], b[1])


def dft(values, wanted=None):
    n = len(values)
    if n == 1:
        return list(values)
    even = dft(values[0::2])
    odd = dft(values[1::2])
    out = [None] * n
    for k in range(n // 2):
        if wanted is not None and k not in wanted and k + n // 2 not in wanted:
            continue
        angle = -2.0 * math.pi * k / n
        turned = scale_by(odd[k], math.cos(angle), math.sin(angle))
        out[k] = plus(even[k], turned)
        out[k + n // 2] = minus(even[k], turned)
    return out


def first_index_list():
    chosen = []
    for c in range(5):
        for e in range(8):
            k1 = c + 8 * e
            if c in (0, 4) and k1 > RADIX // 2:
                continue
            chosen.append(k1)
    return chosen


def turn_tables(fft_len):
    k1 = np.array(first_index_list())[:, None]
    angle = 2.0 * np.pi * ((k1 * np.arange(LANES)[None, :]) % fft_len) / fft_len
    return np.cos(angle), np.sin(angle)


def wave_matrix(fft_len):
    gain = 1.0 / (64.0 * math.sqrt(fft_len))
    half = LANES // 2
    n2 = np.arange(LANES)[None, :]
    k2 = np.arange(half)[:, None]
    rows = []
    for index, flip in ((k2, 1.0), (LANES - 1 - k2, -1.0)):
        angle = 2.0 * np.pi * ((index * n2) % LANES) / LANES
        cos, sin = np.cos(angle) * gain, np.sin(angle) * gain
        rows.append(np.concatenate([cos, sin], axis=1))
        rows.append(np.concatenate([-sin, cos], axis=1) * flip)
    return np.concatenate(rows, axis=0)


def split_two(value):
    high = value.astype(jnp.bfloat16)
    return high, (value - high.astype(jnp.float32)).astype(jnp.bfloat16)


def transform_kernel(
    chan_count, joined, in_ref, cos_ref, sin_ref, wave_high_ref, wave_low_ref, out_ref, mid_ref, high_ref, low_ref
):
    _, rows, block_len = in_ref.shape
    per_block = block_len // LANES
    tile = 16
    chosen = first_index_list()

    def row_tile(step, carry):
        at = pl.ds(pl.multiple_of(step * tile, tile), tile)
        present = set()
        for low_n in range(8):
            column = []
            for high_n in range(8):
                n1 = high_n * 8 + low_n
                lanes = slice((n1 % per_block) * LANES, (n1 % per_block + 1) * LANES)
                column.append((in_ref[n1 // per_block, at, lanes].astype(jnp.float32), None))
            spread = dft(column, wanted=range(5))
            for c in range(5):
                angle = -2.0 * math.pi * low_n * c / RADIX
                re, im = scale_by(spread[c], math.cos(angle), math.sin(angle))
                for part, value in enumerate((re, im)):
                    if value is not None:
                        mid_ref[low_n, c, part] = value
                        present.add((low_n, c, part))
        for c in range(5):
            wanted = [e for e in range(8) if c + 8 * e in chosen]
            values = []
            for low_n in range(8):
                values.append(
                    tuple(
                        mid_ref[low_n, c, part] if (low_n, c, part) in present else None
                        for part in range(2)
                    )
                )
            spread = dft(values, wanted=wanted)
            for e in wanted:
                place = chosen.index(c + 8 * e)
                cos = cos_ref[place : place + 1, :]
                sin = sin_ref[place : place + 1, :]
                re, im = spread[e]
                if im is None:
                    turned_re, turned_im = re * cos, -(re * sin)
                else:
                    turned_re, turned_im = re * cos + im * sin, im * cos - re * sin
                a, b = split_two(turned_re)
                high_ref[place, at, :LANES] = a
                low_ref[place, at, :LANES] = b
                a, b = split_two(turned_im)
                high_ref[place, at, LANES:] = a
                low_ref[place, at, LANES:] = b
        return carry

    lax.fori_loop(0, rows // tile, row_tile, 0)

    dims = (((1,), (1,)), ((), ()))
    wave_high = wave_high_ref[...]
    wave_low = wave_low_ref[...]
    quarter = LANES // 4
    group = max(2, 2 * LANES // rows)
    for first in range(0, len(chosen), group):
        places = range(first, min(first + group, len(chosen)))
        high = high_ref[first : first + len(places)].reshape(len(places) * rows, 2 * LANES)
        low = low_ref[first : first + len(places)].reshape(len(places) * rows, 2 * LANES)
        total = lax.dot_general(wave_high, high, dims, preferred_element_type=jnp.float32)
        total += lax.dot_general(wave_high, low, dims, preferred_element_type=jnp.float32)
        total += lax.dot_general(wave_low, high, dims, preferred_element_type=jnp.float32)

        def put(place, side, half, part, value):
            k1 = chosen[place]
            if side == 1 and (k1 == 0 or k1 == RADIX // 2):
                return
            index = RADIX - k1 if side else k1
            at = (index % chan_count, half, index // chan_count)
            if not joined:
                at += (part,)
            out_ref[at] = value.astype(jnp.bfloat16)

        for side in range(2):
            for half in range(2):
                row_re = side * LANES + half * quarter
                row_im = row_re + 2 * quarter
                if not joined:
                    for i, place in enumerate(places):
                        columns = slice(i * rows, (i + 1) * rows)
                        put(place, side, half, 0, total[row_re : row_re + quarter, columns])
                        put(place, side, half, 1, total[row_im : row_im + quarter, columns])
                    continue
                for i in range(0, len(places), 2):
                    columns = slice(i * rows, min((i + 2) * rows, len(places) * rows))
                    re = total[row_re : row_re + quarter, columns]
                    im = total[row_im : row_im + quarter, columns]
                    if i + 1 == len(places):
                        put(places[i], side, half, 0, jnp.concatenate([re, im], axis=1))
                        continue
                    low_lanes = lax.broadcasted_iota(jnp.int32, re.shape, 1) < rows
                    put(places[i], side, half, 0, jnp.where(low_lanes, re, pltpu.roll(im, rows, 1)))
                    put(
                        places[i + 1], side, half, 0, jnp.where(low_lanes, pltpu.roll(re, rows, 1), im)
                    )


def transform_tables(fft_len):
    cos, sin = turn_tables(fft_len)
    wave = wave_matrix(fft_len)
    wave_high = wave.astype(jnp.bfloat16)
    wave_low = (wave - wave_high.astype(np.float64)).astype(jnp.bfloat16)
    return (
        jnp.asarray(cos, jnp.float32),
        jnp.asarray(sin, jnp.float32),
        jnp.asarray(wave_high),
        jnp.asarray(wave_low),
    )


def transform_scratch(rows):
    count = len(first_index_list())
    return [
        pltpu.VMEM((8, 5, 2, 16, LANES), jnp.float32),
        pltpu.VMEM((count, rows, 2 * LANES), jnp.bfloat16),
        pltpu.VMEM((count, rows, 2 * LANES), jnp.bfloat16),
    ]


def transform(samples):
    chan_count, rows, block_len = samples.shape
    whole = pl.BlockSpec(memory_space=pltpu.VMEM)
    shape = (chan_count, 2, RADIX // chan_count, 2, LANES // 4, rows)
    return pl.pallas_call(
        functools.partial(transform_kernel, chan_count, False),
        out_shape=jax.ShapeDtypeStruct(shape, jnp.bfloat16),
        in_specs=[whole] * 5,
        out_specs=whole,
        scratch_shapes=transform_scratch(rows),
        compiler_params=pltpu.CompilerParams(vmem_limit_bytes=VMEM_LIMIT),
        name="transform",
    )(samples, *transform_tables(chan_count * block_len))


def transform_by_shift_kernel(chan_count, *refs):
    chan_ref, tables = refs[0], refs[1:5]
    in_refs, out_refs = refs[5 : 5 + chan_count], refs[5 + chan_count : 5 + 2 * chan_count]
    block_ref, result_ref, mid_ref, high_ref, low_ref, in_sem, out_sem = refs[5 + 2 * chan_count :]
    chan = chan_ref[0]
    fetches = []
    for shift, in_ref in enumerate(in_refs):
        source = lax.rem(chan + chan_count - shift, chan_count)
        fetches.append(pltpu.make_async_copy(in_ref, block_ref.at[source], in_sem.at[shift]))
        fetches[-1].start()
    for fetch in fetches:
        fetch.wait()
    transform_kernel(
        chan_count, True, block_ref, *tables, result_ref, mid_ref, high_ref, low_ref
    )
    sends = []
    for shift, out_ref in enumerate(out_refs):
        target = lax.rem(chan + shift, chan_count)
        sends.append(pltpu.make_async_copy(result_ref.at[target], out_ref, out_sem.at[shift]))
        sends[-1].start()
    for send in sends:
        send.wait()


def transform_by_shift(blocks, chan_id):
    chan_count = len(blocks)
    rows, block_len = blocks[0].shape
    whole = pl.BlockSpec(memory_space=pltpu.VMEM)
    apart = pl.BlockSpec(memory_space=pltpu.HBM)
    shape = (2, RADIX // chan_count, LANES // 4, 2 * rows)
    return pl.pallas_call(
        functools.partial(transform_by_shift_kernel, chan_count),
        out_shape=[jax.ShapeDtypeStruct(shape, jnp.bfloat16)] * chan_count,
        in_specs=[pl.BlockSpec(memory_space=pltpu.SMEM)] + [whole] * 4 + [apart] * chan_count,
        out_specs=[apart] * chan_count,
        scratch_shapes=[
            pltpu.VMEM((chan_count, rows, block_len), jnp.bfloat16),
            pltpu.VMEM((chan_count,) + shape, jnp.bfloat16),
        ]
        + transform_scratch(rows)
        + [pltpu.SemaphoreType.DMA((chan_count,)), pltpu.SemaphoreType.DMA((chan_count,))],
        compiler_params=pltpu.CompilerParams(vmem_limit_bytes=VMEM_LIMIT),
        name="transform_by_shift",
    )(chan_id, *transform_tables(chan_count * block_len), *blocks)


EIGHT = 8


def turn_kernel(group_ref, *refs):
    in_refs, (out_ref, near_ref, across_ref, wide_ref) = refs[:-4], refs[-4:]
    chan_count = len(in_refs)
    _, per, k2_count, _ = in_refs[0].shape
    pitch = per * chan_count + 1

    def spread(e, carry):
        for source, in_ref in enumerate(in_refs):
            for k2 in range(0, k2_count, EIGHT):
                value = in_ref[0, e, k2 : k2 + EIGHT, :].astype(jnp.float32)
                row = k2 * pitch + e * chan_count + source
                wide_ref[pl.ds(row, EIGHT, stride=pitch), :] = value
        return carry

    lax.fori_loop(0, per, spread, 0)

    def narrow(k2, carry):
        base = pl.multiple_of(k2 * per, per)
        for e in range(per):
            rows = pl.ds(k2 * pitch + e * chan_count, chan_count)
            out_ref[0, base + e] = wide_ref[rows, :].astype(jnp.bfloat16)
        return carry

    lax.fori_loop(0, k2_count, narrow, 0, unroll=2)

    half, group = pl.program_id(0), group_ref[0]

    @pl.when(half == 1 - group % 2)
    def _():
        near_ref[...] = out_ref[0]

    @pl.when(half == 1 - group // 2)
    def _():
        across_ref[...] = out_ref[0]


def turn(blocks, group_id):
    chan_count = len(blocks)
    halves, per, k2_count, lanes = blocks[0].shape
    one_half = (per * k2_count, chan_count, lanes)
    return pl.pallas_call(
        turn_kernel,
        out_shape=[
            jax.ShapeDtypeStruct((halves,) + one_half, jnp.bfloat16),
            jax.ShapeDtypeStruct(one_half, jnp.bfloat16),
            jax.ShapeDtypeStruct(one_half, jnp.bfloat16),
        ],
        grid_spec=pltpu.PrefetchScalarGridSpec(
            num_scalar_prefetch=1,
            grid=(halves,),
            in_specs=[pl.BlockSpec((1, per, k2_count, lanes), lambda u, g: (u, 0, 0, 0))]
            * chan_count,
            out_specs=[
                pl.BlockSpec((1,) + one_half, lambda u, g: (u, 0, 0, 0)),
                pl.BlockSpec(one_half, lambda u, g: (0, 0, 0)),
                pl.BlockSpec(one_half, lambda u, g: (0, 0, 0)),
            ],
            scratch_shapes=[pltpu.VMEM((k2_count * (per * chan_count + 1), lanes), jnp.float32)],
        ),
        compiler_params=pltpu.CompilerParams(vmem_limit_bytes=VMEM_LIMIT),
        name="turn",
    )(group_id, *blocks)


def left_kernel(*refs):
    chunk_refs, out_ref = refs[:-1], refs[-1]
    _, channels, _, lanes = chunk_refs[0].shape
    sig_count = lanes // 2

    def pair(step, carry):
        rows = []
        for i in range(2):
            values = [ref[0, 2 * step + i].astype(jnp.float32) for ref in chunk_refs]
            rows += values + [pltpu.roll(value, sig_count, 1) for value in values]
        stacked = jnp.concatenate(rows, axis=0)
        out_ref[0, step] = stacked.T[:sig_count].astype(jnp.bfloat16)
        return carry

    lax.fori_loop(0, channels // 2, pair, 0, unroll=32)


def left_operand(chunks):
    halves, channels, chan_count, lanes = chunks[0].shape
    depth = 2 * 2 * len(chunks) * chan_count
    tile = 128
    return pl.pallas_call(
        left_kernel,
        out_shape=jax.ShapeDtypeStruct((halves, channels // 2, lanes // 2, depth), jnp.bfloat16),
        grid=(halves, channels // tile),
        in_specs=[pl.BlockSpec((1, tile, chan_count, lanes), lambda u, i: (u, i, 0, 0))]
        * len(chunks),
        out_specs=pl.BlockSpec((1, tile // 2, lanes // 2, depth), lambda u, i: (u, i, 0, 0)),
        compiler_params=pltpu.CompilerParams(vmem_limit_bytes=VMEM_LIMIT),
        name="left_operand",
    )(*chunks)


def correlate_kernel(chunk_count, spec_count, group_ref, plan_ref, left_ref, *refs):
    del group_ref, plan_ref
    chunk_refs = refs[:chunk_count]
    out_ref, sum_ref = refs[-2:]
    _, channels, chan_count, lanes = (1,) + chunk_refs[0].shape
    sig_count = lanes // 2
    pitch = channels + 1
    sign = jnp.where(
        lax.broadcasted_iota(jnp.int32, (chan_count, lanes), 1) < sig_count, 1.0, -1.0
    ).astype(jnp.float32)

    def pair(step, carry):
        blocks = []
        for i in range(2):
            values = [ref[2 * step + i].astype(jnp.float32) for ref in chunk_refs]
            rows = [value * sign for value in values]
            rows += [pltpu.roll(value, sig_count, 1) for value in values]
            blocks.append(jnp.concatenate(rows, axis=0).astype(jnp.bfloat16))
        zero = jnp.zeros_like(blocks[0])
        weights = jnp.concatenate(
            [
                jnp.concatenate([blocks[0], zero], axis=1),
                jnp.concatenate([zero, blocks[1]], axis=1),
            ],
            axis=0,
        )
        both = jnp.dot(left_ref[0, step], weights, preferred_element_type=jnp.float32)
        for i in range(2):
            q = 2 * step + i
            for a in range(0, sig_count, EIGHT):
                sum_ref[pl.ds(a * pitch + q, EIGHT, stride=pitch), :] = both[
                    a : a + EIGHT, i * lanes : (i + 1) * lanes
                ]
        return carry

    lax.fori_loop(0, channels // 2, pair, 0, unroll=32)

    def finish(a, carry):
        rows = pl.ds(a * pitch, channels)
        out_ref[0, a] = (sum_ref[rows, :] * (1.0 / spec_count)).astype(jnp.bfloat16)
        return carry

    lax.fori_loop(0, sig_count, finish, 0, unroll=16)


def correlate(left, chunks, group_id, plan, distance, spec_count, so_far):
    channels, chan_count, lanes = chunks[0].shape
    sig_count, depth = left.shape[2:]
    rounds = plan.shape[0]
    tile = 128

    def half_of(group):
        return (group[0] > (group[0] ^ distance)).astype(jnp.int32)

    def round_of(group, plan):
        mate = group[0] ^ distance
        found = jnp.int32(0)
        for r in range(1, rounds):
            found = jnp.where(plan[r, group[0]] == mate, r, found)
        return found

    in_specs = [
        pl.BlockSpec((1, tile // 2, sig_count, depth), lambda i, g, p: (half_of(g), i, 0, 0)),
    ] + [pl.BlockSpec((tile, chan_count, lanes), lambda i, g, p: (i, 0, 0))] * len(chunks)
    operands = [left, *chunks]
    aliases = {}
    if so_far is not None:
        in_specs.append(pl.BlockSpec(memory_space=pl.ANY))
        operands.append(so_far)
        aliases = {len(operands) + 1: 0}
    return pl.pallas_call(
        functools.partial(correlate_kernel, len(chunks), spec_count),
        out_shape=jax.ShapeDtypeStruct((rounds, sig_count, channels, lanes), jnp.bfloat16),
        grid_spec=pltpu.PrefetchScalarGridSpec(
            num_scalar_prefetch=2,
            grid=(channels // tile,),
            in_specs=in_specs,
            out_specs=pl.BlockSpec(
                (1, sig_count, tile, lanes), lambda i, g, p: (round_of(g, p), 0, i, 0)
            ),
            scratch_shapes=[pltpu.VMEM((sig_count * (tile + 1), lanes), jnp.float32)],
        ),
        input_output_aliases=aliases,
        compiler_params=pltpu.CompilerParams(vmem_limit_bytes=VMEM_LIMIT),
        cost_estimate=pl.CostEstimate(
            flops=2 * channels * sig_count * depth * lanes,
            bytes_accessed=16 * 1024 * 1024,
            transcendentals=0,
        ),
        name="correlate",
    )(group_id, plan, *operands)


def correlate_plain(mine, theirs):
    left = mine.reshape(*mine.shape[:2], -1)
    right_re = theirs.reshape(left.shape)
    right_im = jnp.stack([-theirs[..., 1], theirs[..., 0]], axis=-1).reshape(left.shape)
    vis_re = jnp.einsum("kas,kbs->akb", left, right_re, preferred_element_type=jnp.float32)
    vis_im = jnp.einsum("kas,kbs->akb", left, right_im, preferred_element_type=jnp.float32)
    return jnp.concatenate([vis_re, vis_im], axis=-1) * (1.0 / mine.shape[2])


def by_channel(half, sig_count, spec_count):
    _, per, parts, k2, _ = half.shape
    turned = half.transpose(3, 1, 0, 4, 2).reshape(k2 * per, spec_count, sig_count, parts)
    return turned.transpose(0, 2, 1, 3)


def local_plain(voltages, plan):
    sig_count, frames, block_len = voltages.shape
    chan_count = lax.axis_size("chan")
    group_count = lax.axis_size("grp")
    spec_count = frames - TAPS + 1
    rows = spec_count * sig_count // chan_count
    chan_id = lax.axis_index("chan").astype(jnp.int32)
    group_id = lax.axis_index("grp")

    frames_first = voltages.transpose(1, 0, 2)
    filtered = filter_taps(frames_first, chan_id.reshape(1), chan_count, 0, spec_count)
    filtered = filtered.reshape(chan_count, rows, block_len)
    frames_here = lax.all_to_all(filtered, "chan", split_axis=0, concat_axis=0, tiled=True)
    spectra = transform(frames_here)
    channel = lax.all_to_all(spectra, "chan", split_axis=0, concat_axis=0, tiled=True)

    lower_half, upper_half = channel[:, 0], channel[:, 1]
    group_ids = jnp.arange(group_count)
    partner = jnp.sum(jnp.where(group_ids[None, :] == group_id, plan, 0), axis=1)
    listed = jnp.any(partner[:, None] == group_ids[None, :], axis=0)
    slot_shape = (group_count,) + (1,) * lower_half.ndim
    chosen_half = jnp.where(
        (group_ids > group_id).reshape(slot_shape), upper_half[None], lower_half[None]
    )
    slots = jnp.where(listed.reshape(slot_shape), chosen_half, jnp.zeros_like(chosen_half))
    received = lax.all_to_all(slots, "grp", split_axis=0, concat_axis=0, tiled=True)
    halves = (group_id > partner).astype(jnp.int32)
    results = []
    for round_index in range(plan.shape[0]):
        mine = lax.dynamic_index_in_dim(channel, halves[round_index], 1, keepdims=False)
        theirs = lax.dynamic_index_in_dim(received, partner[round_index], 0, keepdims=False)
        results.append(
            correlate_plain(
                by_channel(mine, sig_count, spec_count), by_channel(theirs, sig_count, spec_count)
            )
        )
    return jnp.stack(results).astype(jnp.bfloat16)


def local_overlapped(voltages, plan):
    _, frames, _ = voltages.shape
    chan_count = lax.axis_size("chan")
    group_count = lax.axis_size("grp")
    spec_count = frames - TAPS + 1
    chan_id = lax.axis_index("chan").astype(jnp.int32).reshape(1)
    group_id = lax.axis_index("grp").astype(jnp.int32).reshape(1)
    frames_first = voltages.transpose(1, 0, 2)

    def over_chan(blocks):
        moved = list(blocks)
        for shift in farthest_first(chan_count):
            pairs = [(c, (c + shift) % chan_count) for c in range(chan_count)]
            moved[shift] = lax.ppermute(blocks[shift], "chan", pairs)
        return moved

    def to_mate(value, distance):
        return lax.ppermute(value, "grp", [(g, g ^ distance) for g in range(group_count)])

    turned, near, across = [], [], []
    channels = []
    chunks = spec_count // chan_count
    for chunk in range(chunks):
        blocks = filter_by_shift(frames_first, chan_id, chan_count, chunk * chan_count)
        blocks = over_chan(blocks)
        blocks = transform_by_shift(blocks, chan_id)
        channels.append(over_chan(blocks))
    for channel in channels:
        halves, for_near, for_across = turn(channel, group_id)
        turned.append(halves)
        near = near + [to_mate(for_near, 1)]
        across = across + [to_mate(for_across, 2)]
    left = left_operand(turned)
    result = correlate(left, near, group_id, plan, 1, spec_count, None)
    across, result = lax.optimization_barrier((across, result))
    relayed = [to_mate(value, 1) for value in across]
    result = correlate(left, across, group_id, plan, 2, spec_count, result)
    return correlate(left, relayed, group_id, plan, 3, spec_count, result)


def farthest_first(chan_count):
    return sorted(range(1, chan_count), key=lambda shift: abs(shift - chan_count // 2))


def overlaps(group_count, chan_count):
    return group_count == 4 and chan_count == EIGHT


def local(voltages, plan):
    sig_count, frames, _ = voltages.shape
    chan_count = lax.axis_size("chan")
    group_count = lax.axis_size("grp")
    if (
        overlaps(group_count, chan_count)
        and plan.shape[0] == group_count - 1
        and frames - TAPS + 1 == 2 * chan_count
        and 2 * sig_count == LANES
    ):
        return local_overlapped(voltages, plan)
    return local_plain(voltages, plan)


def solution(mesh):
    in_specs = (P("grp", None, "chan"), P())
    out_specs = P(None, "grp", "chan", None)
    return jax.shard_map(local, mesh=mesh, in_specs=in_specs, out_specs=out_specs, check_vma=False)
```

```python
import functools
import math

import jax
import jax.numpy as jnp
import numpy as np
from jax import lax
from jax.experimental import pallas as pl
from jax.experimental.pallas import tpu as pltpu
from jax.sharding import PartitionSpec as P


TAPS = 16
LANES = 128
RADIX = 64
EIGHT = 8
VMEM_LIMIT = 67_000_000


def tap_table(fft_len):
    position = np.arange(TAPS * fft_len, dtype=np.float64)
    total = TAPS * fft_len
    window = 0.5 - 0.5 * np.cos(2.0 * np.pi * position / total)
    return (window * np.sinc((position - 0.5 * total) / fft_len)).reshape(TAPS, fft_len)


def filter_kernel(chan_ref, volt_ref, coeff_ref, out_ref):
    del chan_ref
    frames, sig_tile, block_len = volt_ref.shape
    spec_count = frames - TAPS + 1

    def one_tile(tile, carry):
        cols = pl.ds(pl.multiple_of(tile * LANES, LANES), LANES)
        coeff = [
            jnp.broadcast_to(coeff_ref[0, t : t + 1, cols], (EIGHT, LANES)) for t in range(TAPS)
        ]
        for low in range(0, sig_tile, EIGHT):
            rows = slice(low, low + EIGHT)
            total = [None] * spec_count
            for frame in range(frames):
                sample = volt_ref[frame, rows, cols].astype(jnp.float32)
                for s in range(max(0, frame - TAPS + 1), min(spec_count - 1, frame) + 1):
                    term = coeff[frame - s] * sample
                    total[s] = term if total[s] is None else total[s] + term
                if frame >= TAPS - 1:
                    s = frame - TAPS + 1
                    out_ref[s, rows, cols] = total[s].astype(jnp.bfloat16)
                    total[s] = None
        return carry

    lax.fori_loop(0, block_len // LANES, one_tile, 0)


def filter_taps(frames_first, chan_id, chan_count, first, spec_count):
    _, sig_count, block_len = frames_first.shape
    frames = spec_count + TAPS - 1
    table = tap_table(block_len * chan_count).astype(np.float32)
    table = np.ascontiguousarray(table.reshape(TAPS, chan_count, block_len).transpose(1, 0, 2))
    sig_tile = 32
    return pl.pallas_call(
        filter_kernel,
        out_shape=jax.ShapeDtypeStruct((spec_count, sig_count, block_len), jnp.bfloat16),
        grid_spec=pltpu.PrefetchScalarGridSpec(
            num_scalar_prefetch=1,
            grid=(sig_count // sig_tile,),
            in_specs=[
                pl.BlockSpec(
                    (pl.Element(frames), pl.Element(sig_tile), pl.Element(block_len)),
                    lambda i, c: (first, i * sig_tile, 0),
                ),
                pl.BlockSpec((1, TAPS, block_len), lambda i, c: (c[0], 0, 0)),
            ],
            out_specs=pl.BlockSpec((spec_count, sig_tile, block_len), lambda i, c: (0, i, 0)),
        ),
        compiler_params=pltpu.CompilerParams(vmem_limit_bytes=VMEM_LIMIT),
        name="filter_taps",
    )(chan_id, frames_first, jnp.asarray(table))


def filter_by_pair_kernel(pairs, chan_ref, volt_ref, coeff_ref, *refs):
    out_refs, block_ref = refs[:-1], refs[-1]
    filter_kernel(chan_ref, volt_ref, coeff_ref, block_ref)
    for pair, out_ref in zip(pairs, out_refs):
        out_ref[...] = block_ref[(chan_ref[0] ^ pair) % len(pairs)]


def filter_by_pair(frames_first, chan_id, chan_count, first, pairs):
    _, sig_count, block_len = frames_first.shape
    count = len(pairs)
    frames = count + TAPS - 1
    table = tap_table(block_len * chan_count).astype(np.float32)
    table = np.ascontiguousarray(table.reshape(TAPS, chan_count, block_len).transpose(1, 0, 2))
    sig_tile = 32

    def frames_at(i, chan):
        lowest = (chan[0] ^ pairs[0]) // count * count
        return first + lowest, i * sig_tile, 0

    return pl.pallas_call(
        functools.partial(filter_by_pair_kernel, pairs),
        out_shape=[jax.ShapeDtypeStruct((sig_count, block_len), jnp.bfloat16)] * count,
        grid_spec=pltpu.PrefetchScalarGridSpec(
            num_scalar_prefetch=1,
            grid=(sig_count // sig_tile,),
            in_specs=[
                pl.BlockSpec(
                    (pl.Element(frames), pl.Element(sig_tile), pl.Element(block_len)), frames_at
                ),
                pl.BlockSpec((1, TAPS, block_len), lambda i, c: (c[0], 0, 0)),
            ],
            out_specs=[pl.BlockSpec((sig_tile, block_len), lambda i, c: (i, 0))] * count,
            scratch_shapes=[pltpu.VMEM((count, sig_tile, block_len), jnp.bfloat16)],
        ),
        compiler_params=pltpu.CompilerParams(vmem_limit_bytes=VMEM_LIMIT),
        name="filter_by_pair",
    )(chan_id, frames_first, jnp.asarray(table))


def cadd(a, b):
    if a is None:
        return b
    if b is None:
        return a
    return a + b


def csub(a, b):
    if b is None:
        return a
    if a is None:
        return -b
    return a - b


def scale_by(value, re, im):
    vr, vi = value
    eps = 1e-12

    def mul(x, f):
        if x is None or abs(f) < eps:
            return None
        if abs(f - 1.0) < eps:
            return x
        if abs(f + 1.0) < eps:
            return -x
        return x * f

    return csub(mul(vr, re), mul(vi, im)), cadd(mul(vr, im), mul(vi, re))


def plus(a, b):
    return cadd(a[0], b[0]), cadd(a[1], b[1])


def minus(a, b):
    return csub(a[0], b[0]), csub(a[1], b[1])


def dft(values, wanted=None):
    n = len(values)
    if n == 1:
        return list(values)
    even = dft(values[0::2])
    odd = dft(values[1::2])
    out = [None] * n
    for k in range(n // 2):
        if wanted is not None and k not in wanted and k + n // 2 not in wanted:
            continue
        angle = -2.0 * math.pi * k / n
        turned = scale_by(odd[k], math.cos(angle), math.sin(angle))
        out[k] = plus(even[k], turned)
        out[k + n // 2] = minus(even[k], turned)
    return out


def first_index_list():
    chosen = []
    for c in range(5):
        for e in range(8):
            k1 = c + 8 * e
            if c in (0, 4) and k1 > RADIX // 2:
                continue
            chosen.append(k1)
    return chosen


def turn_tables(fft_len):
    k1 = np.array(first_index_list())[:, None]
    angle = 2.0 * np.pi * ((k1 * np.arange(LANES)[None, :]) % fft_len) / fft_len
    return np.cos(angle), np.sin(angle)


def wave_matrix(fft_len):
    gain = 1.0 / (64.0 * math.sqrt(fft_len))
    half = LANES // 2
    n2 = np.arange(LANES)[None, :]
    k2 = np.arange(half)[:, None]
    rows = []
    for index, flip in ((k2, 1.0), (LANES - 1 - k2, -1.0)):
        angle = 2.0 * np.pi * ((index * n2) % LANES) / LANES
        cos, sin = np.cos(angle) * gain, np.sin(angle) * gain
        rows.append(np.concatenate([cos, sin], axis=1))
        rows.append(np.concatenate([-sin, cos], axis=1) * flip)
    return np.concatenate(rows, axis=0)


def split_two(value):
    high = value.astype(jnp.bfloat16)
    return high, (value - high.astype(jnp.float32)).astype(jnp.bfloat16)


def transform_kernel(
    chan_count, joined, in_ref, cos_ref, sin_ref, wave_high_ref, wave_low_ref, out_ref, mid_ref, high_ref, low_ref
):
    _, rows, block_len = in_ref.shape
    per_block = block_len // LANES
    tile = 16
    chosen = first_index_list()

    def row_tile(step, carry):
        at = pl.ds(pl.multiple_of(step * tile, tile), tile)
        present = set()
        for low_n in range(8):
            column = []
            for high_n in range(8):
                n1 = high_n * 8 + low_n
                lanes = slice((n1 % per_block) * LANES, (n1 % per_block + 1) * LANES)
                column.append((in_ref[n1 // per_block, at, lanes].astype(jnp.float32), None))
            spread = dft(column, wanted=range(5))
            for c in range(5):
                angle = -2.0 * math.pi * low_n * c / RADIX
                re, im = scale_by(spread[c], math.cos(angle), math.sin(angle))
                for part, value in enumerate((re, im)):
                    if value is not None:
                        mid_ref[low_n, c, part] = value
                        present.add((low_n, c, part))
        for c in range(5):
            wanted = [e for e in range(8) if c + 8 * e in chosen]
            values = []
            for low_n in range(8):
                values.append(
                    tuple(
                        mid_ref[low_n, c, part] if (low_n, c, part) in present else None
                        for part in range(2)
                    )
                )
            spread = dft(values, wanted=wanted)
            for e in wanted:
                place = chosen.index(c + 8 * e)
                cos = cos_ref[place : place + 1, :]
                sin = sin_ref[place : place + 1, :]
                re, im = spread[e]
                if im is None:
                    turned_re, turned_im = re * cos, -(re * sin)
                else:
                    turned_re, turned_im = re * cos + im * sin, im * cos - re * sin
                a, b = split_two(turned_re)
                high_ref[place, at, :LANES] = a
                low_ref[place, at, :LANES] = b
                a, b = split_two(turned_im)
                high_ref[place, at, LANES:] = a
                low_ref[place, at, LANES:] = b
        return carry

    lax.fori_loop(0, rows // tile, row_tile, 0)

    dims = (((1,), (1,)), ((), ()))
    wave_high = wave_high_ref[...]
    wave_low = wave_low_ref[...]
    quarter = LANES // 4
    group = max(2, 2 * LANES // rows)
    for first in range(0, len(chosen), group):
        places = range(first, min(first + group, len(chosen)))
        high = high_ref[first : first + len(places)].reshape(len(places) * rows, 2 * LANES)
        low = low_ref[first : first + len(places)].reshape(len(places) * rows, 2 * LANES)
        total = lax.dot_general(wave_high, high, dims, preferred_element_type=jnp.float32)
        total += lax.dot_general(wave_high, low, dims, preferred_element_type=jnp.float32)
        total += lax.dot_general(wave_low, high, dims, preferred_element_type=jnp.float32)

        def put(place, side, half, part, value):
            k1 = chosen[place]
            if side == 1 and (k1 == 0 or k1 == RADIX // 2):
                return
            index = RADIX - k1 if side else k1
            at = (index % chan_count, half, index // chan_count)
            if not joined:
                at += (part,)
            out_ref[at] = value.astype(jnp.bfloat16)

        for side in range(2):
            for half in range(2):
                row_re = side * LANES + half * quarter
                row_im = row_re + 2 * quarter
                if not joined:
                    for i, place in enumerate(places):
                        columns = slice(i * rows, (i + 1) * rows)
                        put(place, side, half, 0, total[row_re : row_re + quarter, columns])
                        put(place, side, half, 1, total[row_im : row_im + quarter, columns])
                    continue
                for i in range(0, len(places), 2):
                    columns = slice(i * rows, min((i + 2) * rows, len(places) * rows))
                    re = total[row_re : row_re + quarter, columns]
                    im = total[row_im : row_im + quarter, columns]
                    if i + 1 == len(places):
                        put(places[i], side, half, 0, jnp.concatenate([re, im], axis=1))
                        continue
                    low_lanes = lax.broadcasted_iota(jnp.int32, re.shape, 1) < rows
                    put(places[i], side, half, 0, jnp.where(low_lanes, re, pltpu.roll(im, rows, 1)))
                    put(
                        places[i + 1], side, half, 0, jnp.where(low_lanes, pltpu.roll(re, rows, 1), im)
                    )


def transform_tables(fft_len):
    cos, sin = turn_tables(fft_len)
    wave = wave_matrix(fft_len)
    wave_high = wave.astype(jnp.bfloat16)
    wave_low = (wave - wave_high.astype(np.float64)).astype(jnp.bfloat16)
    return (
        jnp.asarray(cos, jnp.float32),
        jnp.asarray(sin, jnp.float32),
        jnp.asarray(wave_high),
        jnp.asarray(wave_low),
    )


def transform_scratch(rows):
    count = len(first_index_list())
    return [
        pltpu.VMEM((8, 5, 2, 16, LANES), jnp.float32),
        pltpu.VMEM((count, rows, 2 * LANES), jnp.bfloat16),
        pltpu.VMEM((count, rows, 2 * LANES), jnp.bfloat16),
    ]


def transform(samples):
    chan_count, rows, block_len = samples.shape
    whole = pl.BlockSpec(memory_space=pltpu.VMEM)
    shape = (chan_count, 2, RADIX // chan_count, 2, LANES // 4, rows)
    return pl.pallas_call(
        functools.partial(transform_kernel, chan_count, False),
        out_shape=jax.ShapeDtypeStruct(shape, jnp.bfloat16),
        in_specs=[whole] * 5,
        out_specs=whole,
        scratch_shapes=transform_scratch(rows),
        compiler_params=pltpu.CompilerParams(vmem_limit_bytes=VMEM_LIMIT),
        name="transform",
    )(samples, *transform_tables(chan_count * block_len))


def transform_by_pair_kernel(chan_count, *refs):
    chan_ref, tables = refs[0], refs[1:5]
    in_refs, out_refs = refs[5 : 5 + chan_count], refs[5 + chan_count : 5 + 2 * chan_count]
    block_ref, result_ref, mid_ref, high_ref, low_ref, in_sem, out_sem = refs[5 + 2 * chan_count :]
    chan = chan_ref[0]
    fetches = []
    for pair, in_ref in enumerate(in_refs):
        source = chan ^ pair
        fetches.append(pltpu.make_async_copy(in_ref, block_ref.at[source], in_sem.at[pair]))
        fetches[-1].start()
    for fetch in fetches:
        fetch.wait()
    transform_kernel(
        chan_count, True, block_ref, *tables, result_ref, mid_ref, high_ref, low_ref
    )
    sends = []
    for pair, out_ref in enumerate(out_refs):
        target = chan ^ pair
        sends.append(pltpu.make_async_copy(result_ref.at[target], out_ref, out_sem.at[pair]))
        sends[-1].start()
    for send in sends:
        send.wait()


def transform_by_pair(blocks, chan_id):
    chan_count = len(blocks)
    rows, block_len = blocks[0].shape
    whole = pl.BlockSpec(memory_space=pltpu.VMEM)
    apart = pl.BlockSpec(memory_space=pltpu.HBM)
    shape = (2, RADIX // chan_count, LANES // 4, 2 * rows)
    return pl.pallas_call(
        functools.partial(transform_by_pair_kernel, chan_count),
        out_shape=[jax.ShapeDtypeStruct(shape, jnp.bfloat16)] * chan_count,
        in_specs=[pl.BlockSpec(memory_space=pltpu.SMEM)] + [whole] * 4 + [apart] * chan_count,
        out_specs=[apart] * chan_count,
        scratch_shapes=[
            pltpu.VMEM((chan_count, rows, block_len), jnp.bfloat16),
            pltpu.VMEM((chan_count,) + shape, jnp.bfloat16),
        ]
        + transform_scratch(rows)
        + [pltpu.SemaphoreType.DMA((chan_count,)), pltpu.SemaphoreType.DMA((chan_count,))],
        compiler_params=pltpu.CompilerParams(vmem_limit_bytes=VMEM_LIMIT),
        name="transform_by_pair",
    )(chan_id, *transform_tables(chan_count * block_len), *blocks)


def turn_kernel(group_ref, *refs):
    in_refs, (out_ref, near_ref, across_ref, wide_ref) = refs[:-4], refs[-4:]
    chan_count = len(in_refs)
    _, per, k2_count, _ = in_refs[0].shape
    pitch = per * chan_count + 1

    def spread(e, carry):
        for source, in_ref in enumerate(in_refs):
            for k2 in range(0, k2_count, EIGHT):
                value = in_ref[0, e, k2 : k2 + EIGHT, :].astype(jnp.float32)
                row = k2 * pitch + e * chan_count + source
                wide_ref[pl.ds(row, EIGHT, stride=pitch), :] = value
        return carry

    lax.fori_loop(0, per, spread, 0)

    def narrow(k2, carry):
        base = pl.multiple_of(k2 * per, per)
        for e in range(per):
            rows = pl.ds(k2 * pitch + e * chan_count, chan_count)
            out_ref[0, base + e] = wide_ref[rows, :].astype(jnp.bfloat16)
        return carry

    lax.fori_loop(0, k2_count, narrow, 0, unroll=2)

    half, group = pl.program_id(0), group_ref[0]

    @pl.when(half == 1 - group % 2)
    def _():
        near_ref[...] = out_ref[0]

    @pl.when(half == 1 - group // 2)
    def _():
        across_ref[...] = out_ref[0]


def turn(blocks, group_id):
    chan_count = len(blocks)
    halves, per, k2_count, lanes = blocks[0].shape
    one_half = (per * k2_count, chan_count, lanes)
    return pl.pallas_call(
        turn_kernel,
        out_shape=[
            jax.ShapeDtypeStruct((halves,) + one_half, jnp.bfloat16),
            jax.ShapeDtypeStruct(one_half, jnp.bfloat16),
            jax.ShapeDtypeStruct(one_half, jnp.bfloat16),
        ],
        grid_spec=pltpu.PrefetchScalarGridSpec(
            num_scalar_prefetch=1,
            grid=(halves,),
            in_specs=[pl.BlockSpec((1, per, k2_count, lanes), lambda u, g: (u, 0, 0, 0))]
            * chan_count,
            out_specs=[
                pl.BlockSpec((1,) + one_half, lambda u, g: (u, 0, 0, 0)),
                pl.BlockSpec(one_half, lambda u, g: (0, 0, 0)),
                pl.BlockSpec(one_half, lambda u, g: (0, 0, 0)),
            ],
            scratch_shapes=[pltpu.VMEM((k2_count * (per * chan_count + 1), lanes), jnp.float32)],
        ),
        compiler_params=pltpu.CompilerParams(vmem_limit_bytes=VMEM_LIMIT),
        name="turn",
    )(group_id, *blocks)


def left_kernel(*refs):
    chunk_refs, out_ref = refs[:-1], refs[-1]
    _, channels, _, lanes = chunk_refs[0].shape
    sig_count = lanes // 2
    together = 2 * lanes // out_ref.shape[3]
    width = out_ref.shape[3]
    count = channels // out_ref.shape[1]
    row = lax.broadcasted_iota(jnp.int32, (sig_count, lanes), 0)
    column = lax.broadcasted_iota(jnp.int32, (sig_count, lanes), 1)
    identity = (row == column).astype(jnp.bfloat16)

    def some_pairs(step, carry):
        rows = []
        for i in range(count * together):
            values = [ref[0, count * together * step + i].astype(jnp.float32) for ref in chunk_refs]
            rows += values + [pltpu.roll(value, sig_count, 1) for value in values]
        stacked = jnp.concatenate(rows, axis=0).astype(jnp.bfloat16)
        turned = lax.dot_general(
            identity, stacked, (((1,), (1,)), ((), ())), preferred_element_type=jnp.float32
        )
        for i in range(together):
            out_ref[0, together * step + i] = turned[:, i * width : (i + 1) * width].astype(
                jnp.bfloat16
            )
        return carry

    lax.fori_loop(0, channels // (count * together), some_pairs, 0, unroll=16)


def left_operand(chunks):
    halves, channels, chan_count, lanes = chunks[0].shape
    depth = 2 * len(chunks) * chan_count
    count = lanes // depth
    tile = 128
    return pl.pallas_call(
        left_kernel,
        out_shape=jax.ShapeDtypeStruct((halves, channels // count, lanes // 2, lanes), jnp.bfloat16),
        grid=(halves, channels // tile),
        in_specs=[pl.BlockSpec((1, tile, chan_count, lanes), lambda u, i: (u, i, 0, 0))]
        * len(chunks),
        out_specs=pl.BlockSpec((1, tile // count, lanes // 2, lanes), lambda u, i: (u, i, 0, 0)),
        compiler_params=pltpu.CompilerParams(vmem_limit_bytes=VMEM_LIMIT),
        name="left_operand",
    )(*chunks)


def correlate_kernel(chunk_count, spec_count, group_ref, plan_ref, left_ref, *refs):
    del group_ref, plan_ref
    chunk_refs = refs[:chunk_count]
    out_ref, sum_ref = refs[-2:]
    _, channels, chan_count, lanes = (1,) + chunk_refs[0].shape
    sig_count = lanes // 2
    pitch = channels + 1
    sign = jnp.where(
        lax.broadcasted_iota(jnp.int32, (chan_count, lanes), 1) < sig_count, 1.0, -1.0
    ).astype(jnp.float32)

    def pairs(step, carry):
        left = left_ref[0, step]
        for i in range(2):
            pair(2 * step + i, left[:, i * sig_count : (i + 1) * sig_count])
        return carry

    def pair(step, left):
        blocks = []
        for i in range(2):
            values = [ref[2 * step + i].astype(jnp.float32) for ref in chunk_refs]
            rows = [value * sign for value in values]
            rows += [pltpu.roll(value, sig_count, 1) for value in values]
            blocks.append(jnp.concatenate(rows, axis=0).astype(jnp.bfloat16))
        zero = jnp.zeros_like(blocks[0])
        weights = jnp.concatenate(
            [
                jnp.concatenate([blocks[0], zero], axis=1),
                jnp.concatenate([zero, blocks[1]], axis=1),
            ],
            axis=0,
        )
        both = jnp.dot(left, weights, preferred_element_type=jnp.float32)
        for i in range(2):
            q = 2 * step + i
            for a in range(0, sig_count, EIGHT):
                sum_ref[pl.ds(a * pitch + q, EIGHT, stride=pitch), :] = both[
                    a : a + EIGHT, i * lanes : (i + 1) * lanes
                ]

    lax.fori_loop(0, channels // 4, pairs, 0, unroll=32)

    def finish(a, carry):
        rows = pl.ds(a * pitch, channels)
        out_ref[0, a] = (sum_ref[rows, :] * (1.0 / spec_count)).astype(jnp.bfloat16)
        return carry

    lax.fori_loop(0, sig_count, finish, 0, unroll=16)


def correlate(left, chunks, group_id, plan, distance, spec_count, so_far):
    channels, chan_count, lanes = chunks[0].shape
    per_left = channels // left.shape[1]
    sig_count, depth = left.shape[2:]
    rounds = plan.shape[0]
    tile = 128

    def half_of(group):
        return (group[0] > (group[0] ^ distance)).astype(jnp.int32)

    def round_of(group, plan):
        mate = group[0] ^ distance
        found = jnp.int32(0)
        for r in range(1, rounds):
            found = jnp.where(plan[r, group[0]] == mate, r, found)
        return found

    in_specs = [
        pl.BlockSpec((1, tile // per_left, sig_count, depth), lambda i, g, p: (half_of(g), i, 0, 0)),
    ] + [pl.BlockSpec((tile, chan_count, lanes), lambda i, g, p: (i, 0, 0))] * len(chunks)
    operands = [left, *chunks]
    aliases = {}
    if so_far is not None:
        in_specs.append(pl.BlockSpec(memory_space=pl.ANY))
        operands.append(so_far)
        aliases = {len(operands) + 1: 0}
    return pl.pallas_call(
        functools.partial(correlate_kernel, len(chunks), spec_count),
        out_shape=jax.ShapeDtypeStruct((rounds, sig_count, channels, lanes), jnp.bfloat16),
        grid_spec=pltpu.PrefetchScalarGridSpec(
            num_scalar_prefetch=2,
            grid=(channels // tile,),
            in_specs=in_specs,
            out_specs=pl.BlockSpec(
                (1, sig_count, tile, lanes), lambda i, g, p: (round_of(g, p), 0, i, 0)
            ),
            scratch_shapes=[pltpu.VMEM((sig_count * (tile + 1), lanes), jnp.float32)],
        ),
        input_output_aliases=aliases,
        compiler_params=pltpu.CompilerParams(vmem_limit_bytes=VMEM_LIMIT),
        cost_estimate=pl.CostEstimate(
            flops=2 * channels * sig_count * depth * lanes,
            bytes_accessed=16 * 1024 * 1024,
            transcendentals=0,
        ),
        name="correlate",
    )(group_id, plan, *operands)


def correlate_plain(mine, theirs):
    left = mine.reshape(*mine.shape[:2], -1)
    right_re = theirs.reshape(left.shape)
    right_im = jnp.stack([-theirs[..., 1], theirs[..., 0]], axis=-1).reshape(left.shape)
    vis_re = jnp.einsum("kas,kbs->akb", left, right_re, preferred_element_type=jnp.float32)
    vis_im = jnp.einsum("kas,kbs->akb", left, right_im, preferred_element_type=jnp.float32)
    return jnp.concatenate([vis_re, vis_im], axis=-1) * (1.0 / mine.shape[2])


def by_channel(half, sig_count, spec_count):
    _, per, parts, k2, _ = half.shape
    turned = half.transpose(3, 1, 0, 4, 2).reshape(k2 * per, spec_count, sig_count, parts)
    return turned.transpose(0, 2, 1, 3)


def local_plain(voltages, plan):
    sig_count, frames, block_len = voltages.shape
    chan_count = lax.axis_size("chan")
    group_count = lax.axis_size("grp")
    spec_count = frames - TAPS + 1
    rows = spec_count * sig_count // chan_count
    chan_id = lax.axis_index("chan").astype(jnp.int32)
    group_id = lax.axis_index("grp")

    frames_first = voltages.transpose(1, 0, 2)
    filtered = filter_taps(frames_first, chan_id.reshape(1), chan_count, 0, spec_count)
    filtered = filtered.reshape(chan_count, rows, block_len)
    frames_here = lax.all_to_all(filtered, "chan", split_axis=0, concat_axis=0, tiled=True)
    spectra = transform(frames_here)
    channel = lax.all_to_all(spectra, "chan", split_axis=0, concat_axis=0, tiled=True)

    lower_half, upper_half = channel[:, 0], channel[:, 1]
    group_ids = jnp.arange(group_count)
    partner = jnp.sum(jnp.where(group_ids[None, :] == group_id, plan, 0), axis=1)
    listed = jnp.any(partner[:, None] == group_ids[None, :], axis=0)
    slot_shape = (group_count,) + (1,) * lower_half.ndim
    chosen_half = jnp.where(
        (group_ids > group_id).reshape(slot_shape), upper_half[None], lower_half[None]
    )
    slots = jnp.where(listed.reshape(slot_shape), chosen_half, jnp.zeros_like(chosen_half))
    received = lax.all_to_all(slots, "grp", split_axis=0, concat_axis=0, tiled=True)
    halves = (group_id > partner).astype(jnp.int32)
    results = []
    for round_index in range(plan.shape[0]):
        mine = lax.dynamic_index_in_dim(channel, halves[round_index], 1, keepdims=False)
        theirs = lax.dynamic_index_in_dim(received, partner[round_index], 0, keepdims=False)
        results.append(
            correlate_plain(
                by_channel(mine, sig_count, spec_count), by_channel(theirs, sig_count, spec_count)
            )
        )
    return jnp.stack(results).astype(jnp.bfloat16)


def local_overlapped(voltages, plan):
    _, frames, _ = voltages.shape
    chan_count = lax.axis_size("chan")
    group_count = lax.axis_size("grp")
    spec_count = frames - TAPS + 1
    chan_id = lax.axis_index("chan").astype(jnp.int32).reshape(1)
    group_id = lax.axis_index("grp").astype(jnp.int32).reshape(1)
    frames_first = voltages.transpose(1, 0, 2)

    def over_chan(blocks):
        moved = list(blocks)
        for pair in farthest_first(chan_count):
            moved[pair] = lax.ppermute(
                blocks[pair], "chan", [(c, c ^ pair) for c in range(chan_count)]
            )
        return moved

    def to_mate(value, distance):
        return lax.ppermute(value, "grp", [(g, g ^ distance) for g in range(group_count)])

    turned, near, across = [], [], []
    channels = []
    chunks = spec_count // chan_count
    for chunk in range(chunks):
        if chunk:
            parts = (range(chan_count),)
        else:
            parts = (range(chan_count // 2, chan_count), range(chan_count // 2))
        blocks = [None] * chan_count
        for pairs in parts:
            blocks[pairs.start : pairs.stop] = filter_by_pair(
                frames_first, chan_id, chan_count, chunk * chan_count, pairs
            )
        blocks = over_chan(blocks)
        blocks = transform_by_pair(blocks, chan_id)
        channels.append(over_chan(blocks))
    for channel in channels:
        halves, for_near, for_across = turn(channel, group_id)
        turned.append(halves)
        near = near + [to_mate(for_near, 1)]
        across = across + [to_mate(for_across, 2)]
    left = left_operand(turned)
    result = correlate(left, near, group_id, plan, 1, spec_count, None)
    across, result = lax.optimization_barrier((across, result))
    relayed = [to_mate(value, 1) for value in across]
    result = correlate(left, across, group_id, plan, 2, spec_count, result)
    return correlate(left, relayed, group_id, plan, 3, spec_count, result)


def farthest_first(chan_count):
    half = chan_count // 2
    return list(range(half, chan_count)) + list(range(1, half))


def overlaps(group_count, chan_count):
    return group_count == 4 and chan_count == EIGHT


def local(voltages, plan):
    sig_count, frames, _ = voltages.shape
    chan_count = lax.axis_size("chan")
    group_count = lax.axis_size("grp")
    if (
        overlaps(group_count, chan_count)
        and plan.shape[0] == group_count - 1
        and frames - TAPS + 1 == 2 * chan_count
        and 2 * sig_count == LANES
    ):
        return local_overlapped(voltages, plan)
    return local_plain(voltages, plan)


def solution(mesh):
    in_specs = (P("grp", None, "chan"), P())
    out_specs = P(None, "grp", "chan", None)
    return jax.shard_map(local, mesh=mesh, in_specs=in_specs, out_specs=out_specs, check_vma=False)
```

```python
import functools
import math

import jax
import jax.numpy as jnp
import numpy as np
from jax import lax
from jax.experimental import pallas as pl
from jax.experimental.pallas import tpu as pltpu
from jax.sharding import PartitionSpec as P


TAPS = 16
LANES = 128
RADIX = 64
EIGHT = 8
VMEM_LIMIT = 67_000_000


def tap_table(fft_len):
    position = np.arange(TAPS * fft_len, dtype=np.float64)
    total = TAPS * fft_len
    window = 0.5 - 0.5 * np.cos(2.0 * np.pi * position / total)
    return (window * np.sinc((position - 0.5 * total) / fft_len)).reshape(TAPS, fft_len)


def filter_kernel(chan_ref, volt_ref, coeff_ref, out_ref):
    del chan_ref
    frames, sig_tile, block_len = volt_ref.shape
    spec_count = frames - TAPS + 1

    def one_tile(tile, carry):
        cols = pl.ds(pl.multiple_of(tile * LANES, LANES), LANES)
        coeff = [
            jnp.broadcast_to(coeff_ref[0, t : t + 1, cols], (EIGHT, LANES)) for t in range(TAPS)
        ]
        for low in range(0, sig_tile, EIGHT):
            rows = slice(low, low + EIGHT)
            total = [None] * spec_count
            for frame in range(frames):
                sample = volt_ref[frame, rows, cols].astype(jnp.float32)
                for s in range(max(0, frame - TAPS + 1), min(spec_count - 1, frame) + 1):
                    term = coeff[frame - s] * sample
                    total[s] = term if total[s] is None else total[s] + term
                if frame >= TAPS - 1:
                    s = frame - TAPS + 1
                    out_ref[s, rows, cols] = total[s].astype(jnp.bfloat16)
                    total[s] = None
        return carry

    lax.fori_loop(0, block_len // LANES, one_tile, 0)


def filter_taps(frames_first, chan_id, chan_count, first, spec_count):
    _, sig_count, block_len = frames_first.shape
    frames = spec_count + TAPS - 1
    table = tap_table(block_len * chan_count).astype(np.float32)
    table = np.ascontiguousarray(table.reshape(TAPS, chan_count, block_len).transpose(1, 0, 2))
    sig_tile = 32
    return pl.pallas_call(
        filter_kernel,
        out_shape=jax.ShapeDtypeStruct((spec_count, sig_count, block_len), jnp.bfloat16),
        grid_spec=pltpu.PrefetchScalarGridSpec(
            num_scalar_prefetch=1,
            grid=(sig_count // sig_tile,),
            in_specs=[
                pl.BlockSpec(
                    (pl.Element(frames), pl.Element(sig_tile), pl.Element(block_len)),
                    lambda i, c: (first, i * sig_tile, 0),
                ),
                pl.BlockSpec((1, TAPS, block_len), lambda i, c: (c[0], 0, 0)),
            ],
            out_specs=pl.BlockSpec((spec_count, sig_tile, block_len), lambda i, c: (0, i, 0)),
        ),
        compiler_params=pltpu.CompilerParams(vmem_limit_bytes=VMEM_LIMIT),
        name="filter_taps",
    )(chan_id, frames_first, jnp.asarray(table))


def filter_by_pair_kernel(pairs, chan_ref, volt_ref, coeff_ref, *refs):
    out_refs, block_ref = refs[:-1], refs[-1]
    filter_kernel(chan_ref, volt_ref, coeff_ref, block_ref)
    for pair, out_ref in zip(pairs, out_refs):
        out_ref[...] = block_ref[(chan_ref[0] ^ pair) % len(pairs)]


def filter_by_pair(frames_first, chan_id, chan_count, first, pairs):
    _, sig_count, block_len = frames_first.shape
    count = len(pairs)
    frames = count + TAPS - 1
    table = tap_table(block_len * chan_count).astype(np.float32)
    table = np.ascontiguousarray(table.reshape(TAPS, chan_count, block_len).transpose(1, 0, 2))
    sig_tile = 32

    def frames_at(i, chan):
        lowest = (chan[0] ^ pairs[0]) // count * count
        return first + lowest, i * sig_tile, 0

    return pl.pallas_call(
        functools.partial(filter_by_pair_kernel, pairs),
        out_shape=[jax.ShapeDtypeStruct((sig_count, block_len), jnp.bfloat16)] * count,
        grid_spec=pltpu.PrefetchScalarGridSpec(
            num_scalar_prefetch=1,
            grid=(sig_count // sig_tile,),
            in_specs=[
                pl.BlockSpec(
                    (pl.Element(frames), pl.Element(sig_tile), pl.Element(block_len)), frames_at
                ),
                pl.BlockSpec((1, TAPS, block_len), lambda i, c: (c[0], 0, 0)),
            ],
            out_specs=[pl.BlockSpec((sig_tile, block_len), lambda i, c: (i, 0))] * count,
            scratch_shapes=[pltpu.VMEM((count, sig_tile, block_len), jnp.bfloat16)],
        ),
        compiler_params=pltpu.CompilerParams(vmem_limit_bytes=VMEM_LIMIT),
        name="filter_by_pair",
    )(chan_id, frames_first, jnp.asarray(table))


def cadd(a, b):
    if a is None:
        return b
    if b is None:
        return a
    return a + b


def csub(a, b):
    if b is None:
        return a
    if a is None:
        return -b
    return a - b


def scale_by(value, re, im):
    vr, vi = value
    eps = 1e-12

    def mul(x, f):
        if x is None or abs(f) < eps:
            return None
        if abs(f - 1.0) < eps:
            return x
        if abs(f + 1.0) < eps:
            return -x
        return x * f

    return csub(mul(vr, re), mul(vi, im)), cadd(mul(vr, im), mul(vi, re))


def plus(a, b):
    return cadd(a[0], b[0]), cadd(a[1], b[1])


def minus(a, b):
    return csub(a[0], b[0]), csub(a[1], b[1])


def dft(values, wanted=None):
    n = len(values)
    if n == 1:
        return list(values)
    even = dft(values[0::2])
    odd = dft(values[1::2])
    out = [None] * n
    for k in range(n // 2):
        if wanted is not None and k not in wanted and k + n // 2 not in wanted:
            continue
        angle = -2.0 * math.pi * k / n
        turned = scale_by(odd[k], math.cos(angle), math.sin(angle))
        out[k] = plus(even[k], turned)
        out[k + n // 2] = minus(even[k], turned)
    return out


def first_index_list():
    chosen = []
    for c in range(5):
        for e in range(8):
            k1 = c + 8 * e
            if c in (0, 4) and k1 > RADIX // 2:
                continue
            chosen.append(k1)
    return chosen


def turn_tables(fft_len):
    k1 = np.array(first_index_list())[:, None]
    angle = 2.0 * np.pi * ((k1 * np.arange(LANES)[None, :]) % fft_len) / fft_len
    return np.cos(angle), np.sin(angle)


def wave_matrix(fft_len):
    gain = 1.0 / (64.0 * math.sqrt(fft_len))
    half = LANES // 2
    n2 = np.arange(LANES)[None, :]
    k2 = np.arange(half)[:, None]
    rows = []
    for index, flip in ((k2, 1.0), (LANES - 1 - k2, -1.0)):
        angle = 2.0 * np.pi * ((index * n2) % LANES) / LANES
        cos, sin = np.cos(angle) * gain, np.sin(angle) * gain
        rows.append(np.concatenate([cos, sin], axis=1))
        rows.append(np.concatenate([-sin, cos], axis=1) * flip)
    return np.concatenate(rows, axis=0)


def split_two(value):
    high = value.astype(jnp.bfloat16)
    return high, (value - high.astype(jnp.float32)).astype(jnp.bfloat16)


def transform_kernel(
    chan_count, joined, in_ref, cos_ref, sin_ref, wave_high_ref, wave_low_ref, out_ref, mid_ref, high_ref, low_ref
):
    _, rows, block_len = in_ref.shape
    per_block = block_len // LANES
    tile = 16
    chosen = first_index_list()

    def row_tile(step, carry):
        at = pl.ds(pl.multiple_of(step * tile, tile), tile)
        present = set()
        for low_n in range(8):
            column = []
            for high_n in range(8):
                n1 = high_n * 8 + low_n
                lanes = slice((n1 % per_block) * LANES, (n1 % per_block + 1) * LANES)
                column.append((in_ref[n1 // per_block, at, lanes].astype(jnp.float32), None))
            spread = dft(column, wanted=range(5))
            for c in range(5):
                angle = -2.0 * math.pi * low_n * c / RADIX
                re, im = scale_by(spread[c], math.cos(angle), math.sin(angle))
                for part, value in enumerate((re, im)):
                    if value is not None:
                        mid_ref[low_n, c, part] = value
                        present.add((low_n, c, part))
        for c in range(5):
            wanted = [e for e in range(8) if c + 8 * e in chosen]
            values = []
            for low_n in range(8):
                values.append(
                    tuple(
                        mid_ref[low_n, c, part] if (low_n, c, part) in present else None
                        for part in range(2)
                    )
                )
            spread = dft(values, wanted=wanted)
            for e in wanted:
                place = chosen.index(c + 8 * e)
                cos = cos_ref[place : place + 1, :]
                sin = sin_ref[place : place + 1, :]
                re, im = spread[e]
                if im is None:
                    turned_re, turned_im = re * cos, -(re * sin)
                else:
                    turned_re, turned_im = re * cos + im * sin, im * cos - re * sin
                a, b = split_two(turned_re)
                high_ref[place, at, :LANES] = a
                low_ref[place, at, :LANES] = b
                a, b = split_two(turned_im)
                high_ref[place, at, LANES:] = a
                low_ref[place, at, LANES:] = b
        return carry

    lax.fori_loop(0, rows // tile, row_tile, 0)

    dims = (((1,), (1,)), ((), ()))
    wave_high = wave_high_ref[...]
    wave_low = wave_low_ref[...]
    quarter = LANES // 4
    group = max(2, 2 * LANES // rows)
    for first in range(0, len(chosen), group):
        places = range(first, min(first + group, len(chosen)))
        high = high_ref[first : first + len(places)].reshape(len(places) * rows, 2 * LANES)
        low = low_ref[first : first + len(places)].reshape(len(places) * rows, 2 * LANES)
        total = lax.dot_general(wave_high, high, dims, preferred_element_type=jnp.float32)
        total += lax.dot_general(wave_high, low, dims, preferred_element_type=jnp.float32)
        total += lax.dot_general(wave_low, high, dims, preferred_element_type=jnp.float32)

        def put(place, side, half, part, value):
            k1 = chosen[place]
            if side == 1 and (k1 == 0 or k1 == RADIX // 2):
                return
            index = RADIX - k1 if side else k1
            at = (index % chan_count, half, index // chan_count)
            if not joined:
                at += (part,)
            out_ref[at] = value.astype(jnp.bfloat16)

        for side in range(2):
            for half in range(2):
                row_re = side * LANES + half * quarter
                row_im = row_re + 2 * quarter
                if not joined:
                    for i, place in enumerate(places):
                        columns = slice(i * rows, (i + 1) * rows)
                        put(place, side, half, 0, total[row_re : row_re + quarter, columns])
                        put(place, side, half, 1, total[row_im : row_im + quarter, columns])
                    continue
                for i in range(0, len(places), 2):
                    columns = slice(i * rows, min((i + 2) * rows, len(places) * rows))
                    re = total[row_re : row_re + quarter, columns]
                    im = total[row_im : row_im + quarter, columns]
                    if i + 1 == len(places):
                        put(places[i], side, half, 0, jnp.concatenate([re, im], axis=1))
                        continue
                    low_lanes = lax.broadcasted_iota(jnp.int32, re.shape, 1) < rows
                    put(places[i], side, half, 0, jnp.where(low_lanes, re, pltpu.roll(im, rows, 1)))
                    put(
                        places[i + 1], side, half, 0, jnp.where(low_lanes, pltpu.roll(re, rows, 1), im)
                    )


def transform_tables(fft_len):
    cos, sin = turn_tables(fft_len)
    wave = wave_matrix(fft_len)
    wave_high = wave.astype(jnp.bfloat16)
    wave_low = (wave - wave_high.astype(np.float64)).astype(jnp.bfloat16)
    return (
        jnp.asarray(cos, jnp.float32),
        jnp.asarray(sin, jnp.float32),
        jnp.asarray(wave_high),
        jnp.asarray(wave_low),
    )


def transform_scratch(rows):
    count = len(first_index_list())
    return [
        pltpu.VMEM((8, 5, 2, 16, LANES), jnp.float32),
        pltpu.VMEM((count, rows, 2 * LANES), jnp.bfloat16),
        pltpu.VMEM((count, rows, 2 * LANES), jnp.bfloat16),
    ]


def transform(samples):
    chan_count, rows, block_len = samples.shape
    whole = pl.BlockSpec(memory_space=pltpu.VMEM)
    shape = (chan_count, 2, RADIX // chan_count, 2, LANES // 4, rows)
    return pl.pallas_call(
        functools.partial(transform_kernel, chan_count, False),
        out_shape=jax.ShapeDtypeStruct(shape, jnp.bfloat16),
        in_specs=[whole] * 5,
        out_specs=whole,
        scratch_shapes=transform_scratch(rows),
        compiler_params=pltpu.CompilerParams(vmem_limit_bytes=VMEM_LIMIT),
        name="transform",
    )(samples, *transform_tables(chan_count * block_len))


def transform_by_pair_kernel(chan_count, *refs):
    chan_ref, tables = refs[0], refs[1:5]
    in_refs, out_refs = refs[5 : 5 + chan_count], refs[5 + chan_count : 5 + 2 * chan_count]
    block_ref, result_ref, mid_ref, high_ref, low_ref, in_sem, out_sem = refs[5 + 2 * chan_count :]
    chan = chan_ref[0]
    fetches = []
    for pair, in_ref in enumerate(in_refs):
        source = chan ^ pair
        fetches.append(pltpu.make_async_copy(in_ref, block_ref.at[source], in_sem.at[pair]))
        fetches[-1].start()
    for fetch in fetches:
        fetch.wait()
    transform_kernel(
        chan_count, True, block_ref, *tables, result_ref, mid_ref, high_ref, low_ref
    )
    sends = []
    for pair, out_ref in enumerate(out_refs):
        target = chan ^ pair
        sends.append(pltpu.make_async_copy(result_ref.at[target], out_ref, out_sem.at[pair]))
        sends[-1].start()
    for send in sends:
        send.wait()


def transform_by_pair(blocks, chan_id):
    chan_count = len(blocks)
    rows, block_len = blocks[0].shape
    whole = pl.BlockSpec(memory_space=pltpu.VMEM)
    apart = pl.BlockSpec(memory_space=pltpu.HBM)
    shape = (2, RADIX // chan_count, LANES // 4, 2 * rows)
    return pl.pallas_call(
        functools.partial(transform_by_pair_kernel, chan_count),
        out_shape=[jax.ShapeDtypeStruct(shape, jnp.bfloat16)] * chan_count,
        in_specs=[pl.BlockSpec(memory_space=pltpu.SMEM)] + [whole] * 4 + [apart] * chan_count,
        out_specs=[apart] * chan_count,
        scratch_shapes=[
            pltpu.VMEM((chan_count, rows, block_len), jnp.bfloat16),
            pltpu.VMEM((chan_count,) + shape, jnp.bfloat16),
        ]
        + transform_scratch(rows)
        + [pltpu.SemaphoreType.DMA((chan_count,)), pltpu.SemaphoreType.DMA((chan_count,))],
        compiler_params=pltpu.CompilerParams(vmem_limit_bytes=VMEM_LIMIT),
        name="transform_by_pair",
    )(chan_id, *transform_tables(chan_count * block_len), *blocks)


def turn_kernel(other, group_ref, *refs):
    wide_ref = refs[-1]
    if other:
        in_refs, (across_ref, out_ref, near_ref) = refs[:-4], refs[-4:-1]
    else:
        in_refs, out_ref = refs[:-2], refs[-2]
    chan_count = len(in_refs)
    _, per, k2_count, _ = in_refs[0].shape
    pitch = per * chan_count + 1

    def spread(e, carry):
        for source, in_ref in enumerate(in_refs):
            for k2 in range(0, k2_count, EIGHT):
                value = in_ref[0, e, k2 : k2 + EIGHT, :].astype(jnp.float32)
                row = k2 * pitch + e * chan_count + source
                wide_ref[pl.ds(row, EIGHT, stride=pitch), :] = value
        return carry

    lax.fori_loop(0, per, spread, 0)

    def narrow(k2, carry):
        base = pl.multiple_of(k2 * per, per)
        for e in range(per):
            rows = pl.ds(k2 * pitch + e * chan_count, chan_count)
            out_ref[base + e] = wide_ref[rows, :].astype(jnp.bfloat16)
        return carry

    lax.fori_loop(0, k2_count, narrow, 0, unroll=4)

    if other:
        group = group_ref[0]
        same = group % 2 == group // 2

        @pl.when(same)
        def _():
            near_ref[...] = across_ref[...]

        @pl.when(jnp.logical_not(same))
        def _():
            near_ref[...] = out_ref[...]


def turn(blocks, group_id, across=None):
    chan_count = len(blocks)
    _, per, k2_count, lanes = blocks[0].shape
    one_half = (per * k2_count, chan_count, lanes)
    other = across is not None
    whole = pl.BlockSpec(one_half, lambda u, g: (0, 0, 0))

    def half_at(u, group):
        upper = group[0] // 2
        return upper if other else 1 - upper, 0, 0, 0

    results = pl.pallas_call(
        functools.partial(turn_kernel, other),
        out_shape=[jax.ShapeDtypeStruct(one_half, jnp.bfloat16)] * (1 + other),
        grid_spec=pltpu.PrefetchScalarGridSpec(
            num_scalar_prefetch=1,
            grid=(1,),
            in_specs=[pl.BlockSpec((1, per, k2_count, lanes), half_at)] * chan_count
            + [whole] * other,
            out_specs=[whole] * (1 + other),
            scratch_shapes=[pltpu.VMEM((k2_count * (per * chan_count + 1), lanes), jnp.float32)],
        ),
        compiler_params=pltpu.CompilerParams(vmem_limit_bytes=VMEM_LIMIT),
        name="turn",
    )(group_id, *blocks, *([across] if other else []))
    return results if other else results[0]


def left_kernel(chunk_count, *refs):
    out_ref = refs[-1]
    channels, _, lanes = refs[0].shape
    sig_count = lanes // 2
    width = out_ref.shape[3]
    together = 2 * lanes // width
    count = channels // out_ref.shape[1]
    row = lax.broadcasted_iota(jnp.int32, (sig_count, lanes), 0)
    column = lax.broadcasted_iota(jnp.int32, (sig_count, lanes), 1)
    identity = (row == column).astype(jnp.bfloat16)

    def some_entries(chunk_refs, step, carry):
        rows = []
        for i in range(count * together):
            values = [ref[count * together * step + i].astype(jnp.float32) for ref in chunk_refs]
            rows += values + [pltpu.roll(value, sig_count, 1) for value in values]
        stacked = jnp.concatenate(rows, axis=0).astype(jnp.bfloat16)
        turned = lax.dot_general(
            identity, stacked, (((1,), (1,)), ((), ())), preferred_element_type=jnp.float32
        )
        for i in range(together):
            out_ref[0, together * step + i] = turned[:, i * width : (i + 1) * width].astype(
                jnp.bfloat16
            )
        return carry

    for half in range((len(refs) - 1) // chunk_count):

        @pl.when(pl.program_id(0) == half)
        def _():
            chunk_refs = refs[half * chunk_count : (half + 1) * chunk_count]
            steps = channels // (count * together)
            lax.fori_loop(0, steps, functools.partial(some_entries, chunk_refs), 0, unroll=16)


def left_operand(halves):
    chunk_count = len(halves[0])
    channels, chan_count, lanes = halves[0][0].shape
    depth = 2 * chunk_count * chan_count
    count = lanes // depth
    tile = 128
    last = channels // tile - 1

    def spec(half):
        def index(u, i):
            return jnp.where(u == half, i, jnp.where(u < half, 0, last)), 0, 0

        return pl.BlockSpec((tile, chan_count, lanes), index)

    return pl.pallas_call(
        functools.partial(left_kernel, chunk_count),
        out_shape=jax.ShapeDtypeStruct(
            (len(halves), channels // count, lanes // 2, lanes), jnp.bfloat16
        ),
        grid=(len(halves), channels // tile),
        in_specs=[spec(half) for half, chunks in enumerate(halves) for _ in chunks],
        out_specs=pl.BlockSpec((1, tile // count, lanes // 2, lanes), lambda u, i: (u, i, 0, 0)),
        compiler_params=pltpu.CompilerParams(vmem_limit_bytes=VMEM_LIMIT),
        name="left_operand",
    )(*[chunk for chunks in halves for chunk in chunks])


def correlate_kernel(chunk_count, spec_count, group_ref, plan_ref, left_ref, *refs):
    del group_ref, plan_ref
    chunk_refs = refs[:chunk_count]
    out_ref, sum_ref = refs[-2:]
    _, channels, chan_count, lanes = (1,) + chunk_refs[0].shape
    sig_count = lanes // 2
    pitch = channels + 1
    sign = jnp.where(
        lax.broadcasted_iota(jnp.int32, (chan_count, lanes), 1) < sig_count, 1.0, -1.0
    ).astype(jnp.float32)

    def pairs(step, carry):
        left = left_ref[0, step]
        for i in range(2):
            pair(2 * step + i, left[:, i * sig_count : (i + 1) * sig_count])
        return carry

    def pair(step, left):
        blocks = []
        for i in range(2):
            values = [ref[2 * step + i].astype(jnp.float32) for ref in chunk_refs]
            rows = [value * sign for value in values]
            rows += [pltpu.roll(value, sig_count, 1) for value in values]
            blocks.append(jnp.concatenate(rows, axis=0).astype(jnp.bfloat16))
        zero = jnp.zeros_like(blocks[0])
        weights = jnp.concatenate(
            [
                jnp.concatenate([blocks[0], zero], axis=1),
                jnp.concatenate([zero, blocks[1]], axis=1),
            ],
            axis=0,
        )
        both = jnp.dot(left, weights, preferred_element_type=jnp.float32)
        for i in range(2):
            q = 2 * step + i
            for a in range(0, sig_count, EIGHT):
                sum_ref[pl.ds(a * pitch + q, EIGHT, stride=pitch), :] = both[
                    a : a + EIGHT, i * lanes : (i + 1) * lanes
                ]

    lax.fori_loop(0, channels // 4, pairs, 0, unroll=32)

    def finish(a, carry):
        rows = pl.ds(a * pitch, channels)
        out_ref[0, a] = (sum_ref[rows, :] * (1.0 / spec_count)).astype(jnp.bfloat16)
        return carry

    lax.fori_loop(0, sig_count, finish, 0, unroll=16)


def correlate(left, chunks, group_id, plan, distance, spec_count, so_far):
    channels, chan_count, lanes = chunks[0].shape
    per_left = channels // left.shape[1]
    sig_count, depth = left.shape[2:]
    rounds = plan.shape[0]
    tile = 128

    def half_of(group):
        if distance > 1:
            return 0
        return jnp.where(group[0] % 2 == group[0] // 2, 0, 1)

    def round_of(group, plan):
        mate = group[0] ^ distance
        found = jnp.int32(0)
        for r in range(1, rounds):
            found = jnp.where(plan[r, group[0]] == mate, r, found)
        return found

    in_specs = [
        pl.BlockSpec((1, tile // per_left, sig_count, depth), lambda i, g, p: (half_of(g), i, 0, 0)),
    ] + [pl.BlockSpec((tile, chan_count, lanes), lambda i, g, p: (i, 0, 0))] * len(chunks)
    operands = [left, *chunks]
    aliases = {}
    if so_far is not None:
        in_specs.append(pl.BlockSpec(memory_space=pl.ANY))
        operands.append(so_far)
        aliases = {len(operands) + 1: 0}
    return pl.pallas_call(
        functools.partial(correlate_kernel, len(chunks), spec_count),
        out_shape=jax.ShapeDtypeStruct((rounds, sig_count, channels, lanes), jnp.bfloat16),
        grid_spec=pltpu.PrefetchScalarGridSpec(
            num_scalar_prefetch=2,
            grid=(channels // tile,),
            in_specs=in_specs,
            out_specs=pl.BlockSpec(
                (1, sig_count, tile, lanes), lambda i, g, p: (round_of(g, p), 0, i, 0)
            ),
            scratch_shapes=[pltpu.VMEM((sig_count * (tile + 1), lanes), jnp.float32)],
        ),
        input_output_aliases=aliases,
        compiler_params=pltpu.CompilerParams(vmem_limit_bytes=VMEM_LIMIT),
        cost_estimate=pl.CostEstimate(
            flops=2 * channels * sig_count * depth * lanes,
            bytes_accessed=16 * 1024 * 1024,
            transcendentals=0,
        ),
        name="correlate",
    )(group_id, plan, *operands)


def correlate_plain(mine, theirs):
    left = mine.reshape(*mine.shape[:2], -1)
    right_re = theirs.reshape(left.shape)
    right_im = jnp.stack([-theirs[..., 1], theirs[..., 0]], axis=-1).reshape(left.shape)
    vis_re = jnp.einsum("kas,kbs->akb", left, right_re, preferred_element_type=jnp.float32)
    vis_im = jnp.einsum("kas,kbs->akb", left, right_im, preferred_element_type=jnp.float32)
    return jnp.concatenate([vis_re, vis_im], axis=-1) * (1.0 / mine.shape[2])


def by_channel(half, sig_count, spec_count):
    _, per, parts, k2, _ = half.shape
    turned = half.transpose(3, 1, 0, 4, 2).reshape(k2 * per, spec_count, sig_count, parts)
    return turned.transpose(0, 2, 1, 3)


def local_plain(voltages, plan):
    sig_count, frames, block_len = voltages.shape
    chan_count = lax.axis_size("chan")
    group_count = lax.axis_size("grp")
    spec_count = frames - TAPS + 1
    rows = spec_count * sig_count // chan_count
    chan_id = lax.axis_index("chan").astype(jnp.int32)
    group_id = lax.axis_index("grp")

    frames_first = voltages.transpose(1, 0, 2)
    filtered = filter_taps(frames_first, chan_id.reshape(1), chan_count, 0, spec_count)
    filtered = filtered.reshape(chan_count, rows, block_len)
    frames_here = lax.all_to_all(filtered, "chan", split_axis=0, concat_axis=0, tiled=True)
    spectra = transform(frames_here)
    channel = lax.all_to_all(spectra, "chan", split_axis=0, concat_axis=0, tiled=True)

    lower_half, upper_half = channel[:, 0], channel[:, 1]
    group_ids = jnp.arange(group_count)
    partner = jnp.sum(jnp.where(group_ids[None, :] == group_id, plan, 0), axis=1)
    listed = jnp.any(partner[:, None] == group_ids[None, :], axis=0)
    slot_shape = (group_count,) + (1,) * lower_half.ndim
    chosen_half = jnp.where(
        (group_ids > group_id).reshape(slot_shape), upper_half[None], lower_half[None]
    )
    slots = jnp.where(listed.reshape(slot_shape), chosen_half, jnp.zeros_like(chosen_half))
    received = lax.all_to_all(slots, "grp", split_axis=0, concat_axis=0, tiled=True)
    halves = (group_id > partner).astype(jnp.int32)
    results = []
    for round_index in range(plan.shape[0]):
        mine = lax.dynamic_index_in_dim(channel, halves[round_index], 1, keepdims=False)
        theirs = lax.dynamic_index_in_dim(received, partner[round_index], 0, keepdims=False)
        results.append(
            correlate_plain(
                by_channel(mine, sig_count, spec_count), by_channel(theirs, sig_count, spec_count)
            )
        )
    return jnp.stack(results).astype(jnp.bfloat16)


def local_overlapped(voltages, plan):
    _, frames, _ = voltages.shape
    chan_count = lax.axis_size("chan")
    group_count = lax.axis_size("grp")
    spec_count = frames - TAPS + 1
    chan_id = lax.axis_index("chan").astype(jnp.int32).reshape(1)
    group_id = lax.axis_index("grp").astype(jnp.int32).reshape(1)
    frames_first = voltages.transpose(1, 0, 2)

    def over_chan(blocks):
        moved = list(blocks)
        for pair in farthest_first(chan_count):
            moved[pair] = lax.ppermute(
                blocks[pair], "chan", [(c, c ^ pair) for c in range(chan_count)]
            )
        return moved

    def to_mate(value, distance):
        return lax.ppermute(value, "grp", [(g, g ^ distance) for g in range(group_count)])

    own, near, across, across_own = [], [], [], []
    channels = []
    chunks = spec_count // chan_count
    for chunk in range(chunks):
        if chunk:
            parts = (range(chan_count),)
        else:
            parts = (range(chan_count // 2, chan_count), range(chan_count // 2))
        blocks = [None] * chan_count
        for pairs in parts:
            blocks[pairs.start : pairs.stop] = filter_by_pair(
                frames_first, chan_id, chan_count, chunk * chan_count, pairs
            )
        blocks = over_chan(blocks)
        blocks = transform_by_pair(blocks, chan_id)
        channels.append(over_chan(blocks))
    for channel in channels:
        for_across = turn(channel, group_id)
        across.append(to_mate(for_across, 2))
        kept, for_near = turn(channel, group_id, for_across)
        near.append(to_mate(for_near, 1))
        across_own.append(for_across)
        own.append(kept)
    left = left_operand([own, across_own])
    result = correlate(left, near, group_id, plan, 1, spec_count, None)
    across, result = lax.optimization_barrier((across, result))
    relayed = [to_mate(value, 1) for value in across]
    result = correlate(left, across, group_id, plan, 2, spec_count, result)
    return correlate(left, relayed, group_id, plan, 3, spec_count, result)


def farthest_first(chan_count):
    half = chan_count // 2
    return list(range(half, chan_count)) + list(range(1, half))


def overlaps(group_count, chan_count):
    return group_count == 4 and chan_count == EIGHT


def local(voltages, plan):
    sig_count, frames, _ = voltages.shape
    chan_count = lax.axis_size("chan")
    group_count = lax.axis_size("grp")
    if (
        overlaps(group_count, chan_count)
        and plan.shape[0] == group_count - 1
        and frames - TAPS + 1 == 2 * chan_count
        and 2 * sig_count == LANES
    ):
        return local_overlapped(voltages, plan)
    return local_plain(voltages, plan)


def solution(mesh):
    in_specs = (P("grp", None, "chan"), P())
    out_specs = P(None, "grp", "chan", None)
    return jax.shard_map(local, mesh=mesh, in_specs=in_specs, out_specs=out_specs, check_vma=False)
```

```python
import functools
import math

import jax
import jax.numpy as jnp
import numpy as np
from jax import lax
from jax.experimental import pallas as pl
from jax.experimental.pallas import tpu as pltpu
from jax.sharding import PartitionSpec as P


TAPS = 16
LANES = 128
RADIX = 64
EIGHT = 8
VMEM_LIMIT = 67_000_000


def tap_table(fft_len):
    position = np.arange(TAPS * fft_len, dtype=np.float64)
    total = TAPS * fft_len
    window = 0.5 - 0.5 * np.cos(2.0 * np.pi * position / total)
    return (window * np.sinc((position - 0.5 * total) / fft_len)).reshape(TAPS, fft_len)


def filter_kernel(chan_ref, volt_ref, coeff_ref, out_ref):
    del chan_ref
    frames, sig_tile, block_len = volt_ref.shape
    spec_count = frames - TAPS + 1

    def one_tile(tile, carry):
        cols = pl.ds(pl.multiple_of(tile * LANES, LANES), LANES)
        coeff = [
            jnp.broadcast_to(coeff_ref[0, t : t + 1, cols], (EIGHT, LANES)) for t in range(TAPS)
        ]
        for low in range(0, sig_tile, EIGHT):
            rows = slice(low, low + EIGHT)
            total = [None] * spec_count
            for frame in range(frames):
                sample = volt_ref[frame, rows, cols].astype(jnp.float32)
                for s in range(max(0, frame - TAPS + 1), min(spec_count - 1, frame) + 1):
                    term = coeff[frame - s] * sample
                    total[s] = term if total[s] is None else total[s] + term
                if frame >= TAPS - 1:
                    s = frame - TAPS + 1
                    out_ref[s, rows, cols] = total[s].astype(jnp.bfloat16)
                    total[s] = None
        return carry

    lax.fori_loop(0, block_len // LANES, one_tile, 0)


def filter_taps(frames_first, chan_id, chan_count, first, spec_count):
    _, sig_count, block_len = frames_first.shape
    frames = spec_count + TAPS - 1
    table = tap_table(block_len * chan_count).astype(np.float32)
    table = np.ascontiguousarray(table.reshape(TAPS, chan_count, block_len).transpose(1, 0, 2))
    sig_tile = 32
    return pl.pallas_call(
        filter_kernel,
        out_shape=jax.ShapeDtypeStruct((spec_count, sig_count, block_len), jnp.bfloat16),
        grid_spec=pltpu.PrefetchScalarGridSpec(
            num_scalar_prefetch=1,
            grid=(sig_count // sig_tile,),
            in_specs=[
                pl.BlockSpec(
                    (pl.Element(frames), pl.Element(sig_tile), pl.Element(block_len)),
                    lambda i, c: (first, i * sig_tile, 0),
                ),
                pl.BlockSpec((1, TAPS, block_len), lambda i, c: (c[0], 0, 0)),
            ],
            out_specs=pl.BlockSpec((spec_count, sig_tile, block_len), lambda i, c: (0, i, 0)),
        ),
        compiler_params=pltpu.CompilerParams(vmem_limit_bytes=VMEM_LIMIT),
        name="filter_taps",
    )(chan_id, frames_first, jnp.asarray(table))


def filter_by_pair_kernel(pairs, chan_ref, volt_ref, coeff_ref, *refs):
    out_refs, block_ref = refs[:-1], refs[-1]
    filter_kernel(chan_ref, volt_ref, coeff_ref, block_ref)
    for pair, out_ref in zip(pairs, out_refs):
        out_ref[...] = block_ref[(chan_ref[0] ^ pair) % len(pairs)]


def filter_by_pair(frames_first, chan_id, chan_count, first, pairs):
    _, sig_count, block_len = frames_first.shape
    count = len(pairs)
    frames = count + TAPS - 1
    table = tap_table(block_len * chan_count).astype(np.float32)
    table = np.ascontiguousarray(table.reshape(TAPS, chan_count, block_len).transpose(1, 0, 2))
    sig_tile = 32

    def frames_at(i, chan):
        lowest = (chan[0] ^ pairs[0]) // count * count
        return first + lowest, i * sig_tile, 0

    return pl.pallas_call(
        functools.partial(filter_by_pair_kernel, pairs),
        out_shape=[jax.ShapeDtypeStruct((sig_count, block_len), jnp.bfloat16)] * count,
        grid_spec=pltpu.PrefetchScalarGridSpec(
            num_scalar_prefetch=1,
            grid=(sig_count // sig_tile,),
            in_specs=[
                pl.BlockSpec(
                    (pl.Element(frames), pl.Element(sig_tile), pl.Element(block_len)), frames_at
                ),
                pl.BlockSpec((1, TAPS, block_len), lambda i, c: (c[0], 0, 0)),
            ],
            out_specs=[pl.BlockSpec((sig_tile, block_len), lambda i, c: (i, 0))] * count,
            scratch_shapes=[pltpu.VMEM((count, sig_tile, block_len), jnp.bfloat16)],
        ),
        compiler_params=pltpu.CompilerParams(vmem_limit_bytes=VMEM_LIMIT),
        name="filter_by_pair",
    )(chan_id, frames_first, jnp.asarray(table))


def cadd(a, b):
    if a is None:
        return b
    if b is None:
        return a
    return a + b


def csub(a, b):
    if b is None:
        return a
    if a is None:
        return -b
    return a - b


def scale_by(value, re, im):
    vr, vi = value
    eps = 1e-12

    def mul(x, f):
        if x is None or abs(f) < eps:
            return None
        if abs(f - 1.0) < eps:
            return x
        if abs(f + 1.0) < eps:
            return -x
        return x * f

    return csub(mul(vr, re), mul(vi, im)), cadd(mul(vr, im), mul(vi, re))


def plus(a, b):
    return cadd(a[0], b[0]), cadd(a[1], b[1])


def minus(a, b):
    return csub(a[0], b[0]), csub(a[1], b[1])


def dft(values, wanted=None):
    n = len(values)
    if n == 1:
        return list(values)
    even = dft(values[0::2])
    odd = dft(values[1::2])
    out = [None] * n
    for k in range(n // 2):
        if wanted is not None and k not in wanted and k + n // 2 not in wanted:
            continue
        angle = -2.0 * math.pi * k / n
        turned = scale_by(odd[k], math.cos(angle), math.sin(angle))
        out[k] = plus(even[k], turned)
        out[k + n // 2] = minus(even[k], turned)
    return out


def first_index_list():
    chosen = []
    for c in range(5):
        for e in range(8):
            k1 = c + 8 * e
            if c in (0, 4) and k1 > RADIX // 2:
                continue
            chosen.append(k1)
    return chosen


def turn_tables(fft_len):
    k1 = np.array(first_index_list())[:, None]
    angle = 2.0 * np.pi * ((k1 * np.arange(LANES)[None, :]) % fft_len) / fft_len
    return np.cos(angle), np.sin(angle)


def wave_matrix(fft_len):
    gain = 1.0 / (64.0 * math.sqrt(fft_len))
    half = LANES // 2
    n2 = np.arange(LANES)[None, :]
    k2 = np.arange(half)[:, None]
    rows = []
    for index, flip in ((k2, 1.0), (LANES - 1 - k2, -1.0)):
        angle = 2.0 * np.pi * ((index * n2) % LANES) / LANES
        cos, sin = np.cos(angle) * gain, np.sin(angle) * gain
        rows.append(np.concatenate([cos, sin], axis=1))
        rows.append(np.concatenate([-sin, cos], axis=1) * flip)
    return np.concatenate(rows, axis=0)


def split_two(value):
    high = value.astype(jnp.bfloat16)
    return high, (value - high.astype(jnp.float32)).astype(jnp.bfloat16)


def transform_kernel(
    chan_count, joined, in_ref, cos_ref, sin_ref, wave_high_ref, wave_low_ref, out_ref, mid_ref, high_ref, low_ref
):
    _, rows, block_len = in_ref.shape
    per_block = block_len // LANES
    tile = 16
    chosen = first_index_list()

    def row_tile(step, carry):
        at = pl.ds(pl.multiple_of(step * tile, tile), tile)
        present = set()
        for low_n in range(8):
            column = []
            for high_n in range(8):
                n1 = high_n * 8 + low_n
                lanes = slice((n1 % per_block) * LANES, (n1 % per_block + 1) * LANES)
                column.append((in_ref[n1 // per_block, at, lanes].astype(jnp.float32), None))
            spread = dft(column, wanted=range(5))
            for c in range(5):
                angle = -2.0 * math.pi * low_n * c / RADIX
                re, im = scale_by(spread[c], math.cos(angle), math.sin(angle))
                for part, value in enumerate((re, im)):
                    if value is not None:
                        mid_ref[low_n, c, part] = value
                        present.add((low_n, c, part))
        for c in range(5):
            wanted = [e for e in range(8) if c + 8 * e in chosen]
            values = []
            for low_n in range(8):
                values.append(
                    tuple(
                        mid_ref[low_n, c, part] if (low_n, c, part) in present else None
                        for part in range(2)
                    )
                )
            spread = dft(values, wanted=wanted)
            for e in wanted:
                place = chosen.index(c + 8 * e)
                cos = cos_ref[place : place + 1, :]
                sin = sin_ref[place : place + 1, :]
                re, im = spread[e]
                if im is None:
                    turned_re, turned_im = re * cos, -(re * sin)
                else:
                    turned_re, turned_im = re * cos + im * sin, im * cos - re * sin
                a, b = split_two(turned_re)
                high_ref[place, at, :LANES] = a
                low_ref[place, at, :LANES] = b
                a, b = split_two(turned_im)
                high_ref[place, at, LANES:] = a
                low_ref[place, at, LANES:] = b
        return carry

    lax.fori_loop(0, rows // tile, row_tile, 0)

    dims = (((1,), (1,)), ((), ()))
    wave_high = wave_high_ref[...]
    wave_low = wave_low_ref[...]
    quarter = LANES // 4
    group = max(2, 2 * LANES // rows)
    for first in range(0, len(chosen), group):
        places = range(first, min(first + group, len(chosen)))
        high = high_ref[first : first + len(places)].reshape(len(places) * rows, 2 * LANES)
        low = low_ref[first : first + len(places)].reshape(len(places) * rows, 2 * LANES)
        total = lax.dot_general(
            jnp.concatenate([wave_high, wave_high, wave_low], axis=1),
            jnp.concatenate([high, low, high], axis=1),
            dims,
            preferred_element_type=jnp.float32,
        )

        def put(place, side, half, part, value):
            k1 = chosen[place]
            if side == 1 and (k1 == 0 or k1 == RADIX // 2):
                return
            index = RADIX - k1 if side else k1
            at = (index % chan_count, half, index // chan_count)
            if not joined:
                at += (part,)
            out_ref[at] = value.astype(jnp.bfloat16)

        for side in range(2):
            for half in range(2):
                row_re = side * LANES + half * quarter
                row_im = row_re + 2 * quarter
                if not joined:
                    for i, place in enumerate(places):
                        columns = slice(i * rows, (i + 1) * rows)
                        put(place, side, half, 0, total[row_re : row_re + quarter, columns])
                        put(place, side, half, 1, total[row_im : row_im + quarter, columns])
                    continue
                for i in range(0, len(places), 2):
                    columns = slice(i * rows, min((i + 2) * rows, len(places) * rows))
                    re = total[row_re : row_re + quarter, columns]
                    im = total[row_im : row_im + quarter, columns]
                    if i + 1 == len(places):
                        put(places[i], side, half, 0, jnp.concatenate([re, im], axis=1))
                        continue
                    low_lanes = lax.broadcasted_iota(jnp.int32, re.shape, 1) < rows
                    put(places[i], side, half, 0, jnp.where(low_lanes, re, pltpu.roll(im, rows, 1)))
                    put(
                        places[i + 1], side, half, 0, jnp.where(low_lanes, pltpu.roll(re, rows, 1), im)
                    )


def transform_tables(fft_len):
    cos, sin = turn_tables(fft_len)
    wave = wave_matrix(fft_len)
    wave_high = wave.astype(jnp.bfloat16)
    wave_low = (wave - wave_high.astype(np.float64)).astype(jnp.bfloat16)
    return (
        jnp.asarray(cos, jnp.float32),
        jnp.asarray(sin, jnp.float32),
        jnp.asarray(wave_high),
        jnp.asarray(wave_low),
    )


def transform_scratch(rows):
    count = len(first_index_list())
    return [
        pltpu.VMEM((8, 5, 2, 16, LANES), jnp.float32),
        pltpu.VMEM((count, rows, 2 * LANES), jnp.bfloat16),
        pltpu.VMEM((count, rows, 2 * LANES), jnp.bfloat16),
    ]


def transform(samples):
    chan_count, rows, block_len = samples.shape
    whole = pl.BlockSpec(memory_space=pltpu.VMEM)
    shape = (chan_count, 2, RADIX // chan_count, 2, LANES // 4, rows)
    return pl.pallas_call(
        functools.partial(transform_kernel, chan_count, False),
        out_shape=jax.ShapeDtypeStruct(shape, jnp.bfloat16),
        in_specs=[whole] * 5,
        out_specs=whole,
        scratch_shapes=transform_scratch(rows),
        compiler_params=pltpu.CompilerParams(vmem_limit_bytes=VMEM_LIMIT),
        name="transform",
    )(samples, *transform_tables(chan_count * block_len))


def transform_by_pair_kernel(chan_count, *refs):
    chan_ref, tables = refs[0], refs[1:5]
    in_refs, out_refs = refs[5 : 5 + chan_count], refs[5 + chan_count : 5 + 2 * chan_count]
    block_ref, result_ref, mid_ref, high_ref, low_ref, in_sem, out_sem = refs[5 + 2 * chan_count :]
    chan = chan_ref[0]
    fetches = []
    for pair, in_ref in enumerate(in_refs):
        source = chan ^ pair
        fetches.append(pltpu.make_async_copy(in_ref, block_ref.at[source], in_sem.at[pair]))
        fetches[-1].start()
    for fetch in fetches:
        fetch.wait()
    transform_kernel(
        chan_count, True, block_ref, *tables, result_ref, mid_ref, high_ref, low_ref
    )
    sends = []
    for pair, out_ref in enumerate(out_refs):
        target = chan ^ pair
        sends.append(pltpu.make_async_copy(result_ref.at[target], out_ref, out_sem.at[pair]))
        sends[-1].start()
    for send in sends:
        send.wait()


def transform_by_pair(blocks, chan_id):
    chan_count = len(blocks)
    rows, block_len = blocks[0].shape
    whole = pl.BlockSpec(memory_space=pltpu.VMEM)
    apart = pl.BlockSpec(memory_space=pltpu.HBM)
    shape = (2, RADIX // chan_count, LANES // 4, 2 * rows)
    return pl.pallas_call(
        functools.partial(transform_by_pair_kernel, chan_count),
        out_shape=[jax.ShapeDtypeStruct(shape, jnp.bfloat16)] * chan_count,
        in_specs=[pl.BlockSpec(memory_space=pltpu.SMEM)] + [whole] * 4 + [apart] * chan_count,
        out_specs=[apart] * chan_count,
        scratch_shapes=[
            pltpu.VMEM((chan_count, rows, block_len), jnp.bfloat16),
            pltpu.VMEM((chan_count,) + shape, jnp.bfloat16),
        ]
        + transform_scratch(rows)
        + [pltpu.SemaphoreType.DMA((chan_count,)), pltpu.SemaphoreType.DMA((chan_count,))],
        compiler_params=pltpu.CompilerParams(vmem_limit_bytes=VMEM_LIMIT),
        name="transform_by_pair",
    )(chan_id, *transform_tables(chan_count * block_len), *blocks)


def turn_kernel(other, group_ref, *refs):
    wide_ref = refs[-1]
    if other:
        in_refs, (across_ref, out_ref, near_ref) = refs[:-4], refs[-4:-1]
    else:
        in_refs, out_ref = refs[:-2], refs[-2]
    chan_count = len(in_refs)
    _, per, k2_count, _ = in_refs[0].shape
    pitch = per * chan_count + 1

    def spread(e, carry):
        for source, in_ref in enumerate(in_refs):
            for k2 in range(0, k2_count, EIGHT):
                value = in_ref[0, e, k2 : k2 + EIGHT, :].astype(jnp.float32)
                row = k2 * pitch + e * chan_count + source
                wide_ref[pl.ds(row, EIGHT, stride=pitch), :] = value
        return carry

    lax.fori_loop(0, per, spread, 0)

    def narrow(k2, carry):
        base = pl.multiple_of(k2 * per, per)
        for e in range(per):
            rows = pl.ds(k2 * pitch + e * chan_count, chan_count)
            out_ref[base + e] = wide_ref[rows, :].astype(jnp.bfloat16)
        return carry

    lax.fori_loop(0, k2_count, narrow, 0, unroll=4)

    if other:
        group = group_ref[0]
        same = group % 2 == group // 2

        @pl.when(same)
        def _():
            near_ref[...] = across_ref[...]

        @pl.when(jnp.logical_not(same))
        def _():
            near_ref[...] = out_ref[...]


def turn(blocks, group_id, across=None):
    chan_count = len(blocks)
    _, per, k2_count, lanes = blocks[0].shape
    one_half = (per * k2_count, chan_count, lanes)
    other = across is not None
    whole = pl.BlockSpec(one_half, lambda u, g: (0, 0, 0))

    def half_at(u, group):
        upper = group[0] // 2
        return upper if other else 1 - upper, 0, 0, 0

    results = pl.pallas_call(
        functools.partial(turn_kernel, other),
        out_shape=[jax.ShapeDtypeStruct(one_half, jnp.bfloat16)] * (1 + other),
        grid_spec=pltpu.PrefetchScalarGridSpec(
            num_scalar_prefetch=1,
            grid=(1,),
            in_specs=[pl.BlockSpec((1, per, k2_count, lanes), half_at)] * chan_count
            + [whole] * other,
            out_specs=[whole] * (1 + other),
            scratch_shapes=[pltpu.VMEM((k2_count * (per * chan_count + 1), lanes), jnp.float32)],
        ),
        compiler_params=pltpu.CompilerParams(vmem_limit_bytes=VMEM_LIMIT),
        name="turn",
    )(group_id, *blocks, *([across] if other else []))
    return results if other else results[0]


def left_kernel(chunk_count, *refs):
    out_ref = refs[-1]
    channels, _, lanes = refs[0].shape
    sig_count = lanes // 2
    width = out_ref.shape[3]
    together = 2 * lanes // width
    count = channels // out_ref.shape[1]
    row = lax.broadcasted_iota(jnp.int32, (sig_count, lanes), 0)
    column = lax.broadcasted_iota(jnp.int32, (sig_count, lanes), 1)
    identity = (row == column).astype(jnp.bfloat16)

    def some_entries(chunk_refs, step, carry):
        rows = []
        for i in range(count * together):
            values = [ref[count * together * step + i].astype(jnp.float32) for ref in chunk_refs]
            rows += values + [pltpu.roll(value, sig_count, 1) for value in values]
        stacked = jnp.concatenate(rows, axis=0).astype(jnp.bfloat16)
        turned = lax.dot_general(
            identity, stacked, (((1,), (1,)), ((), ())), preferred_element_type=jnp.float32
        )
        for i in range(together):
            out_ref[0, together * step + i] = turned[:, i * width : (i + 1) * width].astype(
                jnp.bfloat16
            )
        return carry

    for half in range((len(refs) - 1) // chunk_count):

        @pl.when(pl.program_id(0) == half)
        def _():
            chunk_refs = refs[half * chunk_count : (half + 1) * chunk_count]
            steps = channels // (count * together)
            lax.fori_loop(0, steps, functools.partial(some_entries, chunk_refs), 0, unroll=16)


def left_operand(halves):
    chunk_count = len(halves[0])
    channels, chan_count, lanes = halves[0][0].shape
    depth = 2 * chunk_count * chan_count
    count = lanes // depth
    tile = 128
    last = channels // tile - 1

    def spec(half):
        def index(u, i):
            return jnp.where(u == half, i, jnp.where(u < half, 0, last)), 0, 0

        return pl.BlockSpec((tile, chan_count, lanes), index)

    return pl.pallas_call(
        functools.partial(left_kernel, chunk_count),
        out_shape=jax.ShapeDtypeStruct(
            (len(halves), channels // count, lanes // 2, lanes), jnp.bfloat16
        ),
        grid=(len(halves), channels // tile),
        in_specs=[spec(half) for half, chunks in enumerate(halves) for _ in chunks],
        out_specs=pl.BlockSpec((1, tile // count, lanes // 2, lanes), lambda u, i: (u, i, 0, 0)),
        compiler_params=pltpu.CompilerParams(vmem_limit_bytes=VMEM_LIMIT),
        name="left_operand",
    )(*[chunk for chunks in halves for chunk in chunks])


def correlate_kernel(chunk_count, spec_count, group_ref, plan_ref, left_ref, *refs):
    del group_ref, plan_ref
    chunk_refs = refs[:chunk_count]
    out_ref, sum_ref = refs[-2:]
    _, channels, chan_count, lanes = (1,) + chunk_refs[0].shape
    sig_count = lanes // 2
    pitch = channels + 1
    sign = jnp.where(
        lax.broadcasted_iota(jnp.int32, (chan_count, lanes), 1) < sig_count, 1.0, -1.0
    ).astype(jnp.float32)

    def pairs(step, carry):
        left = left_ref[0, step]
        for i in range(2):
            pair(2 * step + i, left[:, i * sig_count : (i + 1) * sig_count])
        return carry

    def pair(step, left):
        blocks = []
        for i in range(2):
            values = [ref[2 * step + i].astype(jnp.float32) for ref in chunk_refs]
            rows = [value * sign for value in values]
            rows += [pltpu.roll(value, sig_count, 1) for value in values]
            blocks.append(jnp.concatenate(rows, axis=0).astype(jnp.bfloat16))
        zero = jnp.zeros_like(blocks[0])
        weights = jnp.concatenate(
            [
                jnp.concatenate([blocks[0], zero], axis=1),
                jnp.concatenate([zero, blocks[1]], axis=1),
            ],
            axis=0,
        )
        both = jnp.dot(left, weights, preferred_element_type=jnp.float32)
        for i in range(2):
            q = 2 * step + i
            for a in range(0, sig_count, EIGHT):
                sum_ref[pl.ds(a * pitch + q, EIGHT, stride=pitch), :] = both[
                    a : a + EIGHT, i * lanes : (i + 1) * lanes
                ]

    lax.fori_loop(0, channels // 4, pairs, 0, unroll=32)

    def finish(a, carry):
        rows = pl.ds(a * pitch, channels)
        out_ref[0, a] = (sum_ref[rows, :] * (1.0 / spec_count)).astype(jnp.bfloat16)
        return carry

    lax.fori_loop(0, sig_count, finish, 0, unroll=16)


def correlate(left, chunks, group_id, plan, distance, spec_count, so_far):
    channels, chan_count, lanes = chunks[0].shape
    per_left = channels // left.shape[1]
    sig_count, depth = left.shape[2:]
    rounds = plan.shape[0]
    tile = 128

    def half_of(group):
        if distance > 1:
            return 0
        return jnp.where(group[0] % 2 == group[0] // 2, 0, 1)

    def round_of(group, plan):
        mate = group[0] ^ distance
        found = jnp.int32(0)
        for r in range(1, rounds):
            found = jnp.where(plan[r, group[0]] == mate, r, found)
        return found

    in_specs = [
        pl.BlockSpec((1, tile // per_left, sig_count, depth), lambda i, g, p: (half_of(g), i, 0, 0)),
    ] + [pl.BlockSpec((tile, chan_count, lanes), lambda i, g, p: (i, 0, 0))] * len(chunks)
    operands = [left, *chunks]
    aliases = {}
    if so_far is not None:
        in_specs.append(pl.BlockSpec(memory_space=pl.ANY))
        operands.append(so_far)
        aliases = {len(operands) + 1: 0}
    return pl.pallas_call(
        functools.partial(correlate_kernel, len(chunks), spec_count),
        out_shape=jax.ShapeDtypeStruct((rounds, sig_count, channels, lanes), jnp.bfloat16),
        grid_spec=pltpu.PrefetchScalarGridSpec(
            num_scalar_prefetch=2,
            grid=(channels // tile,),
            in_specs=in_specs,
            out_specs=pl.BlockSpec(
                (1, sig_count, tile, lanes), lambda i, g, p: (round_of(g, p), 0, i, 0)
            ),
            scratch_shapes=[pltpu.VMEM((sig_count * (tile + 1), lanes), jnp.float32)],
        ),
        input_output_aliases=aliases,
        compiler_params=pltpu.CompilerParams(vmem_limit_bytes=VMEM_LIMIT),
        cost_estimate=pl.CostEstimate(
            flops=2 * channels * sig_count * depth * lanes,
            bytes_accessed=16 * 1024 * 1024,
            transcendentals=0,
        ),
        name="correlate",
    )(group_id, plan, *operands)


def correlate_plain(mine, theirs):
    left = mine.reshape(*mine.shape[:2], -1)
    right_re = theirs.reshape(left.shape)
    right_im = jnp.stack([-theirs[..., 1], theirs[..., 0]], axis=-1).reshape(left.shape)
    vis_re = jnp.einsum("kas,kbs->akb", left, right_re, preferred_element_type=jnp.float32)
    vis_im = jnp.einsum("kas,kbs->akb", left, right_im, preferred_element_type=jnp.float32)
    return jnp.concatenate([vis_re, vis_im], axis=-1) * (1.0 / mine.shape[2])


def by_channel(half, sig_count, spec_count):
    _, per, parts, k2, _ = half.shape
    turned = half.transpose(3, 1, 0, 4, 2).reshape(k2 * per, spec_count, sig_count, parts)
    return turned.transpose(0, 2, 1, 3)


def local_plain(voltages, plan):
    sig_count, frames, block_len = voltages.shape
    chan_count = lax.axis_size("chan")
    group_count = lax.axis_size("grp")
    spec_count = frames - TAPS + 1
    rows = spec_count * sig_count // chan_count
    chan_id = lax.axis_index("chan").astype(jnp.int32)
    group_id = lax.axis_index("grp")

    frames_first = voltages.transpose(1, 0, 2)
    filtered = filter_taps(frames_first, chan_id.reshape(1), chan_count, 0, spec_count)
    filtered = filtered.reshape(chan_count, rows, block_len)
    frames_here = lax.all_to_all(filtered, "chan", split_axis=0, concat_axis=0, tiled=True)
    spectra = transform(frames_here)
    channel = lax.all_to_all(spectra, "chan", split_axis=0, concat_axis=0, tiled=True)

    lower_half, upper_half = channel[:, 0], channel[:, 1]
    group_ids = jnp.arange(group_count)
    partner = jnp.sum(jnp.where(group_ids[None, :] == group_id, plan, 0), axis=1)
    listed = jnp.any(partner[:, None] == group_ids[None, :], axis=0)
    slot_shape = (group_count,) + (1,) * lower_half.ndim
    chosen_half = jnp.where(
        (group_ids > group_id).reshape(slot_shape), upper_half[None], lower_half[None]
    )
    slots = jnp.where(listed.reshape(slot_shape), chosen_half, jnp.zeros_like(chosen_half))
    received = lax.all_to_all(slots, "grp", split_axis=0, concat_axis=0, tiled=True)
    halves = (group_id > partner).astype(jnp.int32)
    results = []
    for round_index in range(plan.shape[0]):
        mine = lax.dynamic_index_in_dim(channel, halves[round_index], 1, keepdims=False)
        theirs = lax.dynamic_index_in_dim(received, partner[round_index], 0, keepdims=False)
        results.append(
            correlate_plain(
                by_channel(mine, sig_count, spec_count), by_channel(theirs, sig_count, spec_count)
            )
        )
    return jnp.stack(results).astype(jnp.bfloat16)


def local_overlapped(voltages, plan):
    _, frames, _ = voltages.shape
    chan_count = lax.axis_size("chan")
    group_count = lax.axis_size("grp")
    spec_count = frames - TAPS + 1
    chan_id = lax.axis_index("chan").astype(jnp.int32).reshape(1)
    group_id = lax.axis_index("grp").astype(jnp.int32).reshape(1)
    frames_first = voltages.transpose(1, 0, 2)

    def over_chan(blocks):
        moved = list(blocks)
        for pair in farthest_first(chan_count):
            moved[pair] = lax.ppermute(
                blocks[pair], "chan", [(c, c ^ pair) for c in range(chan_count)]
            )
        return moved

    def to_mate(value, distance):
        return lax.ppermute(value, "grp", [(g, g ^ distance) for g in range(group_count)])

    own, near, across, across_own = [], [], [], []
    channels = []
    chunks = spec_count // chan_count
    for chunk in range(chunks):
        if chunk:
            parts = (range(chan_count),)
        else:
            parts = (range(chan_count // 2, chan_count), range(chan_count // 2))
        blocks = [None] * chan_count
        for pairs in parts:
            blocks[pairs.start : pairs.stop] = filter_by_pair(
                frames_first, chan_id, chan_count, chunk * chan_count, pairs
            )
        blocks = over_chan(blocks)
        blocks = transform_by_pair(blocks, chan_id)
        channels.append(over_chan(blocks))
    for channel in channels:
        for_across = turn(channel, group_id)
        across.append(to_mate(for_across, 2))
        kept, for_near = turn(channel, group_id, for_across)
        near.append(to_mate(for_near, 1))
        across_own.append(for_across)
        own.append(kept)
    left = left_operand([own, across_own])
    result = correlate(left, near, group_id, plan, 1, spec_count, None)
    across, result = lax.optimization_barrier((across, result))
    relayed = [to_mate(value, 1) for value in across]
    result = correlate(left, across, group_id, plan, 2, spec_count, result)
    return correlate(left, relayed, group_id, plan, 3, spec_count, result)


def farthest_first(chan_count):
    half = chan_count // 2
    return list(range(half, chan_count)) + list(range(1, half))


def overlaps(group_count, chan_count):
    return group_count == 4 and chan_count == EIGHT


def local(voltages, plan):
    sig_count, frames, _ = voltages.shape
    chan_count = lax.axis_size("chan")
    group_count = lax.axis_size("grp")
    if (
        overlaps(group_count, chan_count)
        and plan.shape[0] == group_count - 1
        and frames - TAPS + 1 == 2 * chan_count
        and 2 * sig_count == LANES
    ):
        return local_overlapped(voltages, plan)
    return local_plain(voltages, plan)


def solution(mesh):
    in_specs = (P("grp", None, "chan"), P())
    out_specs = P(None, "grp", "chan", None)
    return jax.shard_map(local, mesh=mesh, in_specs=in_specs, out_specs=out_specs, check_vma=False)
```

```python
import functools
import math

import jax
import jax.numpy as jnp
import numpy as np
from jax import lax
from jax.experimental import pallas as pl
from jax.experimental.pallas import tpu as pltpu
from jax.sharding import PartitionSpec as P


TAPS = 16
LANES = 128
RADIX = 64
EIGHT = 8
VMEM_LIMIT = 67_000_000


def tap_table(fft_len):
    position = np.arange(TAPS * fft_len, dtype=np.float64)
    total = TAPS * fft_len
    window = 0.5 - 0.5 * np.cos(2.0 * np.pi * position / total)
    return (window * np.sinc((position - 0.5 * total) / fft_len)).reshape(TAPS, fft_len)


def filter_kernel(chan_ref, volt_ref, coeff_ref, out_ref):
    del chan_ref
    frames, sig_tile, block_len = volt_ref.shape
    spec_count = frames - TAPS + 1

    def one_tile(tile, carry):
        cols = pl.ds(pl.multiple_of(tile * LANES, LANES), LANES)
        coeff = [
            jnp.broadcast_to(coeff_ref[0, t : t + 1, cols], (EIGHT, LANES)) for t in range(TAPS)
        ]
        for low in range(0, sig_tile, EIGHT):
            rows = slice(low, low + EIGHT)
            total = [None] * spec_count
            for frame in range(frames):
                sample = volt_ref[frame, rows, cols].astype(jnp.float32)
                for s in range(max(0, frame - TAPS + 1), min(spec_count - 1, frame) + 1):
                    term = coeff[frame - s] * sample
                    total[s] = term if total[s] is None else total[s] + term
                if frame >= TAPS - 1:
                    s = frame - TAPS + 1
                    out_ref[s, rows, cols] = total[s].astype(jnp.bfloat16)
                    total[s] = None
        return carry

    lax.fori_loop(0, block_len // LANES, one_tile, 0)


def filter_taps(frames_first, chan_id, chan_count, first, spec_count):
    _, sig_count, block_len = frames_first.shape
    frames = spec_count + TAPS - 1
    table = tap_table(block_len * chan_count).astype(np.float32)
    table = np.ascontiguousarray(table.reshape(TAPS, chan_count, block_len).transpose(1, 0, 2))
    sig_tile = 32
    return pl.pallas_call(
        filter_kernel,
        out_shape=jax.ShapeDtypeStruct((spec_count, sig_count, block_len), jnp.bfloat16),
        grid_spec=pltpu.PrefetchScalarGridSpec(
            num_scalar_prefetch=1,
            grid=(sig_count // sig_tile,),
            in_specs=[
                pl.BlockSpec(
                    (pl.Element(frames), pl.Element(sig_tile), pl.Element(block_len)),
                    lambda i, c: (first, i * sig_tile, 0),
                ),
                pl.BlockSpec((1, TAPS, block_len), lambda i, c: (c[0], 0, 0)),
            ],
            out_specs=pl.BlockSpec((spec_count, sig_tile, block_len), lambda i, c: (0, i, 0)),
        ),
        compiler_params=pltpu.CompilerParams(vmem_limit_bytes=VMEM_LIMIT),
        name="filter_taps",
    )(chan_id, frames_first, jnp.asarray(table))


def filter_by_pair_kernel(pairs, chan_ref, volt_ref, coeff_ref, *refs):
    out_refs, block_ref = refs[:-1], refs[-1]
    filter_kernel(chan_ref, volt_ref, coeff_ref, block_ref)
    for pair, out_ref in zip(pairs, out_refs):
        out_ref[...] = block_ref[(chan_ref[0] ^ pair) % len(pairs)]


def filter_by_pair(frames_first, chan_id, chan_count, first, pairs):
    _, sig_count, block_len = frames_first.shape
    count = len(pairs)
    frames = count + TAPS - 1
    table = tap_table(block_len * chan_count).astype(np.float32)
    table = np.ascontiguousarray(table.reshape(TAPS, chan_count, block_len).transpose(1, 0, 2))
    sig_tile = 32

    def frames_at(i, chan):
        lowest = (chan[0] ^ pairs[0]) // count * count
        return first + lowest, i * sig_tile, 0

    return pl.pallas_call(
        functools.partial(filter_by_pair_kernel, pairs),
        out_shape=[jax.ShapeDtypeStruct((sig_count, block_len), jnp.bfloat16)] * count,
        grid_spec=pltpu.PrefetchScalarGridSpec(
            num_scalar_prefetch=1,
            grid=(sig_count // sig_tile,),
            in_specs=[
                pl.BlockSpec(
                    (pl.Element(frames), pl.Element(sig_tile), pl.Element(block_len)), frames_at
                ),
                pl.BlockSpec((1, TAPS, block_len), lambda i, c: (c[0], 0, 0)),
            ],
            out_specs=[pl.BlockSpec((sig_tile, block_len), lambda i, c: (i, 0))] * count,
            scratch_shapes=[pltpu.VMEM((count, sig_tile, block_len), jnp.bfloat16)],
        ),
        compiler_params=pltpu.CompilerParams(vmem_limit_bytes=VMEM_LIMIT),
        name="filter_by_pair",
    )(chan_id, frames_first, jnp.asarray(table))


def cadd(a, b):
    if a is None:
        return b
    if b is None:
        return a
    return a + b


def csub(a, b):
    if b is None:
        return a
    if a is None:
        return -b
    return a - b


def scale_by(value, re, im):
    vr, vi = value
    eps = 1e-12

    def mul(x, f):
        if x is None or abs(f) < eps:
            return None
        if abs(f - 1.0) < eps:
            return x
        if abs(f + 1.0) < eps:
            return -x
        return x * f

    return csub(mul(vr, re), mul(vi, im)), cadd(mul(vr, im), mul(vi, re))


def plus(a, b):
    return cadd(a[0], b[0]), cadd(a[1], b[1])


def minus(a, b):
    return csub(a[0], b[0]), csub(a[1], b[1])


def dft(values, wanted=None):
    n = len(values)
    if n == 1:
        return list(values)
    even = dft(values[0::2])
    odd = dft(values[1::2])
    out = [None] * n
    for k in range(n // 2):
        if wanted is not None and k not in wanted and k + n // 2 not in wanted:
            continue
        angle = -2.0 * math.pi * k / n
        turned = scale_by(odd[k], math.cos(angle), math.sin(angle))
        out[k] = plus(even[k], turned)
        out[k + n // 2] = minus(even[k], turned)
    return out


def first_index_list():
    chosen = []
    for c in range(5):
        for e in range(8):
            k1 = c + 8 * e
            if c in (0, 4) and k1 > RADIX // 2:
                continue
            chosen.append(k1)
    return chosen


def turn_tables(fft_len):
    k1 = np.array(first_index_list())[:, None]
    angle = 2.0 * np.pi * ((k1 * np.arange(LANES)[None, :]) % fft_len) / fft_len
    return np.cos(angle), np.sin(angle)


def wave_matrix(fft_len):
    gain = 1.0 / (64.0 * math.sqrt(fft_len))
    half = LANES // 2
    n2 = np.arange(LANES)[None, :]
    k2 = np.arange(half)[:, None]
    rows = []
    for index, flip in ((k2, 1.0), (LANES - 1 - k2, -1.0)):
        angle = 2.0 * np.pi * ((index * n2) % LANES) / LANES
        cos, sin = np.cos(angle) * gain, np.sin(angle) * gain
        rows.append(np.concatenate([cos, sin], axis=1))
        rows.append(np.concatenate([-sin, cos], axis=1) * flip)
    return np.concatenate(rows, axis=0)


def split_two(value):
    high = value.astype(jnp.bfloat16)
    return high, (value - high.astype(jnp.float32)).astype(jnp.bfloat16)


def transform_kernel(
    chan_count, joined, in_ref, cos_ref, sin_ref, wave_high_ref, wave_low_ref, out_ref, mid_ref, high_ref, low_ref
):
    _, rows, block_len = in_ref.shape
    per_block = block_len // LANES
    tile = 16
    chosen = first_index_list()

    def row_tile(step, carry):
        at = pl.ds(pl.multiple_of(step * tile, tile), tile)
        present = set()
        for low_n in range(8):
            column = []
            for high_n in range(8):
                n1 = high_n * 8 + low_n
                lanes = slice((n1 % per_block) * LANES, (n1 % per_block + 1) * LANES)
                column.append((in_ref[n1 // per_block, at, lanes].astype(jnp.float32), None))
            spread = dft(column, wanted=range(5))
            for c in range(5):
                angle = -2.0 * math.pi * low_n * c / RADIX
                re, im = scale_by(spread[c], math.cos(angle), math.sin(angle))
                for part, value in enumerate((re, im)):
                    if value is not None:
                        mid_ref[low_n, c, part] = value
                        present.add((low_n, c, part))
        for c in range(5):
            wanted = [e for e in range(8) if c + 8 * e in chosen]
            values = []
            for low_n in range(8):
                values.append(
                    tuple(
                        mid_ref[low_n, c, part] if (low_n, c, part) in present else None
                        for part in range(2)
                    )
                )
            spread = dft(values, wanted=wanted)
            for e in wanted:
                place = chosen.index(c + 8 * e)
                cos = cos_ref[place : place + 1, :]
                sin = sin_ref[place : place + 1, :]
                re, im = spread[e]
                if im is None:
                    turned_re, turned_im = re * cos, -(re * sin)
                else:
                    turned_re, turned_im = re * cos + im * sin, im * cos - re * sin
                a, b = split_two(turned_re)
                high_ref[place, at, :LANES] = a
                low_ref[place, at, :LANES] = b
                a, b = split_two(turned_im)
                high_ref[place, at, LANES:] = a
                low_ref[place, at, LANES:] = b
        return carry

    lax.fori_loop(0, rows // tile, row_tile, 0)

    dims = (((1,), (1,)), ((), ()))
    wave_high = wave_high_ref[...]
    wave_low = wave_low_ref[...]
    quarter = LANES // 4
    group = max(2, 2 * LANES // rows)
    for first in range(0, len(chosen), group):
        places = range(first, min(first + group, len(chosen)))
        high = high_ref[first : first + len(places)].reshape(len(places) * rows, 2 * LANES)
        low = low_ref[first : first + len(places)].reshape(len(places) * rows, 2 * LANES)
        total = lax.dot_general(
            jnp.concatenate([wave_high, wave_high, wave_low], axis=1),
            jnp.concatenate([high, low, high], axis=1),
            dims,
            preferred_element_type=jnp.float32,
        )

        def put(place, side, half, part, value):
            k1 = chosen[place]
            if side == 1 and (k1 == 0 or k1 == RADIX // 2):
                return
            index = RADIX - k1 if side else k1
            at = (index % chan_count, half, index // chan_count)
            if not joined:
                at += (part,)
            out_ref[at] = value.astype(jnp.bfloat16)

        for side in range(2):
            for half in range(2):
                row_re = side * LANES + half * quarter
                row_im = row_re + 2 * quarter
                if not joined:
                    for i, place in enumerate(places):
                        columns = slice(i * rows, (i + 1) * rows)
                        put(place, side, half, 0, total[row_re : row_re + quarter, columns])
                        put(place, side, half, 1, total[row_im : row_im + quarter, columns])
                    continue
                for i in range(0, len(places), 2):
                    columns = slice(i * rows, min((i + 2) * rows, len(places) * rows))
                    re = total[row_re : row_re + quarter, columns]
                    im = total[row_im : row_im + quarter, columns]
                    if i + 1 == len(places):
                        put(places[i], side, half, 0, jnp.concatenate([re, im], axis=1))
                        continue
                    low_lanes = lax.broadcasted_iota(jnp.int32, re.shape, 1) < rows
                    put(places[i], side, half, 0, jnp.where(low_lanes, re, pltpu.roll(im, rows, 1)))
                    put(
                        places[i + 1], side, half, 0, jnp.where(low_lanes, pltpu.roll(re, rows, 1), im)
                    )


def transform_tables(fft_len):
    cos, sin = turn_tables(fft_len)
    wave = wave_matrix(fft_len)
    wave_high = wave.astype(jnp.bfloat16)
    wave_low = (wave - wave_high.astype(np.float64)).astype(jnp.bfloat16)
    return (
        jnp.asarray(cos, jnp.float32),
        jnp.asarray(sin, jnp.float32),
        jnp.asarray(wave_high),
        jnp.asarray(wave_low),
    )


def transform_scratch(rows):
    count = len(first_index_list())
    return [
        pltpu.VMEM((8, 5, 2, 16, LANES), jnp.float32),
        pltpu.VMEM((count, rows, 2 * LANES), jnp.bfloat16),
        pltpu.VMEM((count, rows, 2 * LANES), jnp.bfloat16),
    ]


def transform(samples):
    chan_count, rows, block_len = samples.shape
    whole = pl.BlockSpec(memory_space=pltpu.VMEM)
    shape = (chan_count, 2, RADIX // chan_count, 2, LANES // 4, rows)
    return pl.pallas_call(
        functools.partial(transform_kernel, chan_count, False),
        out_shape=jax.ShapeDtypeStruct(shape, jnp.bfloat16),
        in_specs=[whole] * 5,
        out_specs=whole,
        scratch_shapes=transform_scratch(rows),
        compiler_params=pltpu.CompilerParams(vmem_limit_bytes=VMEM_LIMIT),
        name="transform",
    )(samples, *transform_tables(chan_count * block_len))


def transform_by_pair_kernel(chan_count, *refs):
    chan_ref, tables = refs[0], refs[1:5]
    in_refs, out_refs = refs[5 : 5 + chan_count], refs[5 + chan_count : 5 + 2 * chan_count]
    block_ref, result_ref, mid_ref, high_ref, low_ref, in_sem, out_sem = refs[5 + 2 * chan_count :]
    chan = chan_ref[0]
    fetches = []
    for pair, in_ref in enumerate(in_refs):
        source = chan ^ pair
        fetches.append(pltpu.make_async_copy(in_ref, block_ref.at[source], in_sem.at[pair]))
        fetches[-1].start()
    for fetch in fetches:
        fetch.wait()
    transform_kernel(
        chan_count, True, block_ref, *tables, result_ref, mid_ref, high_ref, low_ref
    )
    sends = []
    for pair, out_ref in enumerate(out_refs):
        target = chan ^ pair
        sends.append(pltpu.make_async_copy(result_ref.at[target], out_ref, out_sem.at[pair]))
        sends[-1].start()
    for send in sends:
        send.wait()


def transform_by_pair(blocks, chan_id):
    chan_count = len(blocks)
    rows, block_len = blocks[0].shape
    whole = pl.BlockSpec(memory_space=pltpu.VMEM)
    apart = pl.BlockSpec(memory_space=pltpu.HBM)
    shape = (2, RADIX // chan_count, LANES // 4, 2 * rows)
    return pl.pallas_call(
        functools.partial(transform_by_pair_kernel, chan_count),
        out_shape=[jax.ShapeDtypeStruct(shape, jnp.bfloat16)] * chan_count,
        in_specs=[pl.BlockSpec(memory_space=pltpu.SMEM)] + [whole] * 4 + [apart] * chan_count,
        out_specs=[apart] * chan_count,
        scratch_shapes=[
            pltpu.VMEM((chan_count, rows, block_len), jnp.bfloat16),
            pltpu.VMEM((chan_count,) + shape, jnp.bfloat16),
        ]
        + transform_scratch(rows)
        + [pltpu.SemaphoreType.DMA((chan_count,)), pltpu.SemaphoreType.DMA((chan_count,))],
        compiler_params=pltpu.CompilerParams(vmem_limit_bytes=VMEM_LIMIT),
        name="transform_by_pair",
    )(chan_id, *transform_tables(chan_count * block_len), *blocks)


def turn_kernel(other, group_ref, *refs):
    wide_ref = refs[-1]
    if other:
        in_refs, (across_ref, out_ref, near_ref) = refs[:-4], refs[-4:-1]
    else:
        in_refs, out_ref = refs[:-2], refs[-2]
    chan_count = len(in_refs)
    _, per, k2_count, _ = in_refs[0].shape
    pitch = per * chan_count + 1

    def spread(e, carry):
        for source, in_ref in enumerate(in_refs):
            for k2 in range(0, k2_count, EIGHT):
                value = in_ref[0, e, k2 : k2 + EIGHT, :].astype(jnp.float32)
                row = k2 * pitch + e * chan_count + source
                wide_ref[pl.ds(row, EIGHT, stride=pitch), :] = value
        return carry

    lax.fori_loop(0, per, spread, 0)

    def narrow(k2, carry):
        base = pl.multiple_of(k2 * per, per)
        for e in range(per):
            rows = pl.ds(k2 * pitch + e * chan_count, chan_count)
            out_ref[base + e] = wide_ref[rows, :].astype(jnp.bfloat16)
        return carry

    lax.fori_loop(0, k2_count, narrow, 0, unroll=4)

    if other:
        group = group_ref[0]
        same = group % 2 == group // 2

        @pl.when(same)
        def _():
            near_ref[...] = across_ref[...]

        @pl.when(jnp.logical_not(same))
        def _():
            near_ref[...] = out_ref[...]


def turn(blocks, group_id, across=None):
    chan_count = len(blocks)
    _, per, k2_count, lanes = blocks[0].shape
    one_half = (per * k2_count, chan_count, lanes)
    other = across is not None
    whole = pl.BlockSpec(one_half, lambda u, g: (0, 0, 0))

    def half_at(u, group):
        upper = group[0] // 2
        return upper if other else 1 - upper, 0, 0, 0

    results = pl.pallas_call(
        functools.partial(turn_kernel, other),
        out_shape=[jax.ShapeDtypeStruct(one_half, jnp.bfloat16)] * (1 + other),
        grid_spec=pltpu.PrefetchScalarGridSpec(
            num_scalar_prefetch=1,
            grid=(1,),
            in_specs=[pl.BlockSpec((1, per, k2_count, lanes), half_at)] * chan_count
            + [whole] * other,
            out_specs=[whole] * (1 + other),
            scratch_shapes=[
                pltpu.VMEM(((k2_count + EIGHT) * (per * chan_count + 1), lanes), jnp.float32)
            ],
        ),
        compiler_params=pltpu.CompilerParams(vmem_limit_bytes=VMEM_LIMIT),
        name="turn",
    )(group_id, *blocks, *([across] if other else []))
    return results if other else results[0]


def left_kernel(chunk_count, *refs):
    out_ref = refs[-1]
    channels, _, lanes = refs[0].shape
    sig_count = lanes // 2
    width = out_ref.shape[3]
    together = 2 * lanes // width
    count = channels // out_ref.shape[1]
    row = lax.broadcasted_iota(jnp.int32, (sig_count, lanes), 0)
    column = lax.broadcasted_iota(jnp.int32, (sig_count, lanes), 1)
    identity = (row == column).astype(jnp.bfloat16)

    def some_entries(chunk_refs, step, carry):
        rows = []
        for i in range(count * together):
            values = [ref[count * together * step + i].astype(jnp.float32) for ref in chunk_refs]
            rows += values + [pltpu.roll(value, sig_count, 1) for value in values]
        stacked = jnp.concatenate(rows, axis=0).astype(jnp.bfloat16)
        turned = lax.dot_general(
            identity, stacked, (((1,), (1,)), ((), ())), preferred_element_type=jnp.float32
        )
        for i in range(together):
            out_ref[0, together * step + i] = turned[:, i * width : (i + 1) * width].astype(
                jnp.bfloat16
            )
        return carry

    for half in range((len(refs) - 1) // chunk_count):

        @pl.when(pl.program_id(0) == half)
        def _():
            chunk_refs = refs[half * chunk_count : (half + 1) * chunk_count]
            steps = channels // (count * together)
            lax.fori_loop(0, steps, functools.partial(some_entries, chunk_refs), 0, unroll=16)


def left_operand(halves):
    chunk_count = len(halves[0])
    channels, chan_count, lanes = halves[0][0].shape
    depth = 2 * chunk_count * chan_count
    count = lanes // depth
    tile = 128
    last = channels // tile - 1

    def spec(half):
        def index(u, i):
            return jnp.where(u == half, i, jnp.where(u < half, 0, last)), 0, 0

        return pl.BlockSpec((tile, chan_count, lanes), index)

    return pl.pallas_call(
        functools.partial(left_kernel, chunk_count),
        out_shape=jax.ShapeDtypeStruct(
            (len(halves), channels // count, lanes // 2, lanes), jnp.bfloat16
        ),
        grid=(len(halves), channels // tile),
        in_specs=[spec(half) for half, chunks in enumerate(halves) for _ in chunks],
        out_specs=pl.BlockSpec((1, tile // count, lanes // 2, lanes), lambda u, i: (u, i, 0, 0)),
        compiler_params=pltpu.CompilerParams(vmem_limit_bytes=VMEM_LIMIT),
        name="left_operand",
    )(*[chunk for chunks in halves for chunk in chunks])


def correlate_kernel(chunk_count, spec_count, group_ref, plan_ref, left_ref, *refs):
    del group_ref, plan_ref
    chunk_refs = refs[:chunk_count]
    out_ref, sum_ref = refs[-2:]
    _, channels, chan_count, lanes = (1,) + chunk_refs[0].shape
    sig_count = lanes // 2
    pitch = channels + 1
    sign = jnp.where(
        lax.broadcasted_iota(jnp.int32, (chan_count, lanes), 1) < sig_count, 1.0, -1.0
    ).astype(jnp.float32)

    def pairs(step, carry):
        left = left_ref[0, step]
        for i in range(2):
            pair(2 * step + i, left[:, i * sig_count : (i + 1) * sig_count])
        return carry

    def pair(step, left):
        blocks = []
        for i in range(2):
            values = [ref[2 * step + i].astype(jnp.float32) for ref in chunk_refs]
            rows = [value * sign for value in values]
            rows += [pltpu.roll(value, sig_count, 1) for value in values]
            blocks.append(jnp.concatenate(rows, axis=0).astype(jnp.bfloat16))
        zero = jnp.zeros_like(blocks[0])
        weights = jnp.concatenate(
            [
                jnp.concatenate([blocks[0], zero], axis=1),
                jnp.concatenate([zero, blocks[1]], axis=1),
            ],
            axis=0,
        )
        both = jnp.dot(left, weights, preferred_element_type=jnp.float32)
        for i in range(2):
            q = 2 * step + i
            for a in range(0, sig_count, EIGHT):
                sum_ref[pl.ds(a * pitch + q, EIGHT, stride=pitch), :] = both[
                    a : a + EIGHT, i * lanes : (i + 1) * lanes
                ]

    lax.fori_loop(0, channels // 4, pairs, 0, unroll=32)

    def finish(a, carry):
        rows = pl.ds(a * pitch, channels)
        out_ref[0, a] = (sum_ref[rows, :] * (1.0 / spec_count)).astype(jnp.bfloat16)
        return carry

    lax.fori_loop(0, sig_count, finish, 0, unroll=16)


def correlate(left, chunks, group_id, plan, distance, spec_count, so_far):
    channels, chan_count, lanes = chunks[0].shape
    per_left = channels // left.shape[1]
    sig_count, depth = left.shape[2:]
    rounds = plan.shape[0]
    tile = 128

    def half_of(group):
        if distance > 1:
            return 0
        return jnp.where(group[0] % 2 == group[0] // 2, 0, 1)

    def round_of(group, plan):
        mate = group[0] ^ distance
        found = jnp.int32(0)
        for r in range(1, rounds):
            found = jnp.where(plan[r, group[0]] == mate, r, found)
        return found

    in_specs = [
        pl.BlockSpec((1, tile // per_left, sig_count, depth), lambda i, g, p: (half_of(g), i, 0, 0)),
    ] + [pl.BlockSpec((tile, chan_count, lanes), lambda i, g, p: (i, 0, 0))] * len(chunks)
    operands = [left, *chunks]
    aliases = {}
    if so_far is not None:
        in_specs.append(pl.BlockSpec(memory_space=pl.ANY))
        operands.append(so_far)
        aliases = {len(operands) + 1: 0}
    return pl.pallas_call(
        functools.partial(correlate_kernel, len(chunks), spec_count),
        out_shape=jax.ShapeDtypeStruct((rounds, sig_count, channels, lanes), jnp.bfloat16),
        grid_spec=pltpu.PrefetchScalarGridSpec(
            num_scalar_prefetch=2,
            grid=(channels // tile,),
            in_specs=in_specs,
            out_specs=pl.BlockSpec(
                (1, sig_count, tile, lanes), lambda i, g, p: (round_of(g, p), 0, i, 0)
            ),
            scratch_shapes=[pltpu.VMEM(((sig_count + EIGHT) * (tile + 1), lanes), jnp.float32)],
        ),
        input_output_aliases=aliases,
        compiler_params=pltpu.CompilerParams(vmem_limit_bytes=VMEM_LIMIT),
        cost_estimate=pl.CostEstimate(
            flops=2 * channels * sig_count * depth * lanes,
            bytes_accessed=16 * 1024 * 1024,
            transcendentals=0,
        ),
        name="correlate",
    )(group_id, plan, *operands)


def correlate_plain(mine, theirs):
    left = mine.reshape(*mine.shape[:2], -1)
    right_re = theirs.reshape(left.shape)
    right_im = jnp.stack([-theirs[..., 1], theirs[..., 0]], axis=-1).reshape(left.shape)
    vis_re = jnp.einsum("kas,kbs->akb", left, right_re, preferred_element_type=jnp.float32)
    vis_im = jnp.einsum("kas,kbs->akb", left, right_im, preferred_element_type=jnp.float32)
    return jnp.concatenate([vis_re, vis_im], axis=-1) * (1.0 / mine.shape[2])


def by_channel(half, sig_count, spec_count):
    _, per, parts, k2, _ = half.shape
    turned = half.transpose(3, 1, 0, 4, 2).reshape(k2 * per, spec_count, sig_count, parts)
    return turned.transpose(0, 2, 1, 3)


def local_plain(voltages, plan):
    sig_count, frames, block_len = voltages.shape
    chan_count = lax.axis_size("chan")
    group_count = lax.axis_size("grp")
    spec_count = frames - TAPS + 1
    rows = spec_count * sig_count // chan_count
    chan_id = lax.axis_index("chan").astype(jnp.int32)
    group_id = lax.axis_index("grp")

    frames_first = voltages.transpose(1, 0, 2)
    filtered = filter_taps(frames_first, chan_id.reshape(1), chan_count, 0, spec_count)
    filtered = filtered.reshape(chan_count, rows, block_len)
    frames_here = lax.all_to_all(filtered, "chan", split_axis=0, concat_axis=0, tiled=True)
    spectra = transform(frames_here)
    channel = lax.all_to_all(spectra, "chan", split_axis=0, concat_axis=0, tiled=True)

    lower_half, upper_half = channel[:, 0], channel[:, 1]
    group_ids = jnp.arange(group_count)
    partner = jnp.sum(jnp.where(group_ids[None, :] == group_id, plan, 0), axis=1)
    listed = jnp.any(partner[:, None] == group_ids[None, :], axis=0)
    slot_shape = (group_count,) + (1,) * lower_half.ndim
    chosen_half = jnp.where(
        (group_ids > group_id).reshape(slot_shape), upper_half[None], lower_half[None]
    )
    slots = jnp.where(listed.reshape(slot_shape), chosen_half, jnp.zeros_like(chosen_half))
    received = lax.all_to_all(slots, "grp", split_axis=0, concat_axis=0, tiled=True)
    halves = (group_id > partner).astype(jnp.int32)
    results = []
    for round_index in range(plan.shape[0]):
        mine = lax.dynamic_index_in_dim(channel, halves[round_index], 1, keepdims=False)
        theirs = lax.dynamic_index_in_dim(received, partner[round_index], 0, keepdims=False)
        results.append(
            correlate_plain(
                by_channel(mine, sig_count, spec_count), by_channel(theirs, sig_count, spec_count)
            )
        )
    return jnp.stack(results).astype(jnp.bfloat16)


def local_overlapped(voltages, plan):
    _, frames, _ = voltages.shape
    chan_count = lax.axis_size("chan")
    group_count = lax.axis_size("grp")
    spec_count = frames - TAPS + 1
    chan_id = lax.axis_index("chan").astype(jnp.int32).reshape(1)
    group_id = lax.axis_index("grp").astype(jnp.int32).reshape(1)
    frames_first = voltages.transpose(1, 0, 2)

    def over_chan(blocks):
        moved = list(blocks)
        for pair in farthest_first(chan_count):
            moved[pair] = lax.ppermute(
                blocks[pair], "chan", [(c, c ^ pair) for c in range(chan_count)]
            )
        return moved

    def to_mate(value, distance):
        return lax.ppermute(value, "grp", [(g, g ^ distance) for g in range(group_count)])

    own, near, across, across_own = [], [], [], []
    channels = []
    chunks = spec_count // chan_count
    for chunk in range(chunks):
        if chunk:
            parts = (range(chan_count),)
        else:
            parts = (range(chan_count // 2, chan_count), range(chan_count // 2))
        blocks = [None] * chan_count
        for pairs in parts:
            blocks[pairs.start : pairs.stop] = filter_by_pair(
                frames_first, chan_id, chan_count, chunk * chan_count, pairs
            )
        blocks = over_chan(blocks)
        blocks = transform_by_pair(blocks, chan_id)
        channels.append(over_chan(blocks))
    for channel in channels:
        for_across = turn(channel, group_id)
        across.append(to_mate(for_across, 2))
        kept, for_near = turn(channel, group_id, for_across)
        near.append(to_mate(for_near, 1))
        across_own.append(for_across)
        own.append(kept)
    left = left_operand([own, across_own])
    result = correlate(left, near, group_id, plan, 1, spec_count, None)
    across, result = lax.optimization_barrier((across, result))
    relayed = [to_mate(value, 1) for value in across]
    result = correlate(left, across, group_id, plan, 2, spec_count, result)
    return correlate(left, relayed, group_id, plan, 3, spec_count, result)


def farthest_first(chan_count):
    half = chan_count // 2
    return list(range(half, chan_count)) + list(range(1, half))


def overlaps(group_count, chan_count):
    return group_count == 4 and chan_count == EIGHT


def local(voltages, plan):
    sig_count, frames, _ = voltages.shape
    chan_count = lax.axis_size("chan")
    group_count = lax.axis_size("grp")
    if (
        overlaps(group_count, chan_count)
        and plan.shape[0] == group_count - 1
        and frames - TAPS + 1 == 2 * chan_count
        and 2 * sig_count == LANES
    ):
        return local_overlapped(voltages, plan)
    return local_plain(voltages, plan)


def solution(mesh):
    in_specs = (P("grp", None, "chan"), P())
    out_specs = P(None, "grp", "chan", None)
    return jax.shard_map(local, mesh=mesh, in_specs=in_specs, out_specs=out_specs, check_vma=False)
```
